32 devices in a mesh: dp: 4 (over z), row: 2 (over x), col: 4 (over y, core).
Axes of the slice: x: 2, y: 2, z: 4, core: 2. Of those that a mesh axis runs over, the one named last changes fastest.
Arguments:
- tokens: bfloat16 [768, 16384], P('row', ('dp', 'col')), may hold values from -6 to 6
- ln_gain: float32 [768], P('row'), may hold values from 0.5 to 1.5
- ln_bias: float32 [768], P('row'), may hold values from -0.3 to 0.3
- qkv_weight: bfloat16 [768, 3, 768], P('row', None, 'col'), may hold values from -0.21875 to 0.21875
- out_weight: bfloat16 [768, 768], P('col', 'row'), may hold values from -6 to 6
- up_weight: bfloat16 [768, 3072], P('row', 'col'), may hold values from -0.21875 to 0.21875
- down_weight: bfloat16 [768, 3072], P('row', 'col'), may hold values from -0.21875 to 0.21875
- mod_weight: bfloat16 [3, 768, 768], P(None, 'row'), may hold values from -0.109375 to 0.109375
- timestep: int32 [8], replicated, may hold values from 0 to 999
- block_size: int32 [8], replicated, may hold values from 32 to 256, as said below
- cotangent: bfloat16 [768, 16384], P('row', ('dp', 'col')), may hold values from -6 to 6
Outputs:
- output: bfloat16 [768, 16384], P('row', ('dp', 'col'))
- tokens_grad: float32 [768, 16384], P('row', ('dp', 'col'))
- ln_gain_grad: float32 [768], P('row')
- ln_bias_grad: float32 [768], P('row')
- qkv_grad: float32 [768, 3, 768], P('row', None, 'col')
- out_grad: float32 [768, 768], P('col', 'row')
- up_grad: float32 [768, 3072], P('row', 'col')
- down_grad: float32 [768, 3072], P('row', 'col')
- mod_grad: float32 [3, 768, 768], P(None, 'row')
The draws below stay inside these ranges and needn't reach their ends.
Inputs may be any that keep to these rules, and one draw needn't show every extreme that they name: `block_size`: each entry is 256 halved zero to three times; some sequence has 256.
All inputs are finite; a program needn't handle non-finite values.
Results may differ from the reference program's by a relative error of at most 0.02.
Values may be sent and summed in bfloat16 or wider, within the bound.
No kernel may reach another device: no remote copies, remote signals or barrier semaphores. Data moves between devices by JAX's collectives and lax.ppermute only.
A program may use at most 256 MiB of HBM per device.

```python
import math
import jax
import jax.numpy as jnp
from jax import lax

D = 768
HEADS = 12
HEAD_DIM = 64
FF = 3072
LENGTH = 2048
BLOCK_MAX = 256
SEQS = 8
TOKENS = 16384


def draw_block_size(key, part):
    halvings = jax.random.randint(jax.random.fold_in(key, 11), (SEQS,), 0, 4)
    chosen = jax.random.randint(jax.random.fold_in(key, 12), (), 0, SEQS)
    halvings = jnp.where(jnp.arange(SEQS) == chosen, 0, halvings)
    largest = jnp.full((SEQS,), BLOCK_MAX, jnp.int32)
    return jnp.right_shift(largest, halvings.astype(jnp.int32)).astype(jnp.int32)


def place_ends(values, key, low, top_value):
    longest = values.shape.index(max(values.shape))
    spots = []
    for shift in (0, 1):
        where = [jax.random.randint(jax.random.fold_in(key, axis), (), 0, length) for axis, length in enumerate(values.shape)]
        where[longest] = (where[longest] + shift) % values.shape[longest]
        spots.append(tuple(where))
    return values.at[spots[0]].set(low).at[spots[1]].set(top_value)


def steps_of(rng, extent, pieces, smallest, high):
    level, own = 1.0, jax.random.fold_in(rng, 6)
    for position, blocks in pieces:
        steps = jnp.exp(jax.random.uniform(jax.random.fold_in(own, position), (blocks,), jnp.float32, smallest / len(pieces), high / len(pieces)))
        level = level * jnp.repeat(steps, extent[position] // blocks).reshape([-1 if axis == position else 1 for axis in range(len(extent))])
    return level


def noise(key, shape, scale, most, shards=(), kind=jnp.bfloat16):
    values = scale * jax.random.normal(key, shape, jnp.float32)
    if shards:
        values = values * steps_of(key, shape, shards, -0.22, 0.18)
    return jnp.clip(values, -most, most).astype(kind)


def setup_inputs(seed: int = 0) -> dict:
    seeds = jax.random.split(jax.random.key(seed), 12)
    tokens = noise(seeds[0], (D, TOKENS), 1.0, 6.0, ((0, 2), (1, 16)))
    ln_gain = jnp.clip(1.0 + 0.1 * jax.random.normal(seeds[1], (D,), jnp.float32), 0.5, 1.5)
    ln_bias = noise(seeds[2], (D,), 0.05, 0.3, ((0, 2),), jnp.float32)
    qkv_weight = noise(seeds[3], (D, 3, D), D ** -0.5, 0.21875, ((0, 2), (2, 4)))
    out_weight = noise(seeds[4], (D, D), (max(1, 2 * D // LENGTH)) ** -0.5, 6.0, ((0, 4), (1, 2)))
    up_weight = noise(seeds[5], (D, FF), D ** -0.5, 0.21875, ((0, 2), (1, 4)))
    down_weight = noise(seeds[6], (D, FF), (FF // 4) ** -0.5, 0.21875, ((0, 2), (1, 4)))
    mod_weight = noise(seeds[7], (3, D, D), (4 * D) ** -0.5, 0.109375, ((1, 2),))
    timestep = place_ends(jax.random.randint(seeds[8], (SEQS,), 0, 1000), jax.random.fold_in(seeds[8], 1), 0, 999).astype(jnp.int32)
    block_size = draw_block_size(jax.random.fold_in(seeds[11], 71), 0)
    cotangent = noise(seeds[10], (D, TOKENS), 1.0, 6.0, ((0, 2), (1, 16)))
    return dict(tokens=tokens, ln_gain=ln_gain, ln_bias=ln_bias, qkv_weight=qkv_weight, out_weight=out_weight, up_weight=up_weight, down_weight=down_weight, mod_weight=mod_weight, timestep=timestep, block_size=block_size, cotangent=cotangent)


@jax.custom_vjp
def low(v):
    return lax.optimization_barrier(v.astype(jnp.bfloat16)).astype(jnp.float32)

@jax.custom_vjp
def low_back(v):
    return v

def low_keep(v):
    return (low(v), None)

def low_pass(kept, grad):
    return (grad,)

def back_keep(v):
    return (v, None)

def back_low(kept, grad):
    return (low(grad),)
low.defvjp(low_keep, low_pass)
low_back.defvjp(back_keep, back_low)
EPSILON = 1e-05
HIGH = lax.Precision.HIGHEST

def time_embed(steps_in, width_all):
    half_width = width_all // 2
    frequency = jnp.exp(-math.log(10000.0) * jnp.arange(half_width, dtype=jnp.float32) / half_width)
    angles = steps_in.astype(jnp.float32)[:, None] * frequency[None, :]
    return jnp.concatenate([jnp.sin(angles), jnp.cos(angles)], axis=1)

def rope_tables(length, head_width):
    half_dim = head_width // 2
    frequency = jnp.exp(-math.log(10000.0) * jnp.arange(half_dim, dtype=jnp.float32) / half_dim)
    angles = jnp.arange(length, dtype=jnp.float32)[:, None] * frequency[None, :]
    return (jnp.cos(angles), jnp.sin(angles))

def rotate(vector, cosine, sine_tab):
    half_dim = vector.shape[-1] // 2
    front_half, back_half = (vector[..., :half_dim], vector[..., half_dim:])
    return jnp.concatenate([front_half * cosine - back_half * sine_tab, back_half * cosine + front_half * sine_tab], axis=-1)

def attend(queries, key_rows, value_rows, block_len):
    length = queries.shape[0]
    rows_per = min(512, length)
    positions = jnp.arange(length, dtype=jnp.int32)
    key_block = positions // block_len
    score_scale = HEAD_DIM ** (-0.5)

    def one_block(offset):
        query_part = lax.dynamic_slice_in_dim(queries, offset, rows_per, 0)
        query_block = lax.dynamic_slice_in_dim(key_block, offset, rows_per, 0)
        scores = jnp.einsum('qhd,khd->hqk', query_part, key_rows, precision=HIGH) * score_scale
        scores = low_back(jnp.where(key_block[None, None, :] <= query_block[None, :, None], scores, -1e+30))
        weights = jax.nn.softmax(scores, axis=-1)
        return jnp.einsum('hqk,khd->qhd', low(weights), value_rows, precision=HIGH)
    offsets = jnp.arange(0, length, rows_per, dtype=jnp.int32)
    blocks_out = lax.map(jax.checkpoint(one_block), offsets)
    return blocks_out.reshape(queries.shape)

def norm_rows(values):
    mean_row = lax.optimization_barrier(jnp.mean(values, axis=1, keepdims=True))
    var_row = lax.optimization_barrier(jnp.mean(values * values, axis=1, keepdims=True)) - mean_row * mean_row
    return (values - mean_row) * lax.rsqrt(var_row + EPSILON)

def layer(hidden_in, ln_gain, ln_bias, qkv_weight, out_weight, up_weight, down_weight, mod_weight, embedded, block_len):
    length = hidden_in.shape[0]
    act_one = low(norm_rows(hidden_in) * ln_gain + ln_bias)
    projected = low_back(jnp.dot(act_one, qkv_weight.reshape(D, 3 * D), precision=HIGH))
    projected = projected.reshape(length, 3, HEADS, HEAD_DIM)
    cosine, sine_tab = rope_tables(length, HEAD_DIM)
    cosine = cosine[:, None, :]
    sine_tab = sine_tab[:, None, :]
    queries = low(rotate(projected[:, 0], cosine, sine_tab))
    key_rows = low(rotate(projected[:, 1], cosine, sine_tab))
    value_rows = low(projected[:, 2])
    attn_mix = low_back(low(attend(queries, key_rows, value_rows, block_len))).reshape(length, D)
    branch_one = low_back(jnp.dot(attn_mix, out_weight, precision=HIGH))
    hidden_one = hidden_in + branch_one
    modulation = jnp.einsum('d,ked->ke', embedded, mod_weight, precision=HIGH)
    act_two = low(norm_rows(hidden_one) * (1.0 + modulation[0]) + modulation[1])
    pre_act = low_back(jnp.dot(act_two, up_weight, precision=HIGH))
    gelu_out = low(jax.nn.gelu(pre_act, approximate=True))
    branch_two = low_back(jnp.dot(gelu_out, down_weight.T, precision=HIGH))
    return hidden_one + (1.0 + modulation[2]) * branch_two

def reference(tokens, ln_gain, ln_bias, qkv_weight, out_weight, up_weight, down_weight, mod_weight, timestep, block_size, cotangent):
    params = tuple((param.astype(jnp.float32) for param in (ln_gain, ln_bias, qkv_weight, out_weight, up_weight, down_weight, mod_weight)))
    inputs = tokens.astype(jnp.float32).T.reshape(SEQS, LENGTH, D)
    cotangents = cotangent.astype(jnp.float32).T.reshape(SEQS, LENGTH, D)
    embedded_all = time_embed(timestep, D)

    def one_sequence(totals, element):
        hidden_in, grad_out, embedded, block_len = element

        def forward(hidden_value, *weight_list):
            return layer(hidden_value, *weight_list, embedded, block_len)
        result, pull_back = jax.vjp(forward, hidden_in, *params)
        pulled = pull_back(grad_out)
        totals = tuple((total + added for total, added in zip(totals, pulled[1:])))
        return (totals, (result.astype(jnp.bfloat16), pulled[0]))
    initial = tuple((jnp.zeros_like(param) for param in params))
    totals, (outputs, input_grads) = lax.scan(one_sequence, initial, (inputs, cotangents, embedded_all, block_size))
    return (outputs.reshape(TOKENS, D).T, input_grads.reshape(TOKENS, D).T, totals[0], totals[1], totals[2], totals[3], totals[4], totals[5], totals[6])
```

```python
from functools import partial
import math

import jax
import jax.numpy as jnp
from jax import lax
from jax.experimental import pallas as pl
from jax.experimental.pallas import tpu as pltpu
from jax.sharding import PartitionSpec as P

HEAD_DIM = 64
LENGTH = 2048
CHUNK = 256
EPSILON = 1e-05
HIGH = lax.Precision.HIGHEST
F32 = jnp.float32
BF16 = jnp.bfloat16


def time_embed(steps_in, width_all):
    half_width = width_all // 2
    frequency = jnp.exp(-math.log(10000.0) * jnp.arange(half_width, dtype=F32) / half_width)
    angles = steps_in.astype(F32)[:, None] * frequency[None, :]
    return jnp.concatenate([jnp.sin(angles), jnp.cos(angles)], axis=1)


def rope_tables(length, head_width):
    half_dim = head_width // 2
    frequency = jnp.exp(-math.log(10000.0) * jnp.arange(half_dim, dtype=F32) / half_dim)
    angles = frequency[:, None] * jnp.arange(length, dtype=F32)[None, :]
    return jnp.cos(angles), jnp.sin(angles)


def dot(left, right, left_dim=1, right_dim=0):
    dims = (((left_dim,), (right_dim,)), ((), ()))
    return lax.dot_general(left, right, dims, preferred_element_type=F32)


def diagonal_mask(block_ref):
    block_len = block_ref[0]
    key_block = lax.broadcasted_iota(jnp.int32, (CHUNK, CHUNK), 0) // block_len
    query_block = lax.broadcasted_iota(jnp.int32, (CHUNK, CHUNK), 1) // block_len
    return key_block <= query_block


def attend_forward_kernel(block_ref, q_ref, k_ref, v_ref, o_ref, lse_ref, keys):
    keys[...] = k_ref[...].T
    visible = diagonal_mask(block_ref)
    for step in range(q_ref.shape[1] // CHUNK):
        here = slice(step * CHUNK, (step + 1) * CHUNK)
        past = slice(0, step * CHUNK)
        query = q_ref[:, here] * BF16(0.125)
        diag = jnp.where(visible, dot(keys[here, :], query), -1e30)
        top = jnp.max(diag, axis=0, keepdims=True)
        if step:
            scores = dot(keys[past, :], query)
            top = jnp.maximum(top, jnp.max(scores, axis=0, keepdims=True))
        weight = jnp.exp(diag - top)
        total = jnp.sum(weight, axis=0, keepdims=True)
        mixed = dot(v_ref[:, here], weight.astype(BF16))
        if step:
            weight = jnp.exp(scores - top)
            total = total + jnp.sum(weight, axis=0, keepdims=True)
            mixed = mixed + dot(v_ref[:, past], weight.astype(BF16))
        o_ref[:, here] = (mixed / total).astype(BF16)
        lse_ref[0, :, here] = top + jnp.log(total)


def attend_forward(block_len, queries, keys, values):
    rows, length = queries.shape
    heads = rows // HEAD_DIM
    spec = pl.BlockSpec((HEAD_DIM, length), lambda h: (h, 0))
    return pl.pallas_call(
        attend_forward_kernel,
        grid=(heads,),
        in_specs=[pl.BlockSpec(memory_space=pltpu.SMEM), spec, spec, spec],
        out_specs=[spec, pl.BlockSpec((1, 1, length), lambda h: (h, 0, 0))],
        out_shape=[
            jax.ShapeDtypeStruct((rows, length), BF16),
            jax.ShapeDtypeStruct((heads, 1, length), F32),
        ],
        scratch_shapes=[pltpu.VMEM((length, HEAD_DIM), BF16)],
        compiler_params=pltpu.CompilerParams(vmem_limit_bytes=58 * 1024 * 1024),
        name="attend_forward",
    )(block_len, queries, keys, values)


def attend_backward_kernel(
    block_ref, q_ref, k_ref, v_ref, g_ref, lse_ref, cos_ref, sin_ref,
    dq_ref, dk_ref, dv_ref, keys, values, queries, grads, key_sum, value_sum,
):
    length = q_ref.shape[1]
    half = HEAD_DIM // 2
    keys[...] = k_ref[...].T
    values[...] = v_ref[...].T
    queries[...] = (q_ref[...] * BF16(0.125)).T
    grads[...] = g_ref[...].T
    visible = diagonal_mask(block_ref)

    def store_unrotated(out_ref, grad, where):
        front, back = grad[:half], grad[half:]
        cosine, sine = cos_ref[:, where], sin_ref[:, where]
        out_ref[:half, where] = (front * cosine + back * sine).astype(BF16)
        out_ref[half:, where] = (back * cosine - front * sine).astype(BF16)

    for step in range(length // CHUNK):
        here = slice(step * CHUNK, (step + 1) * CHUNK)
        past = slice(0, step * CHUNK)
        query = q_ref[:, here] * BF16(0.125)
        grad = g_ref[:, here]
        lse = lse_ref[0, :, here]
        diag = jnp.where(visible, dot(keys[here, :], query), -1e30)
        weight = jnp.exp(diag - lse)
        grad_weight = dot(values[here, :], grad)
        delta = jnp.sum(weight * grad_weight, axis=0, keepdims=True)
        if step:
            weight_past = jnp.exp(dot(keys[past, :], query) - lse)
            grad_past = dot(values[past, :], grad)
            delta = delta + jnp.sum(weight_past * grad_past, axis=0, keepdims=True)
        grad_score = (weight * (grad_weight - delta)).astype(BF16)
        grad_query = dot(k_ref[:, here], grad_score)
        value_sum[here, :] = dot(weight.astype(BF16), grads[here, :])
        key_sum[here, :] = dot(grad_score, queries[here, :])
        if step:
            grad_score = (weight_past * (grad_past - delta)).astype(BF16)
            grad_query = grad_query + dot(k_ref[:, past], grad_score)
            value_sum[past, :] += dot(weight_past.astype(BF16), grads[here, :])
            key_sum[past, :] += dot(grad_score, queries[here, :])
        store_unrotated(dq_ref, grad_query * 0.125, here)
    store_unrotated(dk_ref, key_sum[...].T, slice(0, length))
    dv_ref[...] = value_sum[...].T.astype(BF16)


def attend_backward(block_len, queries, keys, values, grad_mixed, lse, cosine, sine):
    rows, length = queries.shape
    heads = rows // HEAD_DIM
    spec = pl.BlockSpec((HEAD_DIM, length), lambda h: (h, 0))
    table = pl.BlockSpec((HEAD_DIM // 2, length), lambda h: (0, 0))
    return pl.pallas_call(
        attend_backward_kernel,
        grid=(heads,),
        in_specs=[pl.BlockSpec(memory_space=pltpu.SMEM), spec, spec, spec, spec]
        + [pl.BlockSpec((1, 1, length), lambda h: (h, 0, 0)), table, table],
        out_specs=[spec] * 3,
        out_shape=[jax.ShapeDtypeStruct((rows, length), BF16)] * 3,
        scratch_shapes=[pltpu.VMEM((length, HEAD_DIM), BF16)] * 4
        + [pltpu.VMEM((length, HEAD_DIM), F32)] * 2,
        compiler_params=pltpu.CompilerParams(vmem_limit_bytes=58 * 1024 * 1024),
        name="attend_backward",
    )(block_len, queries, keys, values, grad_mixed, lse, cosine, sine)


def swap_rows(value):
    count = lax.axis_size("row")
    return lax.ppermute(value, "row", [(i, i ^ 1) for i in range(count)])


def swap_cores(value):
    count = lax.axis_size("col")
    return lax.ppermute(value, "col", [(i, i ^ 1) for i in range(count)])


def swap_cols(value):
    return lax.ppermute(value, "col", [(i, i ^ 2) for i in range(lax.axis_size("col"))])


def in_order(flag, own, other):
    first = jnp.where(flag == 0, own, other)
    second = jnp.where(flag == 0, other, own)
    return first, second


def cut(value, start, size, axis):
    return lax.dynamic_slice_in_dim(value, start, size, axis)


def reduce_dp(value):
    count = lax.axis_size("dp")
    rows = value.shape[0] // count
    here = lax.axis_index("dp")

    def shift(piece, step):
        return lax.ppermute(piece, "dp", [(i, (i + step) % count) for i in range(count)])

    arrived = [
        shift(cut(value, (here + step) % count * rows, rows, 0), step) for step in range(1, count)
    ]
    total = cut(value, here * rows, rows, 0).astype(F32)
    for piece in arrived:
        total = total + piece.astype(F32)
    total = total.astype(BF16)
    out = jnp.zeros(value.shape, BF16)
    out = lax.dynamic_update_slice_in_dim(out, total, here * rows, 0)
    for step in range(1, count):
        piece = shift(total, step)
        out = lax.dynamic_update_slice_in_dim(out, piece, (here - step) % count * rows, 0)
    return out.astype(F32)


class PairMoves:
    def __init__(self, r, c, feats):
        self.j, self.h, self.k, self.feats = r, c // 2, c % 2, feats
        self.aligned = self.j == self.h

    def sequence(self, value):
        full = jnp.concatenate([value, swap_rows(value)], axis=0)
        return jnp.concatenate(in_order(self.k, full, swap_cores(full)), axis=1)

    def own_tokens(self, value):
        span = value.shape[1] // 2
        other = swap_rows(cut(value, (1 - self.j) * span, span, 1))
        return jnp.concatenate([cut(value, self.j * span, span, 1), other], axis=0)

    def features(self, value):
        return jnp.concatenate([value, swap_rows(value)], axis=0)

    def flip(self, value):
        return jnp.concatenate([value[self.feats :], value[: self.feats]], axis=0)

    def qkv(self, weight):
        other = swap_cols(weight)
        mine = jnp.where(self.aligned, weight, other)
        theirs = jnp.where(self.aligned, other, weight)
        return jnp.concatenate([mine, swap_rows(theirs)], axis=0)

    def feed(self, weight):
        rows = jnp.concatenate([weight, swap_rows(weight)], axis=0)
        return jnp.concatenate([rows, swap_cols(rows)], axis=1)

    def out(self, weight):
        columns = jnp.concatenate([weight, swap_rows(weight)], axis=1)
        other = swap_cols(columns)
        mine = jnp.where(self.aligned, columns, other)
        theirs = jnp.where(self.aligned, other, columns)
        return jnp.concatenate([mine, theirs], axis=0)

    def reduce_feed(self, grad):
        width = grad.shape[1] // 2
        part = grad[:, :width] + swap_cols(grad[:, width:].astype(BF16)).astype(F32)
        part = part[: self.feats] + swap_rows(part[self.feats :].astype(BF16)).astype(F32)
        return reduce_dp(part.astype(BF16))

    def reduce_out(self, grad):
        height = grad.shape[0] // 2
        mine = jnp.where(self.aligned, grad[:height], grad[height:])
        theirs = jnp.where(self.aligned, grad[height:], grad[:height])
        part = mine + swap_cols(theirs.astype(BF16)).astype(F32)
        part = part[:, : self.feats] + swap_rows(part[:, self.feats :].astype(BF16)).astype(F32)
        return reduce_dp(part.astype(BF16))

    def reduce_qkv(self, grad):
        first, second = grad[: self.feats], grad[self.feats :]
        keep = jnp.where(self.aligned, first, second)
        send = jnp.where(self.aligned, second, first)
        part = (keep + swap_cols(send.astype(BF16)).astype(F32)).astype(BF16)
        corner = []
        for row in range(2):
            for core in range(2):
                source = row * 4 + 2 * (1 - row) + core
                corner.append((source, (1 - row) * 4 + 2 * row + core))
        moved = lax.ppermute(part, ("row", "col"), corner)
        return reduce_dp(jnp.where(self.aligned, part, moved))

    def outputs(self, value):
        other = swap_rows(value[self.feats :])
        own = value[: self.feats]
        return jnp.concatenate(in_order(self.j, own, other), axis=1)

    def own_sums(self, sums):
        total = sums[:, : self.feats] + swap_rows(sums[:, self.feats :])
        total = total + swap_cores(total)
        total = total + swap_cols(total)
        count = lax.axis_size("dp")
        reach = 1
        while reach < count:
            total = total + lax.ppermute(total, "dp", [(i, i ^ reach) for i in range(count)])
            reach *= 2
        return total


class AnyMoves:
    def __init__(self, r, c, feats, pairs):
        self.r, self.j, self.q, self.h, self.k = r, r % 2, r // 2, c // 2, c % 2
        self.feats, self.pairs = feats, pairs
        cols = lax.axis_size("col")
        self.cores = [[i, i + 1] for i in range(0, cols, 2)]
        self.likes = [list(range(core, cols, 2)) for core in range(2)]

    def pair_tokens(self, value):
        full = lax.all_gather(value, "row", axis=0, tiled=True)
        return lax.all_gather(full, "col", axis=1, tiled=True, axis_index_groups=self.cores)

    def sequence(self, value):
        return cut(self.pair_tokens(value), self.q * LENGTH, LENGTH, 1)

    def own_tokens(self, value):
        span = LENGTH // 4
        return cut(self.sequence(value), (2 * self.k + self.j) * span, span, 1)

    def features(self, value):
        return lax.all_gather(value, "row", axis=0, tiled=True)

    def flip(self, value):
        return value

    def likes_gather(self, value, axis):
        return lax.all_gather(value, "col", axis=axis, axis_index_groups=self.likes)

    def qkv(self, weight):
        return cut(self.likes_gather(self.features(weight), 0), self.j, 1, 0)[0]

    def feed(self, weight):
        rows = self.features(weight)
        return lax.all_gather(rows, "col", axis=1, tiled=True, axis_index_groups=self.likes)

    def out(self, weight):
        columns = lax.all_gather(weight, "row", axis=1, tiled=True)
        parts = self.likes_gather(columns, 0)
        return jnp.concatenate(in_order(self.j, parts[0], parts[1]), axis=0)

    def scatter(self, grad, row_axis, like_axis):
        grad = lax.psum_scatter(
            grad.astype(BF16), "row", scatter_dimension=row_axis, tiled=True
        )
        grad = lax.psum_scatter(
            grad, "col", scatter_dimension=like_axis, tiled=True, axis_index_groups=self.likes
        )
        return lax.psum(grad, "dp").astype(F32)

    def reduce_feed(self, grad):
        return self.scatter(grad, 0, 1)

    def reduce_out(self, grad):
        height = grad.shape[0] // 2
        ordered = jnp.concatenate(in_order(self.j, grad[:height], grad[height:]), axis=0)
        return self.scatter(ordered, 1, 0)

    def reduce_qkv(self, grad):
        zero = jnp.zeros_like(grad)
        both = jnp.stack(in_order(self.j, grad, zero), axis=1)
        return self.scatter(both, 0, 1)[:, 0]

    def outputs(self, value):
        rows = lax.axis_size("row")
        parts = value.reshape(rows, self.feats, -1)
        parts = lax.all_to_all(parts, "row", split_axis=0, concat_axis=0, tiled=True)
        parts = lax.all_gather(parts, "col", axis=0, axis_index_groups=self.cores)
        span = parts.shape[-1]
        parts = parts.reshape(2, self.pairs, 2, self.feats, span).transpose(3, 1, 0, 2, 4)
        parts = parts.reshape(self.feats, -1)
        width = parts.shape[1] // 2
        return cut(parts, self.k * width, width, 1)

    def own_sums(self, sums):
        total = lax.psum(sums, ("dp", "row", "col"))
        return cut(total, self.r * self.feats, self.feats, 1)


def norm_forward(values):
    mean = jnp.mean(values, axis=0, keepdims=True)
    square = jnp.mean(values * values, axis=0, keepdims=True)
    inv_std = lax.rsqrt(square - mean * mean + EPSILON)
    return (values - mean) * inv_std, inv_std


def norm_backward(grad_norm, normed, inv_std):
    mean_plain = jnp.mean(grad_norm, axis=0, keepdims=True)
    mean_cross = jnp.mean(grad_norm * normed, axis=0, keepdims=True)
    return inv_std * (grad_norm - mean_plain - normed * mean_cross)


def share(value):
    return jnp.concatenate([value, swap_cores(value)], axis=1)


def merge(partial_sum):
    span = partial_sum.shape[1] // 2
    other = swap_cores(partial_sum[:, span:].astype(BF16))
    return partial_sum[:, :span] + other.astype(F32)


def local(
    tokens, ln_gain, ln_bias, qkv_weight, out_weight, up_weight, down_weight,
    mod_weight, timestep, block_size, cotangent,
):
    rows, cols = lax.axis_size("row"), lax.axis_size("col")
    r, c, z = lax.axis_index("row"), lax.axis_index("col"), lax.axis_index("dp")
    h, k = c // 2, c % 2
    width = mod_weight.shape[2]
    feats, local_tokens = tokens.shape
    pairs = 2 * local_tokens // LENGTH
    assert rows == 2 * pairs and cols == 4 and LENGTH % (8 * CHUNK) == 0
    q, j = r // 2, r % 2
    sequences = timestep.shape[0]
    seq = (z * (cols // 2) + h) * pairs + q
    span = LENGTH // 4
    moves = PairMoves(r, c, feats) if pairs == 1 else AnyMoves(r, c, feats, pairs)

    embedded = time_embed(timestep, width)
    steps_here = cut(embedded, seq, 1, 0)[0]
    block_len = cut(block_size, seq, 1, 0)
    cosine, sine = rope_tables(LENGTH, HEAD_DIM)

    x_all = moves.sequence(tokens)
    if pairs == 1:
        own_mod = jnp.einsum("d,ked->ek", steps_here, mod_weight.astype(F32), precision=HIGH)
        columns = jnp.concatenate([own_mod, ln_gain[:, None], ln_bias[:, None]], axis=1)
        columns = jnp.concatenate([columns.T, swap_rows(columns.T)], axis=1).T
        scale, shift, gate = columns[:, 0:1], columns[:, 1:2], columns[:, 2:3]
        gain, bias = columns[:, 3:4], columns[:, 4:5]
    else:
        mods = jnp.einsum("nd,ked->enk", embedded, mod_weight.astype(F32), precision=HIGH)
        mods = moves.features(cut(mods.reshape(feats, -1), 0, 3 * sequences, 1))
        mods = cut(mods, 3 * seq, 3, 1)
        scale, shift, gate = mods[:, 0:1], mods[:, 1:2], mods[:, 2:3]
        gain, bias = moves.features(ln_gain)[:, None], moves.features(ln_bias)[:, None]
    qkv_full = moves.qkv(qkv_weight).reshape(width, -1)
    out_full = moves.out(out_weight)
    up_full = moves.feed(up_weight)
    down_full = moves.feed(down_weight)
    grad_out = moves.own_tokens(cotangent).astype(F32)

    norm_all, _ = norm_forward(x_all.astype(F32))
    act_one = (norm_all * gain + bias).astype(BF16)
    projected = dot(qkv_full, act_one, 0, 0)
    third = projected.shape[0] // 3
    half = HEAD_DIM // 2

    def rotate(value):
        value = value.reshape(-1, 2, half, LENGTH)
        front, back = value[:, 0], value[:, 1]
        turned = [front * cosine - back * sine, back * cosine + front * sine]
        return jnp.stack(turned, axis=1).reshape(third, LENGTH).astype(BF16)

    queries = rotate(projected[:third])
    keys = rotate(projected[third : 2 * third])
    values = projected[2 * third :].astype(BF16)
    mixed, lse = attend_forward(block_len, queries, keys, values)

    def chip_part(value, chip):
        first = cut(value, k * 2 * span + chip * span, span, 1)
        second = cut(value, (1 - k) * 2 * span + chip * span, span, 1)
        return jnp.concatenate([first, second], axis=1)

    attn_mix = jnp.concatenate([chip_part(mixed, j), swap_rows(chip_part(mixed, 1 - j))], axis=0)

    resid = cut(x_all, (2 * k + j) * span, span, 1).astype(F32)
    hidden_one = resid + merge(dot(out_full, attn_mix, 0, 0))
    norm_two, inv_two = norm_forward(hidden_one)
    act_two = share((norm_two * (1.0 + scale) + shift).astype(BF16))
    pre_act = dot(up_full, act_two, 0, 0)
    gelu = partial(jax.nn.gelu, approximate=True)
    gelu_value, gelu_pull = jax.vjp(gelu, pre_act)
    gelu_out = gelu_value.astype(BF16)
    branch_two = merge(dot(down_full, gelu_out))
    result = hidden_one + (1.0 + gate) * branch_two

    grad_two = share((grad_out * (1.0 + gate)).astype(BF16))
    grad_gelu = dot(down_full, grad_two, 0, 0)
    grad_pre = gelu_pull(grad_gelu)[0].astype(BF16)
    down_grad = moves.reduce_feed(dot(grad_two, gelu_out, 1, 1))
    up_grad = moves.reduce_feed(dot(act_two, grad_pre, 1, 1))
    grad_act_two = merge(dot(up_full, grad_pre))
    grad_hidden = grad_out + norm_backward(grad_act_two * (1.0 + scale), norm_two, inv_two)
    grad_one = share(grad_hidden.astype(BF16))
    grad_attn = dot(out_full, grad_one).astype(BF16)
    out_grad = moves.reduce_out(dot(attn_mix, grad_one, 1, 1))

    head_rows = grad_attn.shape[0] // 2
    mine, theirs = grad_attn[:head_rows], swap_rows(grad_attn[head_rows:])
    pieces = []
    mine_cores = in_order(k, mine[:, :span], mine[:, span:])
    their_cores = in_order(k, theirs[:, :span], theirs[:, span:])
    for core in range(2):
        pieces.extend(in_order(j, mine_cores[core], their_cores[core]))
    grad_mixed = jnp.concatenate(pieces, axis=1)
    grads = attend_backward(block_len, queries, keys, values, grad_mixed, lse, cosine, sine)
    grad_projected = jnp.concatenate(grads, axis=0)
    qkv_grad = moves.reduce_qkv(dot(act_one, grad_projected, 1, 1))
    grad_act_one = dot(qkv_full, grad_projected)
    kept = cut(grad_act_one, k * 2 * span, 2 * span, 1)
    sent = cut(grad_act_one, (1 - k) * 2 * span, 2 * span, 1).astype(BF16)
    kept = kept + swap_cores(sent).astype(F32)
    sent = cut(kept, (1 - j) * span, span, 1).astype(BF16)
    grad_act_one = cut(kept, j * span, span, 1) + moves.flip(swap_rows(sent)).astype(F32)
    norm_one, inv_one = norm_forward(resid)
    tokens_grad = grad_hidden + norm_backward(grad_act_one * gain, norm_one, inv_one)

    mod_sums = jnp.stack(
        [
            jnp.sum(grad_act_two * norm_two, axis=1),
            jnp.sum(grad_act_two, axis=1),
            jnp.sum(grad_out * branch_two, axis=1),
        ]
    )
    slots = jnp.arange(sequences) == seq
    slotted = jnp.where(slots[:, None, None], mod_sums[None], 0.0)
    totals = moves.own_sums(slotted.reshape(3 * sequences, width))
    totals = totals.reshape(sequences, 3, feats)
    mod_grad = jnp.einsum("nd,nke->ked", embedded, totals, precision=HIGH)
    norm_sums = jnp.stack([jnp.sum(grad_act_one * norm_one, axis=1), jnp.sum(grad_act_one, axis=1)])
    norm_sums = moves.own_sums(norm_sums)

    return (
        moves.outputs(result.astype(BF16)),
        moves.outputs(tokens_grad.astype(BF16)).astype(F32),
        norm_sums[0],
        norm_sums[1],
        qkv_grad.reshape(qkv_weight.shape),
        out_grad,
        up_grad,
        down_grad,
        mod_grad,
    )


def solution(mesh):
    placed = (
        P("row", ("dp", "col")),
        P("row"),
        P("row"),
        P("row", None, "col"),
        P("col", "row"),
        P("row", "col"),
        P("row", "col"),
        P(None, "row", None),
        P(),
        P(),
        P("row", ("dp", "col")),
    )
    return jax.shard_map(
        local,
        mesh=mesh,
        in_specs=placed,
        out_specs=(
            P("row", ("dp", "col")),
            P("row", ("dp", "col")),
            P("row"),
            P("row"),
            P("row", None, "col"),
            P("col", "row"),
            P("row", "col"),
            P("row", "col"),
            P(None, "row", None),
        ),
        check_vma=False,
    )
```

```python
from functools import partial
import math

import jax
import jax.numpy as jnp
from jax import lax
from jax.experimental import pallas as pl
from jax.experimental.pallas import tpu as pltpu
from jax.sharding import PartitionSpec as P

HEAD_DIM = 64
LENGTH = 2048
CHUNK = 256
EPSILON = 1e-05
HIGH = lax.Precision.HIGHEST
F32 = jnp.float32
BF16 = jnp.bfloat16
GAIN, BIAS, SCALE, SHIFT, GATE = range(5)
CORE, CHIP, ALIGNED, BLOCK = range(4)


def time_embed(steps_in, width_all):
    half_width = width_all // 2
    frequency = jnp.exp(-math.log(10000.0) * jnp.arange(half_width, dtype=F32) / half_width)
    angles = steps_in.astype(F32)[:, None] * frequency[None, :]
    return jnp.concatenate([jnp.sin(angles), jnp.cos(angles)], axis=1)


def rope_tables(length, head_width):
    half_dim = head_width // 2
    frequency = jnp.exp(-math.log(10000.0) * jnp.arange(half_dim, dtype=F32) / half_dim)
    angles = frequency[:, None] * jnp.arange(length, dtype=F32)[None, :]
    return jnp.cos(angles), jnp.sin(angles)


def dot(left, right, left_dim=1, right_dim=0):
    dims = (((left_dim,), (right_dim,)), ((), ()))
    return lax.dot_general(left, right, dims, preferred_element_type=F32)


def call(kernel, name, numbers, inputs, outputs, grid=(1,), scratch=()):
    def spec(shape, block, index):
        if block is None:
            return pl.BlockSpec(shape, lambda *_: (0,) * len(shape))
        return pl.BlockSpec(block, index)

    return pl.pallas_call(
        kernel,
        grid_spec=pltpu.PrefetchScalarGridSpec(
            num_scalar_prefetch=1,
            grid=grid,
            in_specs=[spec(a.shape, block, index) for a, block, index in inputs],
            out_specs=[spec(shape, block, index) for shape, _, block, index in outputs],
            scratch_shapes=list(scratch),
        ),
        out_shape=[jax.ShapeDtypeStruct(shape, dtype) for shape, dtype, _, _ in outputs],
        compiler_params=pltpu.CompilerParams(vmem_limit_bytes=58 * 1024 * 1024),
        cost_estimate=pl.CostEstimate(flops=0, transcendentals=0, bytes_accessed=0),
        name=name,
    )(numbers, *[a for a, _, _ in inputs])


def whole(array):
    return array, None, None


def made(shape, dtype):
    return shape, dtype, None, None


def column(table, row):
    return table[...].T[:, row : row + 1]


def norm_stats(first, second):
    count = first.shape[0] + second.shape[0]
    total = jnp.sum(first, axis=0, keepdims=True) + jnp.sum(second, axis=0, keepdims=True)
    square = jnp.sum(first * first, axis=0, keepdims=True)
    square = square + jnp.sum(second * second, axis=0, keepdims=True)
    mean = total / count
    return mean, lax.rsqrt(square / count - mean * mean + EPSILON)


def project_kernel(
    num, xa, xb, ca, cb, wa, wb, ta, tb, cos_ref, sin_ref, q_ref, k_ref, v_ref, act_ref, weight
):
    step = pl.program_id(0)
    feats = xa.shape[0]

    @pl.when(step == 0)
    def _():
        weight[:, :feats] = wa[...].T
        weight[:, feats:] = wb[...].T

    own = step // 2 == num[CORE]
    first = jnp.where(own, xa[...], ca[...]).astype(F32)
    second = jnp.where(own, xb[...], cb[...]).astype(F32)
    mean, inv_std = norm_stats(first, second)
    first = (first - mean) * inv_std * column(ta, GAIN) + column(ta, BIAS)
    second = (second - mean) * inv_std * column(tb, GAIN) + column(tb, BIAS)
    act_ref[:feats, :] = first.astype(BF16)
    act_ref[feats:, :] = second.astype(BF16)
    projected = dot(weight[...], act_ref[...])
    rows = q_ref.shape[0]
    half = HEAD_DIM // 2
    cosine, sine = cos_ref[...], sin_ref[...]
    for out_ref, base in ((q_ref, 0), (k_ref, rows)):
        for head in range(0, rows, HEAD_DIM):
            front = projected[base + head : base + head + half]
            back = projected[base + head + half : base + head + HEAD_DIM]
            out_ref[head : head + half, :] = (front * cosine - back * sine).astype(BF16)
            out_ref[head + half : head + HEAD_DIM, :] = (back * cosine + front * sine).astype(BF16)
    v_ref[...] = projected[2 * rows :].astype(BF16)


def core_blocks(step, num):
    early = jnp.minimum(step, 1)
    late = jnp.maximum(step - 2, 0)
    flag = num[CORE] == 0
    return jnp.where(flag, early, late), jnp.where(flag, late, early)


def project(num, pieces, weights, tables, cosine, sine):
    feats, tokens = pieces[0].shape
    block = tokens // 2
    columns = weights[0].shape[1]
    rows = columns // 3
    own = lambda s, n: (0, core_blocks(s, n)[0])
    other = lambda s, n: (0, core_blocks(s, n)[1])
    here = lambda s, n: (0, s)
    maps = (own, own, other, other)
    inputs = [(piece, (feats, block), where) for piece, where in zip(pieces, maps)]
    inputs += [whole(w) for w in weights] + [whole(t) for t in tables]
    inputs += [(t, (t.shape[0], block), here) for t in (cosine, sine)]
    outputs = [((rows, 2 * tokens), BF16, (rows, block), here)] * 3
    outputs += [((2 * feats, 2 * tokens), BF16, (2 * feats, block), here)]
    scratch = [pltpu.VMEM((columns, 2 * feats), BF16)]
    return call(project_kernel, "project", num, inputs, outputs, (4,), scratch)


def diagonal_mask(num):
    key_block = lax.broadcasted_iota(jnp.int32, (CHUNK, CHUNK), 0) // num[BLOCK]
    query_block = lax.broadcasted_iota(jnp.int32, (CHUNK, CHUNK), 1) // num[BLOCK]
    return key_block <= query_block


def attend_forward_kernel(num, q_ref, k_ref, v_ref, keep_ref, send_ref, lse_ref, keys):
    keys[...] = k_ref[...].T
    visible = diagonal_mask(num)
    for step in range(q_ref.shape[1] // CHUNK):
        here = slice(step * CHUNK, (step + 1) * CHUNK)
        past = slice(0, step * CHUNK)
        query = q_ref[:, here] * BF16(0.125)
        diag = jnp.where(visible, dot(keys[here, :], query), -1e30)
        top = jnp.max(diag, axis=0, keepdims=True)
        if step:
            scores = dot(keys[past, :], query)
            top = jnp.maximum(top, jnp.max(scores, axis=0, keepdims=True))
        weight = jnp.exp(diag - top)
        total = jnp.sum(weight, axis=0, keepdims=True)
        mixed = dot(v_ref[:, here], weight.astype(BF16))
        if step:
            weight = jnp.exp(scores - top)
            total = total + jnp.sum(weight, axis=0, keepdims=True)
            mixed = mixed + dot(v_ref[:, past], weight.astype(BF16))
        mixed = (mixed / total).astype(BF16)
        lse_ref[0, :, here] = top + jnp.log(total)
        core, chip, part = step // 4, step // 2 % 2, step % 2
        slot = jnp.where(num[CORE] == core, 0, 2) + part
        place = pl.ds(pl.multiple_of(slot * CHUNK, CHUNK), CHUNK)

        @pl.when(num[CHIP] == chip)
        def _():
            keep_ref[:, place] = mixed

        @pl.when(num[CHIP] != chip)
        def _():
            send_ref[:, place] = mixed


def attend_forward(num, queries, keys, values):
    rows, length = queries.shape
    heads = rows // HEAD_DIM
    here = lambda h, n: (h, 0)
    inputs = [(a, (HEAD_DIM, length), here) for a in (queries, keys, values)]
    outputs = [((rows, length // 2), BF16, (HEAD_DIM, length // 2), here)] * 2
    outputs += [((heads, 1, length), F32, (1, 1, length), lambda h, n: (h, 0, 0))]
    scratch = [pltpu.VMEM((length, HEAD_DIM), BF16)]
    return call(attend_forward_kernel, "attend_forward", num, inputs, outputs, (heads,), scratch)


def attend_backward_kernel(
    num, q_ref, k_ref, v_ref, keep_ref, got_ref, lse_ref, cos_ref, sin_ref,
    dq_ref, dk_ref, dv_ref, g_ref, keys, values, queries, grads, key_sum, value_sum,
):
    length = q_ref.shape[1]
    half = HEAD_DIM // 2
    span = length // 4
    for place in range(4):
        core, chip = place // 2, place % 2
        slot = jnp.where(num[CORE] == core, 0, 1)
        there = pl.ds(pl.multiple_of(slot * span, span), span)
        part = jnp.where(num[CHIP] == chip, keep_ref[:, there], got_ref[:, there])
        g_ref[:, place * span : (place + 1) * span] = part
    keys[...] = k_ref[...].T
    values[...] = v_ref[...].T
    queries[...] = (q_ref[...] * BF16(0.125)).T
    grads[...] = g_ref[...].T
    visible = diagonal_mask(num)

    def store_unrotated(out_ref, grad, where):
        front, back = grad[:half], grad[half:]
        cosine, sine = cos_ref[:, where], sin_ref[:, where]
        out_ref[:half, where] = (front * cosine + back * sine).astype(BF16)
        out_ref[half:, where] = (back * cosine - front * sine).astype(BF16)

    for step in range(length // CHUNK):
        here = slice(step * CHUNK, (step + 1) * CHUNK)
        past = slice(0, step * CHUNK)
        query = q_ref[:, here] * BF16(0.125)
        grad = g_ref[:, here]
        lse = lse_ref[0, :, here]
        diag = jnp.where(visible, dot(keys[here, :], query), -1e30)
        weight = jnp.exp(diag - lse)
        grad_weight = dot(values[here, :], grad)
        delta = jnp.sum(weight * grad_weight, axis=0, keepdims=True)
        if step:
            weight_past = jnp.exp(dot(keys[past, :], query) - lse)
            grad_past = dot(values[past, :], grad)
            delta = delta + jnp.sum(weight_past * grad_past, axis=0, keepdims=True)
        grad_score = (weight * (grad_weight - delta)).astype(BF16)
        grad_query = dot(k_ref[:, here], grad_score)
        value_sum[here, :] = dot(weight.astype(BF16), grads[here, :])
        key_sum[here, :] = dot(grad_score, queries[here, :])
        if step:
            grad_score = (weight_past * (grad_past - delta)).astype(BF16)
            grad_query = grad_query + dot(k_ref[:, past], grad_score)
            value_sum[past, :] += dot(weight_past.astype(BF16), grads[here, :])
            key_sum[past, :] += dot(grad_score, queries[here, :])
        store_unrotated(dq_ref, grad_query * 0.125, here)
    store_unrotated(dk_ref, key_sum[...].T, slice(0, length))
    dv_ref[...] = value_sum[...].T.astype(BF16)


def attend_backward(num, queries, keys, values, kept, got, lse, cosine, sine):
    rows, length = queries.shape
    heads = rows // HEAD_DIM
    here = lambda h, n: (h, 0)
    inputs = [(a, (HEAD_DIM, length), here) for a in (queries, keys, values)]
    inputs += [(a, (HEAD_DIM, length // 2), here) for a in (kept, got)]
    inputs += [(lse, (1, 1, length), lambda h, n: (h, 0, 0)), whole(cosine), whole(sine)]
    outputs = [((rows, length), BF16, (HEAD_DIM, length), here)] * 3
    scratch = [pltpu.VMEM((HEAD_DIM, length), BF16)] + [pltpu.VMEM((length, HEAD_DIM), BF16)] * 4
    scratch += [pltpu.VMEM((length, HEAD_DIM), F32)] * 2
    return call(attend_backward_kernel, "attend_backward", num, inputs, outputs, (heads,), scratch)


def mix_kernel(num, keep, got, aa, ba, ab, bb, own_ref, other_ref):
    feats = aa.shape[0]
    heads = keep.shape[0]
    span = own_ref.shape[1]
    aligned = num[ALIGNED] == 1
    mine = jnp.where(aligned, keep[...], got[...])
    theirs = jnp.where(aligned, got[...], keep[...])
    for rows, near, far in ((slice(0, feats), aa, ab), (slice(feats, 2 * feats), ba, bb)):
        total = dot(near[:, :heads], mine) + dot(far[:, :heads], theirs)
        own_ref[rows, :] = total[:, :span]
        other_ref[rows, :] = total[:, span:].astype(BF16)


def mix(num, kept, got, blocks):
    feats = blocks[0].shape[0]
    span = kept.shape[1] // 2
    last = lambda s, n: (0, 3)
    inputs = [whole(kept), whole(got)] + [(b, (feats, 256), last) for b in blocks]
    outputs = [made((2 * feats, span), F32), made((2 * feats, span), BF16)]
    return call(mix_kernel, "mix", num, inputs, outputs)


def enter_kernel(num, own, got, xa, xb, ta, tb, hidden_ref, act_ref):
    feats = xa.shape[0]
    total = own[...] + got[...].astype(F32)
    first = total[:feats] + xa[...].astype(F32)
    second = total[feats:] + xb[...].astype(F32)
    hidden_ref[:feats, :] = first
    hidden_ref[feats:, :] = second
    mean, inv_std = norm_stats(first, second)
    first = (first - mean) * inv_std * (1.0 + column(ta, SCALE)) + column(ta, SHIFT)
    second = (second - mean) * inv_std * (1.0 + column(tb, SCALE)) + column(tb, SHIFT)
    act_ref[:feats, :] = first.astype(BF16)
    act_ref[feats:, :] = second.astype(BF16)


def enter(num, own, got, pieces, tables):
    width, span = own.shape
    chip = lambda s, n: (0, n[CHIP])
    inputs = [whole(own), whole(got)] + [(p, (width // 2, span), chip) for p in pieces]
    inputs += [whole(t) for t in tables]
    outputs = [made((width, span), F32), made((width, span), BF16)]
    return call(enter_kernel, "enter", num, inputs, outputs)


def feed_kernel(
    num, ao_ref, at_ref, go_ref, gt_ref, uaa, uba, uab, ubb, daa, dba, dab, dbb,
    bo_ref, bt_ref, ho_ref, ht_ref, ua_ref, ub_ref, dk_ref, ds_ref, acts, grads, branch, back,
):
    step = pl.program_id(0)
    half_steps = pl.num_programs(0) // 2
    feats = uaa.shape[0]
    span = ao_ref.shape[1]
    near = step < half_steps

    @pl.when(step == 0)
    def _():
        acts[:, :span] = ao_ref[...]
        acts[:, span:] = at_ref[...]
        grads[:, :span] = go_ref[...]
        grads[:, span:] = gt_ref[...]

    up_a = jnp.where(near, uaa[...], uab[...])
    up_b = jnp.where(near, uba[...], ubb[...])
    down_a = jnp.where(near, daa[...], dab[...])
    down_b = jnp.where(near, dba[...], dbb[...])
    act, grad = acts[...], grads[...]
    pre = dot(up_a, act[:feats], 0, 0) + dot(up_b, act[feats:], 0, 0)
    raised = dot(down_a, grad[:feats], 0, 0) + dot(down_b, grad[feats:], 0, 0)
    root = math.sqrt(2.0 / math.pi)
    square = pre * pre
    bent = jnp.tanh(root * pre * (1.0 + 0.044715 * square))
    part = 0.5 + 0.5 * bent
    gelu = (pre * part).astype(BF16)
    slope = part + 0.5 * root * pre * (1.0 - bent * bent) * (1.0 + 3 * 0.044715 * square)
    grad_pre = (raised * slope).astype(BF16)
    for rows, up, down in ((slice(0, feats), up_a, down_a), (slice(feats, 2 * feats), up_b, down_b)):
        forward, backward = dot(down, gelu), dot(up, grad_pre)

        @pl.when(step == 0)
        def _():
            branch[rows, :] = forward
            back[rows, :] = backward

        @pl.when(step > 0)
        def _():
            branch[rows, :] += forward
            back[rows, :] += backward

    ua_ref[...] = dot(act[:feats], grad_pre, 1, 1).astype(BF16)
    ub_ref[...] = dot(act[feats:], grad_pre, 1, 1).astype(BF16)
    down_grad = dot(grad, gelu, 1, 1).astype(BF16)

    @pl.when(near)
    def _():
        dk_ref[...] = down_grad

    @pl.when(jnp.logical_not(near))
    def _():
        ds_ref[...] = down_grad

    @pl.when(step == 2 * half_steps - 1)
    def _():
        bo_ref[...] = branch[:, :span]
        bt_ref[...] = branch[:, span:].astype(BF16)
        ho_ref[...] = back[:, :span]
        ht_ref[...] = back[:, span:].astype(BF16)


def feed(num, acts, grads, ups, downs):
    width, span = acts[0].shape
    feats = width // 2
    hidden = downs[0].shape[1]
    block = 256
    steps = hidden // block
    near = lambda s, n: (0, jnp.minimum(s, steps - 1))
    far = lambda s, n: (0, jnp.maximum(s - steps, 0))
    maps = (near, near, far, far)
    inputs = [whole(a) for a in (*acts, *grads)]
    inputs += [(w, (feats, block), where) for w, where in zip(ups, maps)]
    inputs += [(w, (feats, block), where) for w, where in zip(downs, maps)]
    tokens = [made((width, span), F32), made((width, span), BF16)]
    step = lambda s, n: (0, s)
    outputs = tokens + tokens
    outputs += [((feats, 2 * hidden), BF16, (feats, block), step)] * 2
    outputs += [((width, hidden), BF16, (width, block), near)]
    outputs += [((width, hidden), BF16, (width, block), far)]
    scratch = [pltpu.VMEM((width, 2 * span), BF16)] * 2 + [pltpu.VMEM((width, 2 * span), F32)] * 2
    return call(feed_kernel, "feed", num, inputs, outputs, (2 * steps,), scratch)


def turn_kernel(num, own, got, hidden, ga, gb, ta, tb, grad_ref, one_ref, sums_ref):
    feats = ga.shape[0]
    span = own.shape[1]
    grad = own[...] + got[...].astype(F32)
    values = hidden[...]
    mean, inv_std = norm_stats(values[:feats], values[feats:])
    normed = (values - mean) * inv_std
    cross = grad * normed
    sums_ref[:, 0:1] = jnp.sum(cross, axis=1, keepdims=True)
    sums_ref[:, 1:2] = jnp.sum(grad, axis=1, keepdims=True)
    scale = jnp.concatenate([column(ta, SCALE), column(tb, SCALE)], axis=0) + 1.0
    scaled = grad * scale
    mean_plain = jnp.mean(scaled, axis=0, keepdims=True)
    mean_cross = jnp.mean(scaled * normed, axis=0, keepdims=True)
    back = inv_std * (scaled - mean_plain - normed * mean_cross)
    for rows, grad_out in ((slice(0, feats), ga), (slice(feats, 2 * feats), gb)):
        total = back[rows] + grad_out[...].astype(F32)
        grad_ref[rows, :] = total
        one_ref[rows, :] = total.astype(BF16)


def turn(num, own, got, hidden, cots, tables):
    width, span = own.shape
    chip = lambda s, n: (0, n[CHIP])
    inputs = [whole(own), whole(got), whole(hidden)]
    inputs += [(cots[0], (width // 2, span), chip), whole(cots[1])]
    inputs += [whole(t) for t in tables]
    outputs = [made((width, span), F32), made((width, span), BF16), made((width, 128), F32)]
    return call(turn_kernel, "turn", num, inputs, outputs)


def leave_kernel(num, own, got, hidden, ga, gb, ta, tb, oa_ref, ob_ref, sums_ref):
    feats = ga.shape[0]
    for rows, grad_out, table, out_ref in (
        (slice(0, feats), ga, ta, oa_ref),
        (slice(feats, 2 * feats), gb, tb, ob_ref),
    ):
        branch = own[rows, :] + got[rows, :].astype(F32)
        out_ref[...] = (hidden[rows, :] + (1.0 + column(table, GATE)) * branch).astype(BF16)
        term = grad_out[...].astype(F32) * branch
        sums_ref[rows, 0:1] = jnp.sum(term, axis=1, keepdims=True)


def leave(num, own, got, hidden, cots, tables):
    width, span = own.shape
    chip = lambda s, n: (0, n[CHIP])
    inputs = [whole(own), whole(got), whole(hidden)]
    inputs += [(cots[0], (width // 2, span), chip), whole(cots[1])]
    inputs += [whole(t) for t in tables]
    outputs = [made((width // 2, span), BF16)] * 2 + [made((width, 128), F32)]
    return call(leave_kernel, "leave", num, inputs, outputs)


def unmix_kernel(
    num, one_own, one_other, keep, got, aa, ba, ab, bb, gk_ref, gs_ref, wa_ref, wb_ref
):
    feats = aa.shape[0]
    heads = keep.shape[0]
    span = one_own.shape[1]
    aligned = num[ALIGNED] == 1
    ones = jnp.concatenate([one_own[...], one_other[...]], axis=1)
    near = dot(aa[:, :heads], ones[:feats], 0, 0) + dot(ba[:, :heads], ones[feats:], 0, 0)
    far = dot(ab[:, :heads], ones[:feats], 0, 0) + dot(bb[:, :heads], ones[feats:], 0, 0)
    gk_ref[...] = jnp.where(aligned, near, far).astype(BF16)
    gs_ref[...] = jnp.where(aligned, far, near).astype(BF16)
    mine = jnp.where(aligned, keep[...], got[...])
    theirs = jnp.where(aligned, got[...], keep[...])
    for rows, out_ref in ((slice(0, feats), wa_ref), (slice(feats, 2 * feats), wb_ref)):
        out_ref[:, :heads] = dot(ones[rows], mine, 1, 1).astype(BF16)
        out_ref[:, heads:] = dot(ones[rows], theirs, 1, 1).astype(BF16)


def unmix(num, ones, kept, got, blocks):
    feats = blocks[0].shape[0]
    heads, tokens = kept.shape
    last = lambda s, n: (0, 3)
    inputs = [whole(a) for a in (*ones, kept, got)]
    inputs += [(b, (feats, 256), last) for b in blocks]
    outputs = [made((heads, tokens), BF16)] * 2 + [made((feats, 2 * heads), BF16)] * 2
    return call(unmix_kernel, "unmix", num, inputs, outputs)


def unproject_kernel(num, dq, dk, dv, wa, wb, keep_ref, send_ref):
    step = pl.program_id(0)
    feats = wa.shape[0]
    grad = jnp.concatenate([dq[...], dk[...], dv[...]], axis=0)
    first, second = dot(wa[...], grad), dot(wb[...], grad)
    own = step // 2 == num[CORE]

    @pl.when(own)
    def _():
        keep_ref[:feats, :] = first
        keep_ref[feats:, :] = second

    @pl.when(jnp.logical_not(own))
    def _():
        send_ref[:feats, :] = first.astype(BF16)
        send_ref[feats:, :] = second.astype(BF16)


def unproject(num, grads, weights):
    rows, length = grads[0].shape
    feats = weights[0].shape[0]
    block = length // 4
    here = lambda s, n: (0, s)
    own = lambda s, n: (0, core_blocks(s, n)[0])
    other = lambda s, n: (0, core_blocks(s, n)[1])
    inputs = [(g, (rows, block), here) for g in grads] + [whole(w) for w in weights]
    shape = (2 * feats, length // 2)
    outputs = [(shape, F32, (2 * feats, block), own), (shape, BF16, (2 * feats, block), other)]
    return call(unproject_kernel, "unproject", num, inputs, outputs, (4,))


def weigh_kernel(num, dq, dk, dv, act, wa, wb, ta, tb, ga_ref, gb_ref, sums_ref, total, plain):
    step = pl.program_id(0)
    feats = wa.shape[0]
    grad = jnp.concatenate([dq[...], dk[...], dv[...]], axis=0)
    product = dot(act[...], grad, 1, 1)
    row = dot(jnp.ones((8, grad.shape[1]), BF16), grad, 1, 1)

    @pl.when(step == 0)
    def _():
        total[...] = product
        plain[...] = row

    @pl.when(step > 0)
    def _():
        total[...] += product
        plain[...] += row

    @pl.when(step == pl.num_programs(0) - 1)
    def _():
        for rows, weight, table, out_ref in (
            (slice(0, feats), wa, ta, ga_ref),
            (slice(feats, 2 * feats), wb, tb, gb_ref),
        ):
            grad_weight = total[rows, :]
            out_ref[...] = grad_weight.astype(BF16)
            low = weight[...].astype(F32)
            gain, bias = column(table, GAIN), column(table, BIAS)
            weighed = jnp.sum(low * grad_weight, axis=1, keepdims=True)
            shifted = jnp.sum(low * plain[0:1, :], axis=1, keepdims=True)
            sums_ref[rows, 0:1] = (weighed - bias * shifted) / gain
            sums_ref[rows, 1:2] = shifted


def weigh(num, grads, act, weights, tables):
    rows, length = grads[0].shape
    width = act.shape[0]
    feats, columns = weights[0].shape
    block = length // 4
    here = lambda s, n: (0, s)
    inputs = [(g, (rows, block), here) for g in grads] + [(act, (width, block), here)]
    inputs += [whole(w) for w in weights] + [whole(t) for t in tables]
    outputs = [made((feats, columns), BF16)] * 2 + [made((width, 128), F32)]
    scratch = [pltpu.VMEM((width, columns), F32), pltpu.VMEM((8, columns), F32)]
    return call(weigh_kernel, "weigh", num, inputs, outputs, (4,), scratch)


def finish_kernel(num, own, got, xa, xb, hidden, ta, tb, oa_ref, ob_ref):
    feats = xa.shape[0]
    grad = own[...] + got[...].astype(F32)
    first, second = xa[...].astype(F32), xb[...].astype(F32)
    mean, inv_std = norm_stats(first, second)
    first, second = (first - mean) * inv_std, (second - mean) * inv_std
    grad_a, grad_b = grad[:feats] * column(ta, GAIN), grad[feats:] * column(tb, GAIN)
    count = 2 * feats
    plain = jnp.sum(grad_a, axis=0, keepdims=True) + jnp.sum(grad_b, axis=0, keepdims=True)
    cross = jnp.sum(grad_a * first, axis=0, keepdims=True)
    cross = cross + jnp.sum(grad_b * second, axis=0, keepdims=True)
    plain, cross = plain / count, cross / count
    oa_ref[...] = hidden[:feats, :] + inv_std * (grad_a - plain - first * cross)
    ob_ref[...] = (hidden[feats:, :] + inv_std * (grad_b - plain - second * cross)).astype(BF16)


def finish(num, own, got, pieces, hidden, tables):
    width, span = own.shape
    chip = lambda s, n: (0, n[CHIP])
    inputs = [whole(own), whole(got)] + [(p, (width // 2, span), chip) for p in pieces]
    inputs += [whole(hidden)] + [whole(t) for t in tables]
    outputs = [made((width // 2, span), F32), made((width // 2, span), BF16)]
    return call(finish_kernel, "finish", num, inputs, outputs)


def swap_rows(value):
    count = lax.axis_size("row")
    return lax.ppermute(value, "row", [(i, i ^ 1) for i in range(count)])


def swap_cores(value):
    count = lax.axis_size("col")
    return lax.ppermute(value, "col", [(i, i ^ 1) for i in range(count)])


def swap_cols(value):
    return lax.ppermute(value, "col", [(i, i ^ 2) for i in range(lax.axis_size("col"))])


def swap_dp(value, bit):
    count = lax.axis_size("dp")
    return lax.ppermute(value, "dp", [(i, i ^ bit) for i in range(count)])


def in_order(flag, own, other):
    first = jnp.where(flag == 0, own, other)
    second = jnp.where(flag == 0, other, own)
    return first, second


def cut(value, start, size, axis):
    return lax.dynamic_slice_in_dim(value, start, size, axis)


def after(value, *others):
    return lax.optimization_barrier((value, *others))[0]


def plus(left, right):
    return (left.astype(F32) + right.astype(F32)).astype(BF16)


def reduce_dp(value):
    half = value.shape[0] // 2
    low = lax.axis_index("dp") & 1
    total = plus(cut(value, low * half, half, 0), swap_dp(cut(value, (1 - low) * half, half, 0), 1))
    reach = 2
    while reach < lax.axis_size("dp"):
        total = plus(total, swap_dp(total, reach))
        reach *= 2
    return jnp.concatenate(in_order(low, total, swap_dp(total, 1)), axis=0)


class PairMoves:
    def __init__(self, r, c, feats):
        self.r, self.j, self.h, self.k, self.feats = r, r, c // 2, c % 2, feats
        self.aligned = self.j == self.h

    def pieces(self, value):
        other = swap_rows(value)
        return value, other, swap_cores(value), swap_cores(other)

    def tables(self, mods, gain, bias, seq):
        table = jnp.concatenate([gain[None], bias[None], mods[seq]], axis=0)
        table = jnp.pad(table, ((0, 3), (0, 0)))
        return table, swap_rows(table)

    def cotangents(self, value):
        span = value.shape[1] // 2
        return value, swap_rows(cut(value, (1 - self.j) * span, span, 1))

    def flip(self, value):
        return jnp.concatenate([value[self.feats :], value[: self.feats]], axis=0)

    def qkv(self, weight):
        other = swap_cols(weight)
        mine = jnp.where(self.aligned, weight, other)
        theirs = jnp.where(self.aligned, other, weight)
        return mine, swap_rows(theirs)

    def feed(self, weight):
        other = swap_rows(weight)
        return weight, other, swap_cols(weight), swap_cols(other)

    def reduce_up(self, up_a, up_b, out_a, out_b, sums):
        sums = (sums + swap_cores(sums)).astype(BF16)
        hidden, heads = up_a.shape[1] // 2, out_a.shape[1] // 2
        room = jnp.zeros((self.feats, 256 - heads - sums.shape[1]), BF16)

        def pack(up, out, extra):
            near = [up[:, :hidden], out[:, :heads], extra, room]
            far = [up[:, hidden:], out[:, heads:], extra, room]
            return near, far

        keep = pack(up_a, out_a, sums[: self.feats])
        send = pack(up_b, out_b, sums[self.feats :])
        got = swap_rows(jnp.concatenate(send[0] + send[1], axis=1))
        width = got.shape[1] // 2
        far = plus(jnp.concatenate(keep[1], axis=1), got[:, width:])
        near = plus(jnp.concatenate(keep[0], axis=1), got[:, :width])
        total = reduce_dp(plus(near, swap_cols(far))).astype(F32)
        ends = hidden + heads
        return total[:, :hidden], total[:, hidden:ends].T, total[:, ends : ends + sums.shape[1]]

    def reduce_down(self, near, far):
        part = plus(near, swap_cols(far))
        part = plus(part[: self.feats], swap_rows(part[self.feats :]))
        return reduce_dp(part).astype(F32)

    def reduce_qkv(self, part_a, part_b):
        cycle, corner = [], []
        for core in range(2):
            for row in range(2):
                aligned, beside = row * 4 + 2 * row + core, row * 4 + 2 * (1 - row) + core
                cycle.append((aligned, (1 - row) * 4 + 2 * row + core))
                cycle.append((beside, aligned))
                corner.append((beside, (1 - row) * 4 + 2 * row + core))
        axes = ("row", "col")
        first = lax.ppermute(jnp.where(self.aligned, part_b, part_a), axes, cycle)
        second = lax.ppermute(part_b, axes, corner)
        return reduce_dp(plus(first, jnp.where(self.aligned, part_a, second))).astype(F32)

    def outputs(self, own, other):
        return jnp.concatenate(in_order(self.j, own, swap_rows(other)), axis=1)

    def own_sums(self, sums):
        total = sums[:, : self.feats] + swap_rows(sums[:, self.feats :])
        total = total + swap_cores(total)
        total = total + swap_cols(total)
        reach = 1
        while reach < lax.axis_size("dp"):
            total = total + swap_dp(total, reach)
            reach *= 2
        return total


class AnyMoves:
    def __init__(self, r, c, feats, pairs):
        self.r, self.j, self.q, self.h, self.k = r, r % 2, r // 2, c // 2, c % 2
        self.feats, self.pairs = feats, pairs
        self.half = feats * lax.axis_size("row") // 2
        self.aligned = self.j == 0
        cols = lax.axis_size("col")
        self.cores = [[i, i + 1] for i in range(0, cols, 2)]
        self.likes = [list(range(core, cols, 2)) for core in range(2)]

    def halves(self, value):
        return value[: self.half], value[self.half :]

    def sequence(self, value):
        full = lax.all_gather(value, "row", axis=0, tiled=True)
        full = lax.all_gather(full, "col", axis=1, tiled=True, axis_index_groups=self.cores)
        return cut(full, self.q * LENGTH, LENGTH, 1)

    def pieces(self, value):
        full = self.sequence(value)
        own = cut(full, self.k * LENGTH // 2, LENGTH // 2, 1)
        other = cut(full, (1 - self.k) * LENGTH // 2, LENGTH // 2, 1)
        return *self.halves(own), *self.halves(other)

    def tables(self, mods, gain, bias, seq):
        count = mods.shape[0]
        table = jnp.concatenate([mods.reshape(3 * count, -1), gain[None], bias[None]], axis=0)
        table = lax.all_gather(table, "row", axis=1, tiled=True)
        table = jnp.concatenate([table[3 * count :], cut(table, 3 * seq, 3, 0)], axis=0)
        table = jnp.pad(table, ((0, 3), (0, 0)))
        return table[:, : self.half], table[:, self.half :]

    def cotangents(self, value):
        span = LENGTH // 4
        own = cut(self.sequence(value), (2 * self.k + self.j) * span, span, 1)
        first, second = self.halves(own)
        return jnp.concatenate([first, first], axis=1), second

    def flip(self, value):
        return value

    def likes_gather(self, value):
        rows = lax.all_gather(value, "row", axis=0, tiled=True)
        return lax.all_gather(rows, "col", axis=0, axis_index_groups=self.likes)

    def qkv(self, weight):
        return self.halves(cut(self.likes_gather(weight), self.j, 1, 0)[0])

    def feed(self, weight):
        near, far = self.likes_gather(weight)
        return *self.halves(near), *self.halves(far)

    def scatter(self, grad):
        grad = lax.psum_scatter(grad, "row", scatter_dimension=0, tiled=True)
        grad = lax.psum_scatter(
            grad, "col", scatter_dimension=1, tiled=True, axis_index_groups=self.likes
        )
        return lax.psum(grad, "dp").astype(F32)

    def reduce_up(self, up_a, up_b, out_a, out_b, sums):
        up = self.scatter(jnp.concatenate([up_a, up_b], axis=0))
        out = self.scatter(jnp.concatenate([out_a, out_b], axis=0))
        return up, out.T, self.own_sums(sums.T).T

    def reduce_down(self, near, far):
        return self.scatter(jnp.concatenate([near, far], axis=1))

    def reduce_qkv(self, part_a, part_b):
        grad = jnp.concatenate([part_a, part_b], axis=0)
        both = in_order(self.j, grad, jnp.zeros_like(grad))
        return self.scatter(jnp.concatenate(both, axis=1))

    def outputs(self, own, other):
        value = jnp.concatenate([own.astype(BF16), other], axis=0)
        parts = value.reshape(lax.axis_size("row"), self.feats, -1)
        parts = lax.all_to_all(parts, "row", split_axis=0, concat_axis=0, tiled=True)
        parts = lax.all_gather(parts, "col", axis=0, axis_index_groups=self.cores)
        span = parts.shape[-1]
        parts = parts.reshape(2, self.pairs, 2, self.feats, span).transpose(3, 1, 0, 2, 4)
        parts = parts.reshape(self.feats, -1)
        width = parts.shape[1] // 2
        return cut(parts, self.k * width, width, 1)

    def own_sums(self, sums):
        total = lax.psum(sums, ("dp", "row", "col"))
        return cut(total, self.r * self.feats, self.feats, 1)


def local(
    tokens, ln_gain, ln_bias, qkv_weight, out_weight, up_weight, down_weight,
    mod_weight, timestep, block_size, cotangent,
):
    rows, cols = lax.axis_size("row"), lax.axis_size("col")
    r, c, z = lax.axis_index("row"), lax.axis_index("col"), lax.axis_index("dp")
    width = mod_weight.shape[2]
    feats, local_tokens = tokens.shape
    pairs = 2 * local_tokens // LENGTH
    assert rows == 2 * pairs and cols == 4 and LENGTH % (8 * CHUNK) == 0
    sequences = timestep.shape[0]
    seq = (z * (cols // 2) + c // 2) * pairs + r // 2
    moves = PairMoves(r, c, feats) if pairs == 1 else AnyMoves(r, c, feats, pairs)
    block_len = cut(block_size, seq, 1, 0)[0]
    num = jnp.stack([moves.k, moves.j, moves.aligned.astype(jnp.int32), block_len])

    embedded = time_embed(timestep, width)
    mods = jnp.einsum("nd,ked->nke", embedded, mod_weight.astype(F32), precision=HIGH)
    cosine, sine = rope_tables(LENGTH, HEAD_DIM)

    pieces = moves.pieces(tokens)
    tables = moves.tables(mods, ln_gain, ln_bias, seq)
    qkv = moves.qkv(qkv_weight.reshape(feats, -1))
    heads = out_weight.shape[0]
    packed = jnp.pad(jnp.concatenate([up_weight, out_weight.T], axis=1), ((0, 0), (0, 256 - heads)))
    ups = moves.feed(packed)
    downs = moves.feed(down_weight)
    cots = moves.cotangents(cotangent)

    queries, keys, values, act_one = project(num, pieces, qkv, tables, cosine, sine)
    kept, sent, lse = attend_forward(num, queries, keys, values)
    got = swap_rows(sent)

    own, other = mix(num, kept, got, ups)
    hidden, act = enter(num, own, swap_cores(other), pieces[:2], tables)
    span = act.shape[1]
    gate_a, gate_b = tables[0][4][:, None], tables[1][4][:, None]
    cot_a = cut(cots[0], moves.j * span, span, 1).astype(F32)
    grad_a = cot_a * (1.0 + gate_a)
    grad_b = cots[1].astype(F32) * (1.0 + gate_b)
    grad_two = jnp.concatenate([grad_a, grad_b], axis=0).astype(BF16)
    grads = (grad_two, swap_cores(grad_two))
    fed = feed(num, (act, swap_cores(act)), grads, ups, downs)
    branch_own, branch_other, back_own, back_other, up_a, up_b, down_near, down_far = fed
    down_grad = moves.reduce_down(down_near, down_far)
    back_got = swap_cores(back_other)
    grad_hidden, ones, turn_sums = turn(num, back_own, back_got, hidden, cots, tables)
    branch_got = swap_cores(branch_other)
    result_a, result_b, leave_sums = leave(num, branch_own, branch_got, hidden, cots, tables)
    result = moves.outputs(result_a, result_b)
    both_ones = (ones, swap_cores(ones))
    grad_kept, grad_sent, out_a, out_b = unmix(num, both_ones, kept, got, ups)
    grad_got = swap_rows(grad_sent)
    sums = jnp.concatenate([turn_sums[:, :2], leave_sums[:, :1]], axis=1)
    slots = jnp.arange(sequences) == seq
    sums = jnp.where(slots[None, :, None], sums[:, None, :], 0.0).reshape(width, -1)
    up_grad, out_grad, totals = moves.reduce_up(up_a, up_b, out_a, out_b, sums)
    totals = totals.reshape(feats, sequences, 3)
    mod_grad = jnp.einsum("nd,enk->ked", embedded, totals, precision=HIGH)

    grads = attend_backward(
        num, queries, keys, values, grad_kept, grad_got, lse, cosine, sine
    )
    keep, send = unproject(num, grads, qkv)
    qkv_a, qkv_b, norm_sums = weigh(num, grads, act_one, qkv, tables)
    qkv_grad = moves.reduce_qkv(qkv_a, qkv_b)
    norm_sums = moves.own_sums(norm_sums[:, :2].T)
    kept_core = keep + swap_cores(send).astype(F32)
    crossing = cut(kept_core, (1 - moves.j) * span, span, 1).astype(BF16)
    crossed = swap_rows(moves.flip(crossing))
    own = cut(kept_core, moves.j * span, span, 1)
    tokens_a, tokens_b = finish(num, own, crossed, pieces[:2], grad_hidden, tables)
    tokens_grad = moves.outputs(tokens_a, tokens_b)

    return (
        result,
        tokens_grad.astype(F32),
        norm_sums[0],
        norm_sums[1],
        qkv_grad.reshape(qkv_weight.shape),
        out_grad,
        up_grad,
        down_grad,
        mod_grad,
    )


def solution(mesh):
    placed = (
        P("row", ("dp", "col")),
        P("row"),
        P("row"),
        P("row", None, "col"),
        P("col", "row"),
        P("row", "col"),
        P("row", "col"),
        P(None, "row", None),
        P(),
        P(),
        P("row", ("dp", "col")),
    )
    return jax.shard_map(
        local,
        mesh=mesh,
        in_specs=placed,
        out_specs=(
            P("row", ("dp", "col")),
            P("row", ("dp", "col")),
            P("row"),
            P("row"),
            P("row", None, "col"),
            P("col", "row"),
            P("row", "col"),
            P("row", "col"),
            P(None, "row", None),
        ),
        check_vma=False,
    )
```

```python
from functools import partial
import math

import jax
import jax.numpy as jnp
from jax import lax
from jax.experimental import pallas as pl
from jax.experimental.pallas import tpu as pltpu
from jax.sharding import PartitionSpec as P

HEAD_DIM = 64
LENGTH = 2048
CHUNK = 256
EPSILON = 1e-05
HIGH = lax.Precision.HIGHEST
F32 = jnp.float32
BF16 = jnp.bfloat16
SCALE_T = 0.03
MICROS = dict(project=9, attend_forward=26, mix=5, enter=5, feed=32, turn=6, leave=5, unmix=5, attend_backward=33,
              unproject=8, weigh=9, finish=5)
FLOPS = {k: int(v * SCALE_T * 1_153_000_000) for k, v in MICROS.items()}
GAIN, BIAS, SCALE, SHIFT, GATE = range(5)
CORE, CHIP, ALIGNED, BLOCK = range(4)


def time_embed(steps_in, width_all):
    half_width = width_all // 2
    frequency = jnp.exp(-math.log(10000.0) * jnp.arange(half_width, dtype=F32) / half_width)
    angles = steps_in.astype(F32)[:, None] * frequency[None, :]
    return jnp.concatenate([jnp.sin(angles), jnp.cos(angles)], axis=1)


def rope_tables(length, head_width):
    half_dim = head_width // 2
    frequency = jnp.exp(-math.log(10000.0) * jnp.arange(half_dim, dtype=F32) / half_dim)
    angles = frequency[:, None] * jnp.arange(length, dtype=F32)[None, :]
    return jnp.cos(angles), jnp.sin(angles)


def dot(left, right, left_dim=1, right_dim=0):
    dims = (((left_dim,), (right_dim,)), ((), ()))
    return lax.dot_general(left, right, dims, preferred_element_type=F32)


def call(kernel, name, numbers, inputs, outputs, grid=(1,), scratch=()):
    def spec(shape, block, index):
        if block is None:
            return pl.BlockSpec(shape, lambda *_: (0,) * len(shape))
        return pl.BlockSpec(block, index)

    return pl.pallas_call(
        kernel,
        grid_spec=pltpu.PrefetchScalarGridSpec(
            num_scalar_prefetch=1,
            grid=grid,
            in_specs=[spec(a.shape, block, index) for a, block, index in inputs],
            out_specs=[spec(shape, block, index) for shape, _, block, index in outputs],
            scratch_shapes=list(scratch),
        ),
        out_shape=[jax.ShapeDtypeStruct(shape, dtype) for shape, dtype, _, _ in outputs],
        compiler_params=pltpu.CompilerParams(vmem_limit_bytes=58 * 1024 * 1024),
        cost_estimate=pl.CostEstimate(flops=FLOPS[name], transcendentals=0, bytes_accessed=0),
        name=name,
    )(numbers, *[a for a, _, _ in inputs])


def whole(array):
    return array, None, None


def made(shape, dtype):
    return shape, dtype, None, None


def column(table, row):
    return table[...].T[:, row : row + 1]


def norm_stats(first, second):
    count = first.shape[0] + second.shape[0]
    total = jnp.sum(first, axis=0, keepdims=True) + jnp.sum(second, axis=0, keepdims=True)
    square = jnp.sum(first * first, axis=0, keepdims=True)
    square = square + jnp.sum(second * second, axis=0, keepdims=True)
    mean = total / count
    return mean, lax.rsqrt(square / count - mean * mean + EPSILON)


def project_kernel(
    num, xa, xb, ca, cb, wa, wb, ta, tb, cos_ref, sin_ref, q_ref, k_ref, v_ref, act_ref, weight
):
    step = pl.program_id(0)
    feats = xa.shape[0]

    @pl.when(step == 0)
    def _():
        weight[:, :feats] = wa[...].T
        weight[:, feats:] = wb[...].T

    own = step // 2 == num[CORE]
    first = jnp.where(own, xa[...], ca[...]).astype(F32)
    second = jnp.where(own, xb[...], cb[...]).astype(F32)
    mean, inv_std = norm_stats(first, second)
    first = (first - mean) * inv_std * column(ta, GAIN) + column(ta, BIAS)
    second = (second - mean) * inv_std * column(tb, GAIN) + column(tb, BIAS)
    act_ref[:feats, :] = first.astype(BF16)
    act_ref[feats:, :] = second.astype(BF16)
    projected = dot(weight[...], act_ref[...])
    rows = q_ref.shape[0]
    half = HEAD_DIM // 2
    cosine, sine = cos_ref[...], sin_ref[...]
    for out_ref, base in ((q_ref, 0), (k_ref, rows)):
        for head in range(0, rows, HEAD_DIM):
            front = projected[base + head : base + head + half]
            back = projected[base + head + half : base + head + HEAD_DIM]
            out_ref[head : head + half, :] = (front * cosine - back * sine).astype(BF16)
            out_ref[head + half : head + HEAD_DIM, :] = (back * cosine + front * sine).astype(BF16)
    v_ref[...] = projected[2 * rows :].astype(BF16)


def core_blocks(step, num):
    early = jnp.minimum(step, 1)
    late = jnp.maximum(step - 2, 0)
    flag = num[CORE] == 0
    return jnp.where(flag, early, late), jnp.where(flag, late, early)


def project(num, pieces, weights, tables, cosine, sine):
    feats, tokens = pieces[0].shape
    block = tokens // 2
    columns = weights[0].shape[1]
    rows = columns // 3
    own = lambda s, n: (0, core_blocks(s, n)[0])
    other = lambda s, n: (0, core_blocks(s, n)[1])
    here = lambda s, n: (0, s)
    maps = (own, own, other, other)
    inputs = [(piece, (feats, block), where) for piece, where in zip(pieces, maps)]
    inputs += [whole(w) for w in weights] + [whole(t) for t in tables]
    inputs += [(t, (t.shape[0], block), here) for t in (cosine, sine)]
    outputs = [((rows, 2 * tokens), BF16, (rows, block), here)] * 3
    outputs += [((2 * feats, 2 * tokens), BF16, (2 * feats, block), here)]
    scratch = [pltpu.VMEM((columns, 2 * feats), BF16)]
    return call(project_kernel, "project", num, inputs, outputs, (4,), scratch)


def diagonal_mask(num):
    key_block = lax.broadcasted_iota(jnp.int32, (CHUNK, CHUNK), 0) // num[BLOCK]
    query_block = lax.broadcasted_iota(jnp.int32, (CHUNK, CHUNK), 1) // num[BLOCK]
    return key_block <= query_block


def attend_forward_kernel(num, q_ref, k_ref, v_ref, keep_ref, send_ref, lse_ref, keys):
    keys[...] = k_ref[...].T
    visible = diagonal_mask(num)
    for step in range(q_ref.shape[1] // CHUNK):
        here = slice(step * CHUNK, (step + 1) * CHUNK)
        past = slice(0, step * CHUNK)
        query = q_ref[:, here] * BF16(0.125)
        diag = jnp.where(visible, dot(keys[here, :], query), -1e30)
        top = jnp.max(diag, axis=0, keepdims=True)
        if step:
            scores = dot(keys[past, :], query)
            top = jnp.maximum(top, jnp.max(scores, axis=0, keepdims=True))
        weight = jnp.exp(diag - top)
        total = jnp.sum(weight, axis=0, keepdims=True)
        mixed = dot(v_ref[:, here], weight.astype(BF16))
        if step:
            weight = jnp.exp(scores - top)
            total = total + jnp.sum(weight, axis=0, keepdims=True)
            mixed = mixed + dot(v_ref[:, past], weight.astype(BF16))
        mixed = (mixed / total).astype(BF16)
        lse_ref[0, :, here] = top + jnp.log(total)
        core, chip, part = step // 4, step // 2 % 2, step % 2
        slot = jnp.where(num[CORE] == core, 0, 2) + part
        place = pl.ds(pl.multiple_of(slot * CHUNK, CHUNK), CHUNK)

        @pl.when(num[CHIP] == chip)
        def _():
            keep_ref[:, place] = mixed

        @pl.when(num[CHIP] != chip)
        def _():
            send_ref[:, place] = mixed


def attend_forward(num, first, count, queries, keys, values):
    length = queries.shape[1]
    rows = count * HEAD_DIM
    there = lambda h, n: (first + h, 0)
    here = lambda h, n: (h, 0)
    inputs = [(a, (HEAD_DIM, length), there) for a in (queries, keys, values)]
    outputs = [((rows, length // 2), BF16, (HEAD_DIM, length // 2), here)] * 2
    outputs += [((count, 1, length), F32, (1, 1, length), lambda h, n: (h, 0, 0))]
    scratch = [pltpu.VMEM((length, HEAD_DIM), BF16)]
    return call(attend_forward_kernel, "attend_forward", num, inputs, outputs, (count,), scratch)


def attend_backward_kernel(
    num, q_ref, k_ref, v_ref, keep_ref, got_ref, lse_ref, cos_ref, sin_ref,
    dq_ref, dk_ref, dv_ref, g_ref, keys, values, queries, grads, key_sum, value_sum,
):
    length = q_ref.shape[1]
    half = HEAD_DIM // 2
    span = length // 4
    for place in range(4):
        core, chip = place // 2, place % 2
        slot = jnp.where(num[CORE] == core, 0, 1)
        there = pl.ds(pl.multiple_of(slot * span, span), span)
        part = jnp.where(num[CHIP] == chip, keep_ref[:, there], got_ref[:, there])
        g_ref[:, place * span : (place + 1) * span] = part
    keys[...] = k_ref[...].T
    values[...] = v_ref[...].T
    queries[...] = (q_ref[...] * BF16(0.125)).T
    grads[...] = g_ref[...].T
    visible = diagonal_mask(num)

    def store_unrotated(out_ref, grad, where):
        front, back = grad[:half], grad[half:]
        cosine, sine = cos_ref[:, where], sin_ref[:, where]
        out_ref[:half, where] = (front * cosine + back * sine).astype(BF16)
        out_ref[half:, where] = (back * cosine - front * sine).astype(BF16)

    for step in range(length // CHUNK):
        here = slice(step * CHUNK, (step + 1) * CHUNK)
        past = slice(0, step * CHUNK)
        query = q_ref[:, here] * BF16(0.125)
        grad = g_ref[:, here]
        lse = lse_ref[0, :, here]
        diag = jnp.where(visible, dot(keys[here, :], query), -1e30)
        weight = jnp.exp(diag - lse)
        grad_weight = dot(values[here, :], grad)
        delta = jnp.sum(weight * grad_weight, axis=0, keepdims=True)
        if step:
            weight_past = jnp.exp(dot(keys[past, :], query) - lse)
            grad_past = dot(values[past, :], grad)
            delta = delta + jnp.sum(weight_past * grad_past, axis=0, keepdims=True)
        grad_score = (weight * (grad_weight - delta)).astype(BF16)
        grad_query = dot(k_ref[:, here], grad_score)
        value_sum[here, :] = dot(weight.astype(BF16), grads[here, :])
        key_sum[here, :] = dot(grad_score, queries[here, :])
        if step:
            grad_score = (weight_past * (grad_past - delta)).astype(BF16)
            grad_query = grad_query + dot(k_ref[:, past], grad_score)
            value_sum[past, :] += dot(weight_past.astype(BF16), grads[here, :])
            key_sum[past, :] += dot(grad_score, queries[here, :])
        store_unrotated(dq_ref, grad_query * 0.125, here)
    store_unrotated(dk_ref, key_sum[...].T, slice(0, length))
    dv_ref[...] = value_sum[...].T.astype(BF16)


def attend_backward(num, queries, keys, values, kept, got, lse, cosine, sine):
    rows, length = queries.shape
    heads = rows // HEAD_DIM
    here = lambda h, n: (h, 0)
    inputs = [(a, (HEAD_DIM, length), here) for a in (queries, keys, values)]
    inputs += [(a, (HEAD_DIM, length // 2), here) for a in (kept, got)]
    inputs += [(lse, (1, 1, length), lambda h, n: (h, 0, 0)), whole(cosine), whole(sine)]
    outputs = [((rows, length), BF16, (HEAD_DIM, length), here)] * 3
    scratch = [pltpu.VMEM((HEAD_DIM, length), BF16)] + [pltpu.VMEM((length, HEAD_DIM), BF16)] * 4
    scratch += [pltpu.VMEM((length, HEAD_DIM), F32)] * 2
    return call(attend_backward_kernel, "attend_backward", num, inputs, outputs, (heads,), scratch)


def sorted_heads(num, kept, got):
    aligned = num[ALIGNED] == 1
    kept = jnp.concatenate([k[...] for k in kept], axis=0)
    got = jnp.concatenate([g[...] for g in got], axis=0)
    return jnp.where(aligned, kept, got), jnp.where(aligned, got, kept)


def mix_kernel(num, *refs):
    count = (len(refs) - 6) // 2
    aa, ba, ab, bb, own_ref, other_ref = refs[2 * count :]
    feats = aa.shape[0]
    mine, theirs = sorted_heads(num, refs[:count], refs[count : 2 * count])
    heads = mine.shape[0]
    span = own_ref.shape[1]
    for rows, near, far in ((slice(0, feats), aa, ab), (slice(feats, 2 * feats), ba, bb)):
        total = dot(near[:, :heads], mine) + dot(far[:, :heads], theirs)
        own_ref[rows, :] = total[:, :span]
        other_ref[rows, :] = total[:, span:].astype(BF16)


def mix(num, kept, got, blocks):
    feats = blocks[0].shape[0]
    span = kept[0].shape[1] // 2
    last = lambda s, n: (0, 3)
    inputs = [whole(a) for a in (*kept, *got)] + [(b, (feats, 256), last) for b in blocks]
    outputs = [made((2 * feats, span), F32), made((2 * feats, span), BF16)]
    return call(mix_kernel, "mix", num, inputs, outputs)


def enter_kernel(num, own, got, xa, xb, ta, tb, hidden_ref, act_ref):
    feats = xa.shape[0]
    total = own[...] + got[...].astype(F32)
    first = total[:feats] + xa[...].astype(F32)
    second = total[feats:] + xb[...].astype(F32)
    hidden_ref[:feats, :] = first
    hidden_ref[feats:, :] = second
    mean, inv_std = norm_stats(first, second)
    first = (first - mean) * inv_std * (1.0 + column(ta, SCALE)) + column(ta, SHIFT)
    second = (second - mean) * inv_std * (1.0 + column(tb, SCALE)) + column(tb, SHIFT)
    act_ref[:feats, :] = first.astype(BF16)
    act_ref[feats:, :] = second.astype(BF16)


def enter(num, own, got, pieces, tables):
    width, span = own.shape
    chip = lambda s, n: (0, n[CHIP])
    inputs = [whole(own), whole(got)] + [(p, (width // 2, span), chip) for p in pieces]
    inputs += [whole(t) for t in tables]
    outputs = [made((width, span), F32), made((width, span), BF16)]
    return call(enter_kernel, "enter", num, inputs, outputs)


def feed_kernel(
    num, ao_ref, at_ref, go_ref, gt_ref, uaa, uba, uab, ubb, daa, dba, dab, dbb,
    bo_ref, bt_ref, ho_ref, ht_ref, uk_ref, us_ref, dk_ref, ds_ref, acts, grads, branch, back,
):
    step = pl.program_id(0)
    half_steps = pl.num_programs(0) // 2
    feats = uaa.shape[0]
    span = ao_ref.shape[1]
    near = step < half_steps

    @pl.when(step == 0)
    def _():
        acts[:, :span] = ao_ref[...]
        acts[:, span:] = at_ref[...]
        grads[:, :span] = go_ref[...]
        grads[:, span:] = gt_ref[...]

    up_a = jnp.where(near, uaa[...], uab[...])
    up_b = jnp.where(near, uba[...], ubb[...])
    down_a = jnp.where(near, daa[...], dab[...])
    down_b = jnp.where(near, dba[...], dbb[...])
    act, grad = acts[...], grads[...]
    pre = dot(up_a, act[:feats], 0, 0) + dot(up_b, act[feats:], 0, 0)
    raised = dot(down_a, grad[:feats], 0, 0) + dot(down_b, grad[feats:], 0, 0)
    root = math.sqrt(2.0 / math.pi)
    square = pre * pre
    bent = jnp.tanh(root * pre * (1.0 + 0.044715 * square))
    part = 0.5 + 0.5 * bent
    gelu = (pre * part).astype(BF16)
    slope = part + 0.5 * root * pre * (1.0 - bent * bent) * (1.0 + 3 * 0.044715 * square)
    grad_pre = (raised * slope).astype(BF16)
    for rows, up, down in ((slice(0, feats), up_a, down_a), (slice(feats, 2 * feats), up_b, down_b)):
        forward, backward = dot(down, gelu), dot(up, grad_pre)

        @pl.when(step == 0)
        def _():
            branch[rows, :] = forward
            back[rows, :] = backward

        @pl.when(step > 0)
        def _():
            branch[rows, :] += forward
            back[rows, :] += backward

    up_grad = dot(act, grad_pre, 1, 1).astype(BF16)
    down_grad = dot(grad, gelu, 1, 1).astype(BF16)

    @pl.when(near)
    def _():
        uk_ref[...] = up_grad
        dk_ref[...] = down_grad

    @pl.when(jnp.logical_not(near))
    def _():
        us_ref[...] = up_grad
        ds_ref[...] = down_grad

    @pl.when(step == 2 * half_steps - 1)
    def _():
        bo_ref[...] = branch[:, :span]
        bt_ref[...] = branch[:, span:].astype(BF16)
        ho_ref[...] = back[:, :span]
        ht_ref[...] = back[:, span:].astype(BF16)


def feed(num, acts, grads, ups, downs):
    width, span = acts[0].shape
    feats = width // 2
    hidden = downs[0].shape[1]
    block = 256
    steps = hidden // block
    near = lambda s, n: (0, jnp.minimum(s, steps - 1))
    far = lambda s, n: (0, jnp.maximum(s - steps, 0))
    maps = (near, near, far, far)
    inputs = [whole(a) for a in (*acts, *grads)]
    inputs += [(w, (feats, block), where) for w, where in zip(ups, maps)]
    inputs += [(w, (feats, block), where) for w, where in zip(downs, maps)]
    tokens = [made((width, span), F32), made((width, span), BF16)]
    outputs = tokens + tokens
    outputs += [((width, hidden), BF16, (width, block), where) for where in (near, far)] * 2
    scratch = [pltpu.VMEM((width, 2 * span), BF16)] * 2 + [pltpu.VMEM((width, 2 * span), F32)] * 2
    return call(feed_kernel, "feed", num, inputs, outputs, (2 * steps,), scratch)


def turn_kernel(num, own, got, hidden, ga, gb, ta, tb, grad_ref, one_ref, sums_ref):
    feats = ga.shape[0]
    span = own.shape[1]
    grad = own[...] + got[...].astype(F32)
    values = hidden[...]
    mean, inv_std = norm_stats(values[:feats], values[feats:])
    normed = (values - mean) * inv_std
    cross = grad * normed
    sums_ref[:, 0:1] = jnp.sum(cross, axis=1, keepdims=True)
    sums_ref[:, 1:2] = jnp.sum(grad, axis=1, keepdims=True)
    scale = jnp.concatenate([column(ta, SCALE), column(tb, SCALE)], axis=0) + 1.0
    scaled = grad * scale
    mean_plain = jnp.mean(scaled, axis=0, keepdims=True)
    mean_cross = jnp.mean(scaled * normed, axis=0, keepdims=True)
    back = inv_std * (scaled - mean_plain - normed * mean_cross)
    for rows, grad_out in ((slice(0, feats), ga), (slice(feats, 2 * feats), gb)):
        total = back[rows] + grad_out[...].astype(F32)
        grad_ref[rows, :] = total
        one_ref[rows, :] = total.astype(BF16)


def turn(num, own, got, hidden, cots, tables):
    width, span = own.shape
    chip = lambda s, n: (0, n[CHIP])
    inputs = [whole(own), whole(got), whole(hidden)]
    inputs += [(cots[0], (width // 2, span), chip), whole(cots[1])]
    inputs += [whole(t) for t in tables]
    outputs = [made((width, span), F32), made((width, span), BF16), made((width, 128), F32)]
    return call(turn_kernel, "turn", num, inputs, outputs)


def leave_kernel(num, own, got, hidden, ga, gb, ta, tb, oa_ref, ob_ref, sums_ref):
    feats = ga.shape[0]
    for rows, grad_out, table, out_ref in (
        (slice(0, feats), ga, ta, oa_ref),
        (slice(feats, 2 * feats), gb, tb, ob_ref),
    ):
        branch = own[rows, :] + got[rows, :].astype(F32)
        out_ref[...] = (hidden[rows, :] + (1.0 + column(table, GATE)) * branch).astype(BF16)
        term = grad_out[...].astype(F32) * branch
        sums_ref[rows, 0:1] = jnp.sum(term, axis=1, keepdims=True)


def leave(num, own, got, hidden, cots, tables):
    width, span = own.shape
    chip = lambda s, n: (0, n[CHIP])
    inputs = [whole(own), whole(got), whole(hidden)]
    inputs += [(cots[0], (width // 2, span), chip), whole(cots[1])]
    inputs += [whole(t) for t in tables]
    outputs = [made((width // 2, span), BF16)] * 2 + [made((width, 128), F32)]
    return call(leave_kernel, "leave", num, inputs, outputs)


def unmix_kernel(num, one_own, one_other, *refs):
    count = (len(refs) - 8) // 2
    aa, ba, ab, bb, gk_ref, gs_ref, wn_ref, wf_ref = refs[2 * count :]
    feats = aa.shape[0]
    aligned = num[ALIGNED] == 1
    mine, theirs = sorted_heads(num, refs[:count], refs[count : 2 * count])
    heads = mine.shape[0]
    ones = jnp.concatenate([one_own[...], one_other[...]], axis=1)
    near = dot(aa[:, :heads], ones[:feats], 0, 0) + dot(ba[:, :heads], ones[feats:], 0, 0)
    far = dot(ab[:, :heads], ones[:feats], 0, 0) + dot(bb[:, :heads], ones[feats:], 0, 0)
    gk_ref[...] = jnp.where(aligned, near, far).astype(BF16)
    gs_ref[...] = jnp.where(aligned, far, near).astype(BF16)
    wn_ref[...] = dot(ones, mine, 1, 1).astype(BF16)
    wf_ref[...] = dot(ones, theirs, 1, 1).astype(BF16)


def unmix(num, ones, kept, got, blocks):
    feats = blocks[0].shape[0]
    heads, tokens = sum(k.shape[0] for k in kept), kept[0].shape[1]
    last = lambda s, n: (0, 3)
    inputs = [whole(a) for a in (*ones, *kept, *got)]
    inputs += [(b, (feats, 256), last) for b in blocks]
    outputs = [made((heads, tokens), BF16)] * 2 + [made((2 * feats, heads), BF16)] * 2
    return call(unmix_kernel, "unmix", num, inputs, outputs)


def unproject_kernel(num, *refs):
    wa, wb, keep_ref, send_ref = refs[-4:]
    step = pl.program_id(0)
    feats = wa.shape[0]
    grad = jnp.concatenate([g[...] for g in refs[:-4]], axis=0)
    first, second = dot(wa[...], grad), dot(wb[...], grad)
    own = step // 2 == num[CORE]

    @pl.when(own)
    def _():
        keep_ref[:feats, :] = first
        keep_ref[feats:, :] = second

    @pl.when(jnp.logical_not(own))
    def _():
        send_ref[:feats, :] = first.astype(BF16)
        send_ref[feats:, :] = second.astype(BF16)


def unproject(num, grads, weights):
    rows, length = grads[0].shape
    feats = weights[0].shape[0]
    block = length // 4
    here = lambda s, n: (0, s)
    own = lambda s, n: (0, core_blocks(s, n)[0])
    other = lambda s, n: (0, core_blocks(s, n)[1])
    inputs = [(g, (rows, block), here) for g in grads] + [whole(w) for w in weights]
    shape = (2 * feats, length // 2)
    outputs = [(shape, F32, (2 * feats, block), own), (shape, BF16, (2 * feats, block), other)]
    return call(unproject_kernel, "unproject", num, inputs, outputs, (4,))


def weigh_kernel(num, *refs):
    act, wa, wb, ta, tb, ga_ref, gb_ref, first_ref, sums_ref, total, plain = refs[-11:]
    step = pl.program_id(0)
    feats = wa.shape[0]
    grad = jnp.concatenate([g[...] for g in refs[:-11]], axis=0)
    product = dot(act[...], grad, 1, 1)
    row = dot(jnp.ones((8, grad.shape[1]), BF16), grad, 1, 1)

    @pl.when(step == 0)
    def _():
        total[...] = product
        plain[...] = row

    @pl.when(step > 0)
    def _():
        total[...] += product
        plain[...] += row

    @pl.when(step == pl.num_programs(0) - 1)
    def _():
        for rows, weight, table, out_ref in (
            (slice(0, feats), wa, ta, ga_ref),
            (slice(feats, 2 * feats), wb, tb, gb_ref),
        ):
            grad_weight = total[rows, :]
            out_ref[...] = grad_weight.astype(BF16)
            low = weight[...].astype(F32)
            gain, bias = column(table, GAIN), column(table, BIAS)
            weighed = jnp.sum(low * grad_weight, axis=1, keepdims=True)
            shifted = jnp.sum(low * plain[0:1, :], axis=1, keepdims=True)
            sums_ref[rows, 0:1] = (weighed - bias * shifted) / gain
            sums_ref[rows, 1:2] = shifted
        first_ref[...] = jnp.where(num[ALIGNED] == 1, gb_ref[...], ga_ref[...])


def weigh(num, grads, act, weights, tables):
    rows, length = grads[0].shape
    width = act.shape[0]
    feats, columns = weights[0].shape
    block = length // 4
    here = lambda s, n: (0, s)
    inputs = [(g, (rows, block), here) for g in grads] + [(act, (width, block), here)]
    inputs += [whole(w) for w in weights] + [whole(t) for t in tables]
    outputs = [made((feats, columns), BF16)] * 3 + [made((width, 128), F32)]
    scratch = [pltpu.VMEM((width, columns), F32), pltpu.VMEM((8, columns), F32)]
    return call(weigh_kernel, "weigh", num, inputs, outputs, (4,), scratch)


def finish_kernel(num, own, got, xa, xb, hidden, ta, tb, oa_ref, ob_ref):
    feats = xa.shape[0]
    grad = own[...] + got[...].astype(F32)
    first, second = xa[...].astype(F32), xb[...].astype(F32)
    mean, inv_std = norm_stats(first, second)
    first, second = (first - mean) * inv_std, (second - mean) * inv_std
    grad_a, grad_b = grad[:feats] * column(ta, GAIN), grad[feats:] * column(tb, GAIN)
    count = 2 * feats
    plain = jnp.sum(grad_a, axis=0, keepdims=True) + jnp.sum(grad_b, axis=0, keepdims=True)
    cross = jnp.sum(grad_a * first, axis=0, keepdims=True)
    cross = cross + jnp.sum(grad_b * second, axis=0, keepdims=True)
    plain, cross = plain / count, cross / count
    oa_ref[...] = hidden[:feats, :] + inv_std * (grad_a - plain - first * cross)
    ob_ref[...] = (hidden[feats:, :] + inv_std * (grad_b - plain - second * cross)).astype(BF16)


def finish(num, own, got, pieces, hidden, tables):
    width, span = own.shape
    chip = lambda s, n: (0, n[CHIP])
    inputs = [whole(own), whole(got)] + [(p, (width // 2, span), chip) for p in pieces]
    inputs += [whole(hidden)] + [whole(t) for t in tables]
    outputs = [made((width // 2, span), F32), made((width // 2, span), BF16)]
    return call(finish_kernel, "finish", num, inputs, outputs)


def swap_rows(value):
    count = lax.axis_size("row")
    return lax.ppermute(value, "row", [(i, i ^ 1) for i in range(count)])


def swap_cores(value):
    count = lax.axis_size("col")
    return lax.ppermute(value, "col", [(i, i ^ 1) for i in range(count)])


def swap_cols(value):
    return lax.ppermute(value, "col", [(i, i ^ 2) for i in range(lax.axis_size("col"))])


def swap_dp(value, bit):
    count = lax.axis_size("dp")
    return lax.ppermute(value, "dp", [(i, i ^ bit) for i in range(count)])


def in_order(flag, own, other):
    first = jnp.where(flag == 0, own, other)
    second = jnp.where(flag == 0, other, own)
    return first, second


def cut(value, start, size, axis):
    return lax.dynamic_slice_in_dim(value, start, size, axis)


def after(value, *others):
    return lax.optimization_barrier((value, *others))[0]


def plus(left, right):
    return (left.astype(F32) + right.astype(F32)).astype(BF16)


def dp_first(value):
    half = value.shape[0] // 2
    low = lax.axis_index("dp") & 1
    return plus(cut(value, low * half, half, 0), swap_dp(cut(value, (1 - low) * half, half, 0), 1))


def dp_second(total):
    reach = 2
    while reach < lax.axis_size("dp"):
        total = plus(total, swap_dp(total, reach))
        reach *= 2
    return total


def dp_third(total):
    low = lax.axis_index("dp") & 1
    return jnp.concatenate(in_order(low, total, swap_dp(total, 1)), axis=0).astype(F32)


class PairMoves:
    def __init__(self, r, c, feats, heads):
        self.r, self.j, self.h, self.k, self.feats, self.heads = r, r, c // 2, c % 2, feats, heads
        self.aligned = self.j == self.h

    def pieces(self, value):
        other = swap_rows(value)
        return value, other, swap_cores(value), swap_cores(other)

    def tables(self, mods, gain, bias, seq):
        table = jnp.concatenate([gain[None], bias[None], mods[seq]], axis=0)
        table = jnp.pad(table, ((0, 3), (0, 0)))
        return table, swap_rows(table)

    def cotangents(self, value):
        span = value.shape[1] // 2
        return value, swap_rows(cut(value, (1 - self.j) * span, span, 1))

    def flip(self, value):
        return jnp.concatenate([value[self.feats :], value[: self.feats]], axis=0)

    def qkv(self, weight):
        other = swap_cols(weight)
        mine = jnp.where(self.aligned, weight, other)
        theirs = jnp.where(self.aligned, other, weight)
        self.gate_col = other
        return mine, swap_rows(theirs)

    def feed(self, weight, gate):
        other = swap_rows(after(weight, gate))
        return weight, other, swap_cols(after(weight, self.gate_col)), None

    def corner(self, blocks, gate):
        return *blocks[:3], swap_cols(after(blocks[1], gate))

    first, second, third = map(staticmethod, (dp_first, dp_second, dp_third))

    def across(self, near, got):
        part = plus(near, got)
        return part[: self.feats], swap_rows(part[self.feats :])

    def down_columns(self, near, far):
        return near, swap_cols(far)

    def extras(self, out_near, out_far, sums):
        sums = (sums + swap_cores(sums)).astype(BF16)
        room = jnp.zeros((sums.shape[0], 256 - self.heads - sums.shape[1]), BF16)
        both = jnp.concatenate([out_near, sums, room, out_far, sums, room], axis=1)
        return both[: self.feats], swap_rows(both[self.feats :])

    def extras_last(self, mine, got):
        both = plus(mine, got)
        return both[:, :256], swap_cols(both[:, 256:])

    def join(self, up, mine, got):
        return jnp.concatenate([up, plus(mine, got)], axis=1)

    def unpack(self, total, count):
        hidden = total.shape[1] - 256
        ends = hidden + self.heads
        return total[:, :hidden], total[:, hidden:ends].T, total[:, ends : ends + count]

    def reduce_qkv(self, part_a, part_b, first):
        cycle, corner = [], []
        for core in range(2):
            for row in range(2):
                aligned, beside = row * 4 + 2 * row + core, row * 4 + 2 * (1 - row) + core
                cycle.append((aligned, (1 - row) * 4 + 2 * row + core))
                cycle.append((beside, aligned))
                corner.append((beside, (1 - row) * 4 + 2 * row + core))
        axes = ("row", "col")
        first = lax.ppermute(first, axes, cycle)
        second = lax.ppermute(part_b, axes, corner)
        return first, second, part_a

    def qkv_sum(self, first, second, part_a):
        return plus(first, jnp.where(self.aligned, part_a, second))

    def outputs(self, own, other):
        return jnp.concatenate(in_order(self.j, own, swap_rows(other)), axis=1)

    def own_sums(self, sums):
        total = sums[:, : self.feats] + swap_rows(sums[:, self.feats :])
        total = total + swap_cores(total)
        total = total + swap_cols(total)
        reach = 1
        while reach < lax.axis_size("dp"):
            total = total + swap_dp(total, reach)
            reach *= 2
        return total


class AnyMoves:
    def __init__(self, r, c, feats, heads, pairs):
        self.heads = heads
        self.r, self.j, self.q, self.h, self.k = r, r % 2, r // 2, c // 2, c % 2
        self.feats, self.pairs = feats, pairs
        self.half = feats * lax.axis_size("row") // 2
        self.aligned = self.j == 0
        cols = lax.axis_size("col")
        self.cores = [[i, i + 1] for i in range(0, cols, 2)]
        self.likes = [list(range(core, cols, 2)) for core in range(2)]

    def halves(self, value):
        return value[: self.half], value[self.half :]

    def sequence(self, value):
        full = lax.all_gather(value, "row", axis=0, tiled=True)
        full = lax.all_gather(full, "col", axis=1, tiled=True, axis_index_groups=self.cores)
        return cut(full, self.q * LENGTH, LENGTH, 1)

    def pieces(self, value):
        full = self.sequence(value)
        own = cut(full, self.k * LENGTH // 2, LENGTH // 2, 1)
        other = cut(full, (1 - self.k) * LENGTH // 2, LENGTH // 2, 1)
        return *self.halves(own), *self.halves(other)

    def tables(self, mods, gain, bias, seq):
        count = mods.shape[0]
        table = jnp.concatenate([mods.reshape(3 * count, -1), gain[None], bias[None]], axis=0)
        table = lax.all_gather(table, "row", axis=1, tiled=True)
        table = jnp.concatenate([table[3 * count :], cut(table, 3 * seq, 3, 0)], axis=0)
        table = jnp.pad(table, ((0, 3), (0, 0)))
        return table[:, : self.half], table[:, self.half :]

    def cotangents(self, value):
        span = LENGTH // 4
        own = cut(self.sequence(value), (2 * self.k + self.j) * span, span, 1)
        first, second = self.halves(own)
        return jnp.concatenate([first, first], axis=1), second

    def flip(self, value):
        return value

    def likes_gather(self, value):
        rows = lax.all_gather(value, "row", axis=0, tiled=True)
        return lax.all_gather(rows, "col", axis=0, axis_index_groups=self.likes)

    def qkv(self, weight):
        return self.halves(cut(self.likes_gather(weight), self.j, 1, 0)[0])

    def feed(self, weight, gate):
        near, far = self.likes_gather(weight)
        return *self.halves(near), *self.halves(far)

    def corner(self, blocks, gate):
        return blocks

    def scatter(self, grad):
        grad = lax.psum_scatter(grad, "row", scatter_dimension=0, tiled=True)
        grad = lax.psum_scatter(
            grad, "col", scatter_dimension=1, tiled=True, axis_index_groups=self.likes
        )
        return lax.psum(grad, "dp").astype(F32)

    def first(self, value):
        return value

    second = third = first

    def down_columns(self, near, far):
        return near, far

    def across(self, near, far):
        grad = self.scatter(jnp.concatenate([near, far], axis=1))
        return grad, jnp.zeros_like(grad)

    def extras(self, out_near, out_far, sums):
        return jnp.concatenate([out_near, out_far], axis=1), sums

    def extras_last(self, both, sums):
        return self.scatter(both), self.own_sums(sums.T).T

    def join(self, up, out, sums):
        return up, out, sums

    def unpack(self, total, count):
        up, out, sums = total
        return up.astype(F32), out.T, sums

    def reduce_qkv(self, part_a, part_b, first):
        grad = jnp.concatenate([part_a, part_b], axis=0)
        both = in_order(self.j, grad, jnp.zeros_like(grad))
        total = self.scatter(jnp.concatenate(both, axis=1))
        return total, total, total

    def qkv_sum(self, first, second, part_a):
        return first

    def outputs(self, own, other):
        value = jnp.concatenate([own.astype(BF16), other], axis=0)
        parts = value.reshape(lax.axis_size("row"), self.feats, -1)
        parts = lax.all_to_all(parts, "row", split_axis=0, concat_axis=0, tiled=True)
        parts = lax.all_gather(parts, "col", axis=0, axis_index_groups=self.cores)
        span = parts.shape[-1]
        parts = parts.reshape(2, self.pairs, 2, self.feats, span).transpose(3, 1, 0, 2, 4)
        parts = parts.reshape(self.feats, -1)
        width = parts.shape[1] // 2
        return cut(parts, self.k * width, width, 1)

    def own_sums(self, sums):
        total = lax.psum(sums, ("dp", "row", "col"))
        return cut(total, self.r * self.feats, self.feats, 1)


def local(
    tokens, ln_gain, ln_bias, qkv_weight, out_weight, up_weight, down_weight,
    mod_weight, timestep, block_size, cotangent,
):
    rows, cols = lax.axis_size("row"), lax.axis_size("col")
    r, c, z = lax.axis_index("row"), lax.axis_index("col"), lax.axis_index("dp")
    width = mod_weight.shape[2]
    feats, local_tokens = tokens.shape
    pairs = 2 * local_tokens // LENGTH
    assert rows == 2 * pairs and cols == 4 and LENGTH % (8 * CHUNK) == 0
    sequences = timestep.shape[0]
    seq = (z * (cols // 2) + c // 2) * pairs + r // 2
    heads = out_weight.shape[0]
    moves = PairMoves(r, c, feats, heads) if pairs == 1 else AnyMoves(r, c, feats, heads, pairs)
    block_len = cut(block_size, seq, 1, 0)[0]
    num = jnp.stack([moves.k, moves.j, moves.aligned.astype(jnp.int32), block_len])

    embedded = time_embed(timestep, width)
    mods = jnp.einsum("nd,ked->nke", embedded, mod_weight.astype(F32), precision=HIGH)
    cosine, sine = rope_tables(LENGTH, HEAD_DIM)

    pieces = moves.pieces(tokens)
    tables = moves.tables(mods, ln_gain, ln_bias, seq)
    qkv = moves.qkv(qkv_weight.reshape(feats, -1))
    packed = jnp.pad(jnp.concatenate([up_weight, out_weight.T], axis=1), ((0, 0), (0, 256 - heads)))
    gate = after(qkv[1], pieces[1])
    ups = moves.feed(packed, gate)
    downs = moves.feed(down_weight, gate)

    queries, keys, values, act_one = project(num, pieces, qkv, tables, cosine, sine)
    cots = moves.cotangents(after(cotangent, queries))
    count = heads // HEAD_DIM
    early, early_sent, early_lse = attend_forward(num, 0, 1, queries, keys, values)
    ups = moves.corner(ups, early)
    early_got = swap_rows(early_sent)
    rest = after(queries, early_sent)
    late, late_sent, late_lse = attend_forward(num, 1, count - 1, rest, keys, values)
    kept, got = (early, late), (early_got, swap_rows(late_sent))
    downs = moves.corner(downs, late)
    lse = jnp.concatenate([early_lse, late_lse], axis=0)

    span = cots[1].shape[1]
    gate_a, gate_b = tables[0][4][:, None], tables[1][4][:, None]
    cots = after(cots, late)
    cot_a = cut(cots[0], moves.j * span, span, 1).astype(F32)
    grad_a = cot_a * (1.0 + gate_a)
    grad_b = cots[1].astype(F32) * (1.0 + gate_b)
    grad_two = jnp.concatenate([grad_a, grad_b], axis=0).astype(BF16)
    grads = (grad_two, swap_cores(grad_two))
    own, other = mix(num, (after(kept[0], ups, grads, downs[:3]), kept[1]), got, ups)
    hidden, act = enter(num, own, swap_cores(other), pieces[:2], tables)
    fed = feed(num, (act, swap_cores(act)), grads, ups, downs)
    branch_own, branch_other, back_own, back_other, up_near, up_far, down_near, down_far = fed
    back_got = swap_cores(back_other)
    grad_hidden, ones, turn_sums = turn(num, back_own, back_got, hidden, cots, tables)
    down_part = moves.down_columns(down_near, down_far)
    up_part = moves.down_columns(up_near, up_far)
    branch_got = swap_cores(branch_other)
    both_ones = (ones, swap_cores(ones))
    grad_kept, grad_sent, out_near, out_far = unmix(num, both_ones, kept, got, ups)
    grad_got = swap_rows(grad_sent)
    branch_own = after(branch_own, grad_sent)
    result_a, result_b, leave_sums = leave(num, branch_own, branch_got, hidden, cots, tables)
    result = moves.outputs(result_a, result_b)
    down_part = moves.across(*after(down_part, result_a))
    sums = jnp.concatenate([turn_sums[:, :2], leave_sums[:, :1]], axis=1)
    slots = jnp.arange(sequences) == seq
    sums = jnp.where(slots[None, :, None], sums[:, None, :], 0.0).reshape(width, -1)
    extra = moves.extras(out_near, out_far, sums)

    grad_kept = after(grad_kept, result_a, down_part[0], extra[0])
    grads = attend_backward(num, queries, keys, values, grad_kept, grad_got, lse, cosine, sine)
    up_part, down_part, extra = after((up_part, down_part, extra), grads[0])
    up_part = moves.across(*up_part)
    down_sum = plus(*down_part)
    extra = moves.extras_last(*extra)
    down_sum = moves.first(down_sum)
    weigh_in = after(grads, up_part[0], extra[0])
    qkv_a, qkv_b, qkv_first, norm_sums = weigh(num, weigh_in, act_one, qkv, tables)
    qkv_part = moves.reduce_qkv(qkv_a, qkv_b, qkv_first)
    down_sum = moves.second(after(down_sum, qkv_a))
    keep, send = unproject(num, after(grads, qkv_a), qkv)
    kept_core = keep + swap_cores(send).astype(F32)
    qkv_part = moves.qkv_sum(*qkv_part)
    crossing = cut(after(kept_core, qkv_part), (1 - moves.j) * span, span, 1).astype(BF16)
    crossing = moves.flip(crossing)
    crossed = swap_rows(crossing)
    own = cut(kept_core, moves.j * span, span, 1)
    up_part, extra, qkv_part = after((up_part, extra, qkv_part), crossing)
    up_sum = moves.first(moves.join(plus(*up_part), *extra))
    qkv_sum = moves.first(qkv_part)
    crossed = after(crossed, up_sum, qkv_sum, down_sum)
    tokens_a, tokens_b = finish(num, own, crossed, pieces[:2], grad_hidden, tables)
    tokens_grad = moves.outputs(tokens_a, tokens_b)
    norm_sums = moves.own_sums(after(norm_sums[:, :2], tokens_b).T)
    up_sum, qkv_sum = moves.second(up_sum), moves.second(qkv_sum)
    down_grad = moves.third(after(down_sum, tokens_b)).astype(F32)
    up_grad, out_grad, totals = moves.unpack(moves.third(up_sum), 3 * sequences)
    totals = totals.reshape(feats, sequences, 3)
    mod_grad = jnp.einsum("nd,enk->ked", embedded, totals, precision=HIGH)
    qkv_grad = moves.third(qkv_sum).astype(F32)

    return (
        result,
        tokens_grad.astype(F32),
        norm_sums[0],
        norm_sums[1],
        qkv_grad.reshape(qkv_weight.shape),
        out_grad,
        up_grad,
        down_grad,
        mod_grad,
    )


def solution(mesh):
    placed = (
        P("row", ("dp", "col")),
        P("row"),
        P("row"),
        P("row", None, "col"),
        P("col", "row"),
        P("row", "col"),
        P("row", "col"),
        P(None, "row", None),
        P(),
        P(),
        P("row", ("dp", "col")),
    )
    return jax.shard_map(
        local,
        mesh=mesh,
        in_specs=placed,
        out_specs=(
            P("row", ("dp", "col")),
            P("row", ("dp", "col")),
            P("row"),
            P("row"),
            P("row", None, "col"),
            P("col", "row"),
            P("row", "col"),
            P("row", "col"),
            P(None, "row", None),
        ),
        check_vma=False,
    )
```

```python
from functools import partial
import math

import jax
import jax.numpy as jnp
from jax import lax
from jax.experimental import pallas as pl
from jax.experimental.pallas import tpu as pltpu
from jax.sharding import PartitionSpec as P

HEAD_DIM = 64
LENGTH = 2048
CHUNK = 256
EPSILON = 1e-05
HIGH = lax.Precision.HIGHEST
F32 = jnp.float32
BF16 = jnp.bfloat16
SCALE_T = 0.03
MICROS = dict(project=9, attend_forward=26, mix=5, enter=5, feed=32, turn=6, leave=5, unmix=5, attend_backward=33,
              unproject=30, weigh=30, finish=5)
FULL = ("weigh", "unproject", "finish")
FLOPS = {k: int(v * (1.0 if k in FULL else SCALE_T) * 1_153_000_000) for k, v in MICROS.items()}
GAIN, BIAS, SCALE, SHIFT, GATE = range(5)
CORE, CHIP, ALIGNED, BLOCK, SLOT = range(5)


def time_embed(steps_in, width_all):
    half_width = width_all // 2
    frequency = jnp.exp(-math.log(10000.0) * jnp.arange(half_width, dtype=F32) / half_width)
    angles = steps_in.astype(F32)[:, None] * frequency[None, :]
    return jnp.concatenate([jnp.sin(angles), jnp.cos(angles)], axis=1)


def rope_tables(length, head_width):
    half_dim = head_width // 2
    frequency = jnp.exp(-math.log(10000.0) * jnp.arange(half_dim, dtype=F32) / half_dim)
    angles = frequency[:, None] * jnp.arange(length, dtype=F32)[None, :]
    return jnp.cos(angles), jnp.sin(angles)


def dot(left, right, left_dim=1, right_dim=0):
    dims = (((left_dim,), (right_dim,)), ((), ()))
    return lax.dot_general(left, right, dims, preferred_element_type=F32)


def call(kernel, name, numbers, inputs, outputs, grid=(1,), scratch=()):
    def spec(shape, block, index):
        if block is None:
            return pl.BlockSpec(shape, lambda *_: (0,) * len(shape))
        return pl.BlockSpec(block, index)

    return pl.pallas_call(
        kernel,
        grid_spec=pltpu.PrefetchScalarGridSpec(
            num_scalar_prefetch=1,
            grid=grid,
            in_specs=[spec(a.shape, block, index) for a, block, index in inputs],
            out_specs=[spec(shape, block, index) for shape, _, block, index in outputs],
            scratch_shapes=list(scratch),
        ),
        out_shape=[jax.ShapeDtypeStruct(shape, dtype) for shape, dtype, _, _ in outputs],
        compiler_params=pltpu.CompilerParams(vmem_limit_bytes=58 * 1024 * 1024),
        cost_estimate=pl.CostEstimate(flops=FLOPS[name], transcendentals=0, bytes_accessed=0),
        name=name,
    )(numbers, *[a for a, _, _ in inputs])


def whole(array):
    return array, None, None


def made(shape, dtype):
    return shape, dtype, None, None


def column(table, row):
    return table[...].T[:, row : row + 1]


def norm_stats(first, second):
    count = first.shape[0] + second.shape[0]
    total = jnp.sum(first, axis=0, keepdims=True) + jnp.sum(second, axis=0, keepdims=True)
    square = jnp.sum(first * first, axis=0, keepdims=True)
    square = square + jnp.sum(second * second, axis=0, keepdims=True)
    mean = total / count
    return mean, lax.rsqrt(square / count - mean * mean + EPSILON)


def project_kernel(
    num, xa, xb, ca, cb, wa, wb, ta, tb, cos_ref, sin_ref, q_ref, k_ref, v_ref, act_ref, weight
):
    step = pl.program_id(0)
    feats = xa.shape[0]

    @pl.when(step == 0)
    def _():
        weight[:, :feats] = wa[...].T
        weight[:, feats:] = wb[...].T

    own = step // 2 == num[CORE]
    first = jnp.where(own, xa[...], ca[...]).astype(F32)
    second = jnp.where(own, xb[...], cb[...]).astype(F32)
    mean, inv_std = norm_stats(first, second)
    first = (first - mean) * inv_std * column(ta, GAIN) + column(ta, BIAS)
    second = (second - mean) * inv_std * column(tb, GAIN) + column(tb, BIAS)
    act_ref[:feats, :] = first.astype(BF16)
    act_ref[feats:, :] = second.astype(BF16)
    projected = dot(weight[...], act_ref[...])
    rows = q_ref.shape[0]
    half = HEAD_DIM // 2
    cosine, sine = cos_ref[...], sin_ref[...]
    for out_ref, base in ((q_ref, 0), (k_ref, rows)):
        for head in range(0, rows, HEAD_DIM):
            front = projected[base + head : base + head + half]
            back = projected[base + head + half : base + head + HEAD_DIM]
            out_ref[head : head + half, :] = (front * cosine - back * sine).astype(BF16)
            out_ref[head + half : head + HEAD_DIM, :] = (back * cosine + front * sine).astype(BF16)
    v_ref[...] = projected[2 * rows :].astype(BF16)


def core_blocks(step, num):
    early = jnp.minimum(step, 1)
    late = jnp.maximum(step - 2, 0)
    flag = num[CORE] == 0
    return jnp.where(flag, early, late), jnp.where(flag, late, early)


def project(num, pieces, weights, tables, cosine, sine):
    feats, tokens = pieces[0].shape
    block = tokens // 2
    columns = weights[0].shape[1]
    rows = columns // 3
    own = lambda s, n: (0, core_blocks(s, n)[0])
    other = lambda s, n: (0, core_blocks(s, n)[1])
    here = lambda s, n: (0, s)
    maps = (own, own, other, other)
    inputs = [(piece, (feats, block), where) for piece, where in zip(pieces, maps)]
    inputs += [whole(w) for w in weights] + [whole(t) for t in tables]
    inputs += [(t, (t.shape[0], block), here) for t in (cosine, sine)]
    outputs = [((rows, 2 * tokens), BF16, (rows, block), here)] * 3
    outputs += [((2 * feats, 2 * tokens), BF16, (2 * feats, block), here)]
    scratch = [pltpu.VMEM((columns, 2 * feats), BF16)]
    return call(project_kernel, "project", num, inputs, outputs, (4,), scratch)


def diagonal_mask(num):
    key_block = lax.broadcasted_iota(jnp.int32, (CHUNK, CHUNK), 0) // num[BLOCK]
    query_block = lax.broadcasted_iota(jnp.int32, (CHUNK, CHUNK), 1) // num[BLOCK]
    return key_block <= query_block


def attend_forward_kernel(num, q_ref, k_ref, v_ref, keep_ref, send_ref, lse_ref, keys):
    keys[...] = k_ref[...].T
    visible = diagonal_mask(num)
    for step in range(q_ref.shape[1] // CHUNK):
        here = slice(step * CHUNK, (step + 1) * CHUNK)
        past = slice(0, step * CHUNK)
        query = q_ref[:, here] * BF16(0.125)
        diag = jnp.where(visible, dot(keys[here, :], query), -1e30)
        top = jnp.max(diag, axis=0, keepdims=True)
        if step:
            scores = dot(keys[past, :], query)
            top = jnp.maximum(top, jnp.max(scores, axis=0, keepdims=True))
        weight = jnp.exp(diag - top)
        total = jnp.sum(weight, axis=0, keepdims=True)
        mixed = dot(v_ref[:, here], weight.astype(BF16))
        if step:
            weight = jnp.exp(scores - top)
            total = total + jnp.sum(weight, axis=0, keepdims=True)
            mixed = mixed + dot(v_ref[:, past], weight.astype(BF16))
        mixed = (mixed / total).astype(BF16)
        lse_ref[0, :, here] = top + jnp.log(total)
        core, chip, part = step // 4, step // 2 % 2, step % 2
        slot = jnp.where(num[CORE] == core, 0, 2) + part
        place = pl.ds(pl.multiple_of(slot * CHUNK, CHUNK), CHUNK)

        @pl.when(num[CHIP] == chip)
        def _():
            keep_ref[:, place] = mixed

        @pl.when(num[CHIP] != chip)
        def _():
            send_ref[:, place] = mixed


def attend_forward(num, first, count, queries, keys, values):
    length = queries.shape[1]
    rows = count * HEAD_DIM
    there = lambda h, n: (first + h, 0)
    here = lambda h, n: (h, 0)
    inputs = [(a, (HEAD_DIM, length), there) for a in (queries, keys, values)]
    outputs = [((rows, length // 2), BF16, (HEAD_DIM, length // 2), here)] * 2
    outputs += [((count, 1, length), F32, (1, 1, length), lambda h, n: (h, 0, 0))]
    scratch = [pltpu.VMEM((length, HEAD_DIM), BF16)]
    return call(attend_forward_kernel, "attend_forward", num, inputs, outputs, (count,), scratch)


def attend_backward_kernel(
    num, q_ref, k_ref, v_ref, keep_ref, got_ref, lse_ref, cos_ref, sin_ref,
    dq_ref, dk_ref, dv_ref, g_ref, keys, values, queries, grads, key_sum, value_sum,
):
    length = q_ref.shape[1]
    half = HEAD_DIM // 2
    span = length // 4
    for place in range(4):
        core, chip = place // 2, place % 2
        slot = jnp.where(num[CORE] == core, 0, 1)
        there = pl.ds(pl.multiple_of(slot * span, span), span)
        part = jnp.where(num[CHIP] == chip, keep_ref[:, there], got_ref[:, there])
        g_ref[:, place * span : (place + 1) * span] = part
    keys[...] = k_ref[...].T
    values[...] = v_ref[...].T
    queries[...] = (q_ref[...] * BF16(0.125)).T
    grads[...] = g_ref[...].T
    visible = diagonal_mask(num)

    def store_unrotated(out_ref, grad, where):
        front, back = grad[:half], grad[half:]
        cosine, sine = cos_ref[:, where], sin_ref[:, where]
        out_ref[:half, where] = (front * cosine + back * sine).astype(BF16)
        out_ref[half:, where] = (back * cosine - front * sine).astype(BF16)

    for step in range(length // CHUNK):
        here = slice(step * CHUNK, (step + 1) * CHUNK)
        past = slice(0, step * CHUNK)
        query = q_ref[:, here] * BF16(0.125)
        grad = g_ref[:, here]
        lse = lse_ref[0, :, here]
        diag = jnp.where(visible, dot(keys[here, :], query), -1e30)
        weight = jnp.exp(diag - lse)
        grad_weight = dot(values[here, :], grad)
        delta = jnp.sum(weight * grad_weight, axis=0, keepdims=True)
        if step:
            weight_past = jnp.exp(dot(keys[past, :], query) - lse)
            grad_past = dot(values[past, :], grad)
            delta = delta + jnp.sum(weight_past * grad_past, axis=0, keepdims=True)
        grad_score = (weight * (grad_weight - delta)).astype(BF16)
        grad_query = dot(k_ref[:, here], grad_score)
        value_sum[here, :] = dot(weight.astype(BF16), grads[here, :])
        key_sum[here, :] = dot(grad_score, queries[here, :])
        if step:
            grad_score = (weight_past * (grad_past - delta)).astype(BF16)
            grad_query = grad_query + dot(k_ref[:, past], grad_score)
            value_sum[past, :] += dot(weight_past.astype(BF16), grads[here, :])
            key_sum[past, :] += dot(grad_score, queries[here, :])
        store_unrotated(dq_ref, grad_query * 0.125, here)
    store_unrotated(dk_ref, key_sum[...].T, slice(0, length))
    dv_ref[...] = value_sum[...].T.astype(BF16)


def attend_backward(num, queries, keys, values, kept, got, lse, cosine, sine):
    rows, length = queries.shape
    heads = rows // HEAD_DIM
    here = lambda h, n: (h, 0)
    inputs = [(a, (HEAD_DIM, length), here) for a in (queries, keys, values)]
    inputs += [(a, (HEAD_DIM, length // 2), here) for a in (kept, got)]
    inputs += [(lse, (1, 1, length), lambda h, n: (h, 0, 0)), whole(cosine), whole(sine)]
    outputs = [((rows, length), BF16, (HEAD_DIM, length), here)] * 3
    scratch = [pltpu.VMEM((HEAD_DIM, length), BF16)] + [pltpu.VMEM((length, HEAD_DIM), BF16)] * 4
    scratch += [pltpu.VMEM((length, HEAD_DIM), F32)] * 2
    return call(attend_backward_kernel, "attend_backward", num, inputs, outputs, (heads,), scratch)


def sorted_heads(num, kept, got):
    aligned = num[ALIGNED] == 1
    kept = jnp.concatenate([k[...] for k in kept], axis=0)
    got = jnp.concatenate([g[...] for g in got], axis=0)
    return jnp.where(aligned, kept, got), jnp.where(aligned, got, kept)


def mix_kernel(num, *refs):
    count = (len(refs) - 6) // 2
    aa, ba, ab, bb, own_ref, other_ref = refs[2 * count :]
    feats = aa.shape[0]
    mine, theirs = sorted_heads(num, refs[:count], refs[count : 2 * count])
    heads = mine.shape[0]
    span = own_ref.shape[1]
    for rows, near, far in ((slice(0, feats), aa, ab), (slice(feats, 2 * feats), ba, bb)):
        total = dot(near[:, :heads], mine) + dot(far[:, :heads], theirs)
        own_ref[rows, :] = total[:, :span]
        other_ref[rows, :] = total[:, span:].astype(BF16)


def mix(num, kept, got, blocks):
    feats = blocks[0].shape[0]
    span = kept[0].shape[1] // 2
    last = lambda s, n: (0, 3)
    inputs = [whole(a) for a in (*kept, *got)] + [(b, (feats, 256), last) for b in blocks]
    outputs = [made((2 * feats, span), F32), made((2 * feats, span), BF16)]
    return call(mix_kernel, "mix", num, inputs, outputs)


def enter_kernel(num, own, got, xa, xb, ta, tb, hidden_ref, act_ref):
    feats = xa.shape[0]
    total = own[...] + got[...].astype(F32)
    first = total[:feats] + xa[...].astype(F32)
    second = total[feats:] + xb[...].astype(F32)
    hidden_ref[:feats, :] = first
    hidden_ref[feats:, :] = second
    mean, inv_std = norm_stats(first, second)
    first = (first - mean) * inv_std * (1.0 + column(ta, SCALE)) + column(ta, SHIFT)
    second = (second - mean) * inv_std * (1.0 + column(tb, SCALE)) + column(tb, SHIFT)
    act_ref[:feats, :] = first.astype(BF16)
    act_ref[feats:, :] = second.astype(BF16)


def enter(num, own, got, pieces, tables):
    width, span = own.shape
    chip = lambda s, n: (0, n[CHIP])
    inputs = [whole(own), whole(got)] + [(p, (width // 2, span), chip) for p in pieces]
    inputs += [whole(t) for t in tables]
    outputs = [made((width, span), F32), made((width, span), BF16)]
    return call(enter_kernel, "enter", num, inputs, outputs)


def feed_kernel(
    num, ao_ref, at_ref, go_ref, gt_ref, uaa, uba, uab, ubb, daa, dba, dab, dbb,
    bo_ref, bt_ref, ho_ref, ht_ref, uk_ref, us_ref, dk_ref, ds_ref, acts, grads, branch, back,
):
    step = pl.program_id(0)
    half_steps = pl.num_programs(0) // 2
    feats = uaa.shape[0]
    span = ao_ref.shape[1]
    near = step < half_steps

    @pl.when(step == 0)
    def _():
        acts[:, :span] = ao_ref[...]
        acts[:, span:] = at_ref[...]
        grads[:, :span] = go_ref[...]
        grads[:, span:] = gt_ref[...]

    up_a = jnp.where(near, uaa[...], uab[...])
    up_b = jnp.where(near, uba[...], ubb[...])
    down_a = jnp.where(near, daa[...], dab[...])
    down_b = jnp.where(near, dba[...], dbb[...])
    act, grad = acts[...], grads[...]
    pre = dot(up_a, act[:feats], 0, 0) + dot(up_b, act[feats:], 0, 0)
    raised = dot(down_a, grad[:feats], 0, 0) + dot(down_b, grad[feats:], 0, 0)
    root = math.sqrt(2.0 / math.pi)
    square = pre * pre
    bent = jnp.tanh(root * pre * (1.0 + 0.044715 * square))
    part = 0.5 + 0.5 * bent
    gelu = (pre * part).astype(BF16)
    slope = part + 0.5 * root * pre * (1.0 - bent * bent) * (1.0 + 3 * 0.044715 * square)
    grad_pre = (raised * slope).astype(BF16)
    for rows, up, down in ((slice(0, feats), up_a, down_a), (slice(feats, 2 * feats), up_b, down_b)):
        forward, backward = dot(down, gelu), dot(up, grad_pre)

        @pl.when(step == 0)
        def _():
            branch[rows, :] = forward
            back[rows, :] = backward

        @pl.when(step > 0)
        def _():
            branch[rows, :] += forward
            back[rows, :] += backward

    up_grad = dot(act, grad_pre, 1, 1).astype(BF16)
    down_grad = dot(grad, gelu, 1, 1).astype(BF16)

    @pl.when(near)
    def _():
        uk_ref[...] = up_grad
        dk_ref[...] = down_grad

    @pl.when(jnp.logical_not(near))
    def _():
        us_ref[...] = up_grad
        ds_ref[...] = down_grad

    @pl.when(step == 2 * half_steps - 1)
    def _():
        bo_ref[...] = branch[:, :span]
        bt_ref[...] = branch[:, span:].astype(BF16)
        ho_ref[...] = back[:, :span]
        ht_ref[...] = back[:, span:].astype(BF16)


def feed(num, acts, grads, ups, downs):
    width, span = acts[0].shape
    feats = width // 2
    hidden = downs[0].shape[1]
    block = 256
    steps = hidden // block
    near = lambda s, n: (0, jnp.minimum(s, steps - 1))
    far = lambda s, n: (0, jnp.maximum(s - steps, 0))
    maps = (near, near, far, far)
    inputs = [whole(a) for a in (*acts, *grads)]
    inputs += [(w, (feats, block), where) for w, where in zip(ups, maps)]
    inputs += [(w, (feats, block), where) for w, where in zip(downs, maps)]
    tokens = [made((width, span), F32), made((width, span), BF16)]
    outputs = tokens + tokens
    outputs += [((width, hidden), BF16, (width, block), where) for where in (near, far)] * 2
    scratch = [pltpu.VMEM((width, 2 * span), BF16)] * 2 + [pltpu.VMEM((width, 2 * span), F32)] * 2
    return call(feed_kernel, "feed", num, inputs, outputs, (2 * steps,), scratch)


def turn_kernel(num, own, got, hidden, ga, gb, ta, tb, grad_ref, one_ref, sums_ref):
    feats = ga.shape[0]
    span = own.shape[1]
    grad = own[...] + got[...].astype(F32)
    values = hidden[...]
    mean, inv_std = norm_stats(values[:feats], values[feats:])
    normed = (values - mean) * inv_std
    cross = grad * normed
    sums_ref[:, 0:1] = jnp.sum(cross, axis=1, keepdims=True)
    sums_ref[:, 1:2] = jnp.sum(grad, axis=1, keepdims=True)
    scale = jnp.concatenate([column(ta, SCALE), column(tb, SCALE)], axis=0) + 1.0
    scaled = grad * scale
    mean_plain = jnp.mean(scaled, axis=0, keepdims=True)
    mean_cross = jnp.mean(scaled * normed, axis=0, keepdims=True)
    back = inv_std * (scaled - mean_plain - normed * mean_cross)
    for rows, grad_out in ((slice(0, feats), ga), (slice(feats, 2 * feats), gb)):
        total = back[rows] + grad_out[...].astype(F32)
        grad_ref[rows, :] = total
        one_ref[rows, :] = total.astype(BF16)


def turn(num, own, got, hidden, cots, tables):
    width, span = own.shape
    chip = lambda s, n: (0, n[CHIP])
    inputs = [whole(own), whole(got), whole(hidden)]
    inputs += [(cots[0], (width // 2, span), chip), whole(cots[1])]
    inputs += [whole(t) for t in tables]
    outputs = [made((width, span), F32), made((width, span), BF16), made((width, 128), F32)]
    return call(turn_kernel, "turn", num, inputs, outputs)


def leave_kernel(num, own, got, hidden, ga, gb, ta, tb, turned, oa_ref, ob_ref, sums_ref):
    feats = ga.shape[0]
    lane = lax.broadcasted_iota(jnp.int32, (feats, sums_ref.shape[1]), 1) - 3 * num[SLOT]
    for rows, grad_out, table, out_ref in (
        (slice(0, feats), ga, ta, oa_ref),
        (slice(feats, 2 * feats), gb, tb, ob_ref),
    ):
        branch = own[rows, :] + got[rows, :].astype(F32)
        out_ref[...] = (hidden[rows, :] + (1.0 + column(table, GATE)) * branch).astype(BF16)
        term = grad_out[...].astype(F32) * branch
        total = jnp.where(lane == 2, jnp.sum(term, axis=1, keepdims=True), 0.0)
        total = jnp.where(lane == 1, turned[rows, 1:2], total)
        sums_ref[rows, :] = jnp.where(lane == 0, turned[rows, 0:1], total)


def leave(num, own, got, hidden, cots, tables, turned, lanes):
    width, span = own.shape
    chip = lambda s, n: (0, n[CHIP])
    inputs = [whole(own), whole(got), whole(hidden)]
    inputs += [(cots[0], (width // 2, span), chip), whole(cots[1])]
    inputs += [whole(t) for t in (*tables, turned)]
    outputs = [made((width // 2, span), BF16)] * 2 + [made((width, lanes), F32)]
    return call(leave_kernel, "leave", num, inputs, outputs)


def unmix_kernel(num, one_own, one_other, *refs):
    count = (len(refs) - 8) // 2
    aa, ba, ab, bb, gk_ref, gs_ref, wn_ref, wf_ref = refs[2 * count :]
    feats = aa.shape[0]
    aligned = num[ALIGNED] == 1
    mine, theirs = sorted_heads(num, refs[:count], refs[count : 2 * count])
    heads = mine.shape[0]
    ones = jnp.concatenate([one_own[...], one_other[...]], axis=1)
    near = dot(aa[:, :heads], ones[:feats], 0, 0) + dot(ba[:, :heads], ones[feats:], 0, 0)
    far = dot(ab[:, :heads], ones[:feats], 0, 0) + dot(bb[:, :heads], ones[feats:], 0, 0)
    gk_ref[...] = jnp.where(aligned, near, far).astype(BF16)
    gs_ref[...] = jnp.where(aligned, far, near).astype(BF16)
    wn_ref[...] = dot(ones, mine, 1, 1).astype(BF16)
    wf_ref[...] = dot(ones, theirs, 1, 1).astype(BF16)


def unmix(num, ones, kept, got, blocks):
    feats = blocks[0].shape[0]
    heads, tokens = sum(k.shape[0] for k in kept), kept[0].shape[1]
    last = lambda s, n: (0, 3)
    inputs = [whole(a) for a in (*ones, *kept, *got)]
    inputs += [(b, (feats, 256), last) for b in blocks]
    outputs = [made((heads, tokens), BF16)] * 2 + [made((2 * feats, heads), BF16)] * 2
    return call(unmix_kernel, "unmix", num, inputs, outputs)


def unproject_kernel(num, *refs):
    wa, wb, keep_ref, send_ref = refs[-4:]
    step = pl.program_id(0)
    feats = wa.shape[0]
    grad = jnp.concatenate([g[...] for g in refs[:-4]], axis=0)
    first, second = dot(wa[...], grad), dot(wb[...], grad)
    own = step // 2 == num[CORE]

    @pl.when(own)
    def _():
        keep_ref[:feats, :] = first
        keep_ref[feats:, :] = second

    @pl.when(jnp.logical_not(own))
    def _():
        send_ref[:feats, :] = first.astype(BF16)
        send_ref[feats:, :] = second.astype(BF16)


def unproject(num, grads, weights):
    rows, length = grads[0].shape
    feats = weights[0].shape[0]
    block = length // 4
    here = lambda s, n: (0, s)
    own = lambda s, n: (0, core_blocks(s, n)[0])
    other = lambda s, n: (0, core_blocks(s, n)[1])
    inputs = [(g, (rows, block), here) for g in grads] + [whole(w) for w in weights]
    shape = (2 * feats, length // 2)
    outputs = [(shape, F32, (2 * feats, block), own), (shape, BF16, (2 * feats, block), other)]
    return call(unproject_kernel, "unproject", num, inputs, outputs, (4,))


def weigh_kernel(num, *refs):
    act, wa, wb, ta, tb, ga_ref, gb_ref, first_ref, sums_ref, total, plain = refs[-11:]
    step = pl.program_id(0)
    feats = wa.shape[0]
    grad = jnp.concatenate([g[...] for g in refs[:-11]], axis=0)
    product = dot(act[...], grad, 1, 1)
    row = dot(jnp.ones((8, grad.shape[1]), BF16), grad, 1, 1)

    @pl.when(step == 0)
    def _():
        total[...] = product
        plain[...] = row

    @pl.when(step > 0)
    def _():
        total[...] += product
        plain[...] += row

    @pl.when(step == pl.num_programs(0) - 1)
    def _():
        for rows, weight, table, out_ref in (
            (slice(0, feats), wa, ta, ga_ref),
            (slice(feats, 2 * feats), wb, tb, gb_ref),
        ):
            grad_weight = total[rows, :]
            out_ref[...] = grad_weight.astype(BF16)
            low = weight[...].astype(F32)
            gain, bias = column(table, GAIN), column(table, BIAS)
            weighed = jnp.sum(low * grad_weight, axis=1, keepdims=True)
            shifted = jnp.sum(low * plain[0:1, :], axis=1, keepdims=True)
            for row, value in ((0, (weighed - bias * shifted) / gain), (1, shifted)):
                sums_ref[row : row + 1, rows] = jnp.broadcast_to(value, (feats, 128)).T[:1]
        first_ref[...] = jnp.where(num[ALIGNED] == 1, gb_ref[...], ga_ref[...])


def weigh(num, grads, act, weights, tables):
    rows, length = grads[0].shape
    width = act.shape[0]
    feats, columns = weights[0].shape
    block = length // 4
    here = lambda s, n: (0, s)
    inputs = [(g, (rows, block), here) for g in grads] + [(act, (width, block), here)]
    inputs += [whole(w) for w in weights] + [whole(t) for t in tables]
    outputs = [made((feats, columns), BF16)] * 3 + [made((8, width), F32)]
    scratch = [pltpu.VMEM((width, columns), F32), pltpu.VMEM((8, columns), F32)]
    return call(weigh_kernel, "weigh", num, inputs, outputs, (4,), scratch)


def finish_kernel(num, own, got, xa, xb, hidden, ta, tb, oa_ref, ob_ref):
    feats = xa.shape[0]
    grad = own[...] + got[...].astype(F32)
    first, second = xa[...].astype(F32), xb[...].astype(F32)
    mean, inv_std = norm_stats(first, second)
    first, second = (first - mean) * inv_std, (second - mean) * inv_std
    grad_a, grad_b = grad[:feats] * column(ta, GAIN), grad[feats:] * column(tb, GAIN)
    count = 2 * feats
    plain = jnp.sum(grad_a, axis=0, keepdims=True) + jnp.sum(grad_b, axis=0, keepdims=True)
    cross = jnp.sum(grad_a * first, axis=0, keepdims=True)
    cross = cross + jnp.sum(grad_b * second, axis=0, keepdims=True)
    plain, cross = plain / count, cross / count
    oa_ref[...] = hidden[:feats, :] + inv_std * (grad_a - plain - first * cross)
    ob_ref[...] = (hidden[feats:, :] + inv_std * (grad_b - plain - second * cross)).astype(BF16)


def finish(num, own, got, pieces, hidden, tables):
    width, span = own.shape
    chip = lambda s, n: (0, n[CHIP])
    inputs = [whole(own), whole(got)] + [(p, (width // 2, span), chip) for p in pieces]
    inputs += [whole(hidden)] + [whole(t) for t in tables]
    outputs = [made((width // 2, span), F32), made((width // 2, span), BF16)]
    return call(finish_kernel, "finish", num, inputs, outputs)


def swap_rows(value):
    count = lax.axis_size("row")
    return lax.ppermute(value, "row", [(i, i ^ 1) for i in range(count)])


def swap_cores(value):
    count = lax.axis_size("col")
    return lax.ppermute(value, "col", [(i, i ^ 1) for i in range(count)])


def swap_cols(value):
    return lax.ppermute(value, "col", [(i, i ^ 2) for i in range(lax.axis_size("col"))])


def swap_dp(value, bit):
    count = lax.axis_size("dp")
    return lax.ppermute(value, "dp", [(i, i ^ bit) for i in range(count)])


def in_order(flag, own, other):
    first = jnp.where(flag == 0, own, other)
    second = jnp.where(flag == 0, other, own)
    return first, second


def cut(value, start, size, axis):
    return lax.dynamic_slice_in_dim(value, start, size, axis)


def after(value, *others):
    return lax.optimization_barrier((value, *others))[0]


def tie(*values):
    return lax.optimization_barrier(values)


def plus(left, right):
    return (left.astype(F32) + right.astype(F32)).astype(BF16)


def dp_first(value):
    half = value.shape[0] // 2
    low = lax.axis_index("dp") & 1
    return plus(cut(value, low * half, half, 0), swap_dp(cut(value, (1 - low) * half, half, 0), 1))


def dp_second(total, gate=None):
    reach = 2
    while reach < lax.axis_size("dp"):
        got = swap_dp(total, reach)
        if gate is not None:
            total, gate = tie(total, gate)
        total = plus(total, got)
        reach *= 2
    return total, gate


def dp_third(total):
    low = lax.axis_index("dp") & 1
    return jnp.concatenate(in_order(low, total, swap_dp(total, 1)), axis=0)


class PairMoves:
    def __init__(self, r, c, feats, heads):
        self.r, self.j, self.h, self.k, self.feats, self.heads = r, r, c // 2, c % 2, feats, heads
        self.aligned = self.j == self.h

    def pieces(self, value):
        other = swap_rows(value)
        return value, other, swap_cores(value), swap_cores(other)

    def tables(self, mods, gain, bias, seq):
        table = jnp.concatenate([gain[None], bias[None], mods[seq]], axis=0)
        table = jnp.pad(table, ((0, 3), (0, 0)))
        return table, swap_rows(table)

    def cotangents(self, value):
        span = value.shape[1] // 2
        return value, swap_rows(cut(value, (1 - self.j) * span, span, 1))

    def flip(self, value):
        return jnp.concatenate([value[self.feats :], value[: self.feats]], axis=0)

    def qkv(self, weight):
        other = swap_cols(weight)
        mine = jnp.where(self.aligned, weight, other)
        theirs = jnp.where(self.aligned, other, weight)
        self.gate_col = other
        return mine, swap_rows(theirs)

    def feed(self, weight, gate):
        return weight, swap_rows(after(weight, gate)), swap_cols(after(weight, self.gate_col)), None

    def corner(self, blocks, gate):
        return *blocks[:3], swap_cols(after(blocks[1], gate))

    first, second, third = map(staticmethod, (dp_first, dp_second, dp_third))

    def across(self, near, got):
        part = plus(near, got)
        return part[: self.feats], swap_rows(part[self.feats :])

    def down_columns(self, near, far):
        return near, swap_cols(far)

    def extras(self, out_near, out_far, sums):
        sums = (sums + swap_cores(sums)).astype(BF16)[:, : 256 - self.heads]
        both = jnp.concatenate([out_near, sums, out_far, sums], axis=1)
        return both[: self.feats], swap_rows(both[self.feats :])

    def extras_last(self, mine, got):
        both = plus(mine, got)
        return both[:, :256], swap_cols(both[:, 256:])

    def join(self, up, mine, got):
        return jnp.concatenate([up, plus(mine, got)], axis=1)

    def unpack(self, total, count):
        hidden = total.shape[1] - 256
        ends = hidden + self.heads
        total = total.astype(F32)
        return total[:, :hidden], total[:, hidden:ends].T, total[:, ends : ends + count]

    def reduce_qkv(self, part_a, part_b, first):
        cycle, corner = [], []
        for core in range(2):
            for row in range(2):
                aligned, beside = row * 4 + 2 * row + core, row * 4 + 2 * (1 - row) + core
                cycle.append((aligned, (1 - row) * 4 + 2 * row + core))
                cycle.append((beside, aligned))
                corner.append((beside, (1 - row) * 4 + 2 * row + core))
        axes = ("row", "col")
        first = lax.ppermute(first, axes, cycle)
        second = lax.ppermute(part_b, axes, corner)
        return first, second, part_a

    def qkv_sum(self, first, second, part_a):
        return plus(first, jnp.where(self.aligned, part_a, second))

    def outputs(self, own, other):
        return jnp.concatenate(in_order(self.j, own, swap_rows(other)), axis=1)

    def own_sums(self, sums):
        total = sums + swap_cores(sums)
        return total + swap_cols(total)

    def row_sums(self, sums):
        return sums[:, : self.feats] + swap_rows(sums[:, self.feats :])

    def board(self, grad, sums):
        room = ((0, 32 - sums.shape[0]), (0, grad.shape[1] - sums.shape[1]))
        return jnp.concatenate([grad, jnp.pad(sums.astype(BF16), room)], axis=0)

    def leave_board(self, both, count):
        return both[: self.feats], both[self.feats : self.feats + count, : self.feats]


class AnyMoves:
    def __init__(self, r, c, feats, heads, pairs):
        self.heads = heads
        self.r, self.j, self.q, self.h, self.k = r, r % 2, r // 2, c // 2, c % 2
        self.feats, self.pairs = feats, pairs
        self.half = feats * lax.axis_size("row") // 2
        self.aligned = self.j == 0
        cols = lax.axis_size("col")
        self.cores = [[i, i + 1] for i in range(0, cols, 2)]
        self.likes = [list(range(core, cols, 2)) for core in range(2)]

    def halves(self, value):
        return value[: self.half], value[self.half :]

    def sequence(self, value):
        full = lax.all_gather(value, "row", axis=0, tiled=True)
        full = lax.all_gather(full, "col", axis=1, tiled=True, axis_index_groups=self.cores)
        return cut(full, self.q * LENGTH, LENGTH, 1)

    def pieces(self, value):
        full = self.sequence(value)
        own = cut(full, self.k * LENGTH // 2, LENGTH // 2, 1)
        other = cut(full, (1 - self.k) * LENGTH // 2, LENGTH // 2, 1)
        return *self.halves(own), *self.halves(other)

    def tables(self, mods, gain, bias, seq):
        count = mods.shape[0]
        table = jnp.concatenate([mods.reshape(3 * count, -1), gain[None], bias[None]], axis=0)
        table = lax.all_gather(table, "row", axis=1, tiled=True)
        table = jnp.concatenate([table[3 * count :], cut(table, 3 * seq, 3, 0)], axis=0)
        table = jnp.pad(table, ((0, 3), (0, 0)))
        return table[:, : self.half], table[:, self.half :]

    def cotangents(self, value):
        span = LENGTH // 4
        own = cut(self.sequence(value), (2 * self.k + self.j) * span, span, 1)
        first, second = self.halves(own)
        return jnp.concatenate([first, first], axis=1), second

    def flip(self, value):
        return value

    def likes_gather(self, value):
        rows = lax.all_gather(value, "row", axis=0, tiled=True)
        return lax.all_gather(rows, "col", axis=0, axis_index_groups=self.likes)

    def qkv(self, weight):
        return self.halves(cut(self.likes_gather(weight), self.j, 1, 0)[0])

    def feed(self, weight, gate):
        near, far = self.likes_gather(weight)
        return *self.halves(near), *self.halves(far)

    def corner(self, blocks, gate):
        return blocks

    def scatter(self, grad):
        grad = lax.psum_scatter(grad, "row", scatter_dimension=0, tiled=True)
        grad = lax.psum_scatter(
            grad, "col", scatter_dimension=1, tiled=True, axis_index_groups=self.likes
        )
        return lax.psum(grad, "dp").astype(F32)

    def first(self, value):
        return value

    third = first

    def second(self, value, gate=None):
        return value, gate

    def down_columns(self, near, far):
        return near, far

    def across(self, near, far):
        grad = self.scatter(jnp.concatenate([near, far], axis=1))
        return grad, jnp.zeros_like(grad)

    def extras(self, out_near, out_far, sums):
        return jnp.concatenate([out_near, out_far], axis=1), sums

    def extras_last(self, both, sums):
        return self.scatter(both), self.own_sums(sums.T).T

    def join(self, up, out, sums):
        return up, out, sums

    def row_sums(self, sums):
        return sums

    def board(self, grad, sums):
        return grad, sums

    def leave_board(self, both, count):
        return both

    def unpack(self, total, count):
        up, out, sums = total
        return up.astype(F32), out.T, sums[:, :count]

    def reduce_qkv(self, part_a, part_b, first):
        grad = jnp.concatenate([part_a, part_b], axis=0)
        both = in_order(self.j, grad, jnp.zeros_like(grad))
        total = self.scatter(jnp.concatenate(both, axis=1))
        return total, total, total

    def qkv_sum(self, first, second, part_a):
        return first

    def outputs(self, own, other):
        value = jnp.concatenate([own.astype(BF16), other], axis=0)
        parts = value.reshape(lax.axis_size("row"), self.feats, -1)
        parts = lax.all_to_all(parts, "row", split_axis=0, concat_axis=0, tiled=True)
        parts = lax.all_gather(parts, "col", axis=0, axis_index_groups=self.cores)
        span = parts.shape[-1]
        parts = parts.reshape(2, self.pairs, 2, self.feats, span).transpose(3, 1, 0, 2, 4)
        parts = parts.reshape(self.feats, -1)
        width = parts.shape[1] // 2
        return cut(parts, self.k * width, width, 1)

    def own_sums(self, sums):
        total = lax.psum(sums, ("dp", "row", "col"))
        return cut(total, self.r * self.feats, self.feats, 1)


def local(
    tokens, ln_gain, ln_bias, qkv_weight, out_weight, up_weight, down_weight,
    mod_weight, timestep, block_size, cotangent,
):
    rows, cols = lax.axis_size("row"), lax.axis_size("col")
    r, c, z = lax.axis_index("row"), lax.axis_index("col"), lax.axis_index("dp")
    width = mod_weight.shape[2]
    feats, local_tokens = tokens.shape
    pairs = 2 * local_tokens // LENGTH
    assert rows == 2 * pairs and cols == 4 and LENGTH % (8 * CHUNK) == 0
    sequences = timestep.shape[0]
    seq = (z * (cols // 2) + c // 2) * pairs + r // 2
    heads = out_weight.shape[0]
    moves = PairMoves(r, c, feats, heads) if pairs == 1 else AnyMoves(r, c, feats, heads, pairs)
    block_len = cut(block_size, seq, 1, 0)[0]
    num = jnp.stack([moves.k, moves.j, moves.aligned.astype(jnp.int32), block_len, seq])

    embedded = time_embed(timestep, width)
    mods = jnp.einsum("nd,ked->nke", embedded, mod_weight.astype(F32), precision=HIGH)
    cosine, sine = rope_tables(LENGTH, HEAD_DIM)

    pieces = moves.pieces(tokens)
    tables = moves.tables(mods, ln_gain, ln_bias, seq)
    qkv = moves.qkv(qkv_weight.reshape(feats, -1))
    packed = jnp.pad(jnp.concatenate([up_weight, out_weight.T], axis=1), ((0, 0), (0, 256 - heads)))
    gate = after(qkv[1], pieces[1], tables)
    ups = moves.feed(packed, gate)
    downs = moves.feed(down_weight, gate)

    up_col, *pieces = tie(ups[2], *pieces)
    ups = (*ups[:2], up_col, ups[3])
    queries, keys, values, act_one = project(num, pieces, qkv, tables, cosine, sine)
    cots = moves.cotangents(after(cotangent, queries))
    count = heads // HEAD_DIM
    down_col, queries = tie(downs[2], queries)
    early, early_sent, early_lse = attend_forward(num, 0, 1, queries, keys, values)
    early_got = swap_rows(early_sent)
    up_row, down_row, rest, early = tie(ups[1], downs[1], queries, early)
    ups = moves.corner((ups[0], up_row, *ups[2:]), early)
    downs = moves.corner((downs[0], down_row, down_col, downs[3]), early)
    late, late_sent, late_lse = attend_forward(num, 1, count - 1, rest, keys, values)
    got = (early_got, swap_rows(late_sent))
    early, late, ups, downs, cots = tie(early, late, ups, downs, cots)
    kept = (early, late)
    lse = jnp.concatenate([early_lse, late_lse], axis=0)

    span = cots[1].shape[1]
    own, other = mix(num, kept, got, ups)
    own, cots = tie(own, cots)
    gate_a, gate_b = tables[0][4][:, None], tables[1][4][:, None]
    cot_a = cut(cots[0], moves.j * span, span, 1).astype(F32)
    grad_a = cot_a * (1.0 + gate_a)
    grad_b = cots[1].astype(F32) * (1.0 + gate_b)
    grad_two = jnp.concatenate([grad_a, grad_b], axis=0).astype(BF16)
    grads = (grad_two, swap_cores(grad_two))
    hidden, act = enter(num, own, swap_cores(other), pieces[:2], tables)
    fed = feed(num, (act, swap_cores(act)), grads, ups, downs)
    branch_own, branch_other, back_own, back_other, up_near, up_far, down_near, down_far = fed
    back_got = swap_cores(back_other)
    grad_hidden, ones, turn_sums = turn(num, back_own, back_got, hidden, cots, tables)
    down_part = moves.down_columns(down_near, down_far)
    up_part = moves.down_columns(up_near, up_far)
    branch_got = swap_cores(branch_other)
    both_ones = (ones, swap_cores(ones))
    grad_kept, grad_sent, out_near, out_far = unmix(num, both_ones, kept, got, ups)
    grad_got = swap_rows(grad_sent)
    branch_own = after(branch_own, grad_sent)
    result_a, result_b, leave_sums = leave(
        num, branch_own, branch_got, hidden, cots, tables, turn_sums, -(-3 * sequences // 128) * 128
    )
    result = moves.outputs(result_a, result_b)
    down_part = moves.across(*after(down_part, result_a))
    extra = moves.extras(out_near, out_far, leave_sums)

    grad_kept, down_keep, extra_keep = tie(grad_kept, down_part[0], extra[0])
    grads = attend_backward(num, queries, keys, values, grad_kept, grad_got, lse, cosine, sine)
    down_part, extra = (down_keep, down_part[1]), (extra_keep, extra[1])
    up_part, down_part, extra, grads, result = tie(up_part, down_part, extra, grads, result)
    down_sum = moves.first(plus(*down_part))
    up_keep, up_got = moves.across(*up_part)
    extra_keep, extra_got = moves.extras_last(*extra)
    grads, up_keep, extra_keep = tie(grads, up_keep, extra_keep)
    keep, send = unproject(num, grads, qkv)
    send_got = swap_cores(send)
    up_sum = moves.join(plus(up_keep, up_got), extra_keep, extra_got)
    grads, keep, down_sum, up_sum = tie(grads, keep, down_sum, up_sum)
    qkv_a, qkv_b, qkv_first, norm_sums = weigh(num, grads, act_one, qkv, tables)
    norm_sums = moves.row_sums(norm_sums[:2])
    down_sum, _ = moves.second(down_sum)
    up_sum = moves.first(up_sum)
    send_got, norm_sums = tie(send_got, norm_sums)
    kept_core = keep + send_got.astype(F32)
    crossing = cut(kept_core, (1 - moves.j) * span, span, 1).astype(BF16)
    crossing = moves.flip(crossing)
    own = cut(kept_core, moves.j * span, span, 1)
    crossing, norm_sums, qkv_a, qkv_b, qkv_first = tie(crossing, norm_sums, qkv_a, qkv_b, qkv_first)
    qkv_part = moves.reduce_qkv(qkv_a, qkv_b, qkv_first)
    crossed = swap_rows(crossing)
    norm_sums = moves.own_sums(norm_sums)
    qkv_sum = moves.first(moves.board(moves.qkv_sum(*qkv_part), norm_sums))
    crossed, down_grad = tie(crossed, moves.third(down_sum))
    tokens_a, tokens_b = finish(num, own, crossed, pieces[:2], grad_hidden, tables)
    up_sum, tokens_b = moves.second(up_sum, tokens_b)
    qkv_sum, tokens_b = moves.second(qkv_sum, tokens_b)
    tokens_grad = moves.outputs(tokens_a, tokens_b)
    down_grad = down_grad.astype(F32)
    up_grad, out_grad, totals = moves.unpack(moves.third(up_sum), 3 * sequences)
    totals = totals.reshape(feats, sequences, 3)
    mod_grad = jnp.einsum("nd,enk->ked", embedded, totals, precision=HIGH)
    qkv_grad, norm_sums = moves.leave_board(moves.third(qkv_sum), 2)
    qkv_grad = qkv_grad.astype(F32)

    return (
        result,
        tokens_grad.astype(F32),
        norm_sums[0].astype(F32),
        norm_sums[1].astype(F32),
        qkv_grad.reshape(qkv_weight.shape),
        out_grad,
        up_grad,
        down_grad,
        mod_grad,
    )


def solution(mesh):
    placed = (
        P("row", ("dp", "col")),
        P("row"),
        P("row"),
        P("row", None, "col"),
        P("col", "row"),
        P("row", "col"),
        P("row", "col"),
        P(None, "row", None),
        P(),
        P(),
        P("row", ("dp", "col")),
    )
    return jax.shard_map(
        local,
        mesh=mesh,
        in_specs=placed,
        out_specs=(
            P("row", ("dp", "col")),
            P("row", ("dp", "col")),
            P("row"),
            P("row"),
            P("row", None, "col"),
            P("col", "row"),
            P("row", "col"),
            P("row", "col"),
            P(None, "row", None),
        ),
        check_vma=False,
    )
```

```python
from functools import partial
import math

import jax
import jax.numpy as jnp
from jax import lax
from jax.experimental import pallas as pl
from jax.experimental.pallas import tpu as pltpu
from jax.sharding import PartitionSpec as P

HEAD_DIM = 64
LENGTH = 2048
CHUNK = 256
EPSILON = 1e-05
HIGH = lax.Precision.HIGHEST
F32 = jnp.float32
BF16 = jnp.bfloat16
SCALE_T = 0.03
MICROS = dict(project=9, attend_forward=26, mix=5, enter=5, feed=32, turn=6, leave=5, unmix=5, attend_backward=33,
              unproject=30, weigh=30, finish=5)
FULL = ("weigh", "unproject", "finish")
FLOPS = {k: int(v * (1.0 if k in FULL else SCALE_T) * 1_153_000_000) for k, v in MICROS.items()}
GAIN, BIAS, SCALE, SHIFT, GATE = range(5)
CORE, CHIP, ALIGNED, BLOCK, SLOT = range(5)


def time_embed(steps_in, width_all):
    half_width = width_all // 2
    frequency = jnp.exp(-math.log(10000.0) * jnp.arange(half_width, dtype=F32) / half_width)
    angles = steps_in.astype(F32)[:, None] * frequency[None, :]
    return jnp.concatenate([jnp.sin(angles), jnp.cos(angles)], axis=1)


def rope_tables(length, head_width):
    half_dim = head_width // 2
    frequency = jnp.exp(-math.log(10000.0) * jnp.arange(half_dim, dtype=F32) / half_dim)
    angles = frequency[:, None] * jnp.arange(length, dtype=F32)[None, :]
    return jnp.cos(angles), jnp.sin(angles)


def dot(left, right, left_dim=1, right_dim=0):
    dims = (((left_dim,), (right_dim,)), ((), ()))
    return lax.dot_general(left, right, dims, preferred_element_type=F32)


def call(kernel, name, numbers, inputs, outputs, grid=(1,), scratch=()):
    def spec(shape, block, index):
        if block is None:
            return pl.BlockSpec(shape, lambda *_: (0,) * len(shape))
        return pl.BlockSpec(block, index)

    return pl.pallas_call(
        kernel,
        grid_spec=pltpu.PrefetchScalarGridSpec(
            num_scalar_prefetch=1,
            grid=grid,
            in_specs=[spec(a.shape, block, index) for a, block, index in inputs],
            out_specs=[spec(shape, block, index) for shape, _, block, index in outputs],
            scratch_shapes=list(scratch),
        ),
        out_shape=[jax.ShapeDtypeStruct(shape, dtype) for shape, dtype, _, _ in outputs],
        compiler_params=pltpu.CompilerParams(vmem_limit_bytes=58 * 1024 * 1024),
        cost_estimate=pl.CostEstimate(flops=FLOPS[name], transcendentals=0, bytes_accessed=0),
        name=name,
    )(numbers, *[a for a, _, _ in inputs])


def whole(array):
    return array, None, None


def made(shape, dtype):
    return shape, dtype, None, None


def column(table, row):
    return table[...].T[:, row : row + 1]


def norm_stats(first, second):
    count = first.shape[0] + second.shape[0]
    total = jnp.sum(first, axis=0, keepdims=True) + jnp.sum(second, axis=0, keepdims=True)
    square = jnp.sum(first * first, axis=0, keepdims=True)
    square = square + jnp.sum(second * second, axis=0, keepdims=True)
    mean = total / count
    return mean, lax.rsqrt(square / count - mean * mean + EPSILON)


def project_kernel(
    num, xa, xb, ca, cb, wa, wb, ta, tb, cos_ref, sin_ref, q_ref, k_ref, v_ref, act_ref, weight
):
    step = pl.program_id(0)
    feats = xa.shape[0]

    @pl.when(step == 0)
    def _():
        weight[:, :feats] = wa[...].T
        weight[:, feats:] = wb[...].T

    own = step // 2 == num[CORE]
    first = jnp.where(own, xa[...], ca[...]).astype(F32)
    second = jnp.where(own, xb[...], cb[...]).astype(F32)
    mean, inv_std = norm_stats(first, second)
    first = (first - mean) * inv_std * column(ta, GAIN) + column(ta, BIAS)
    second = (second - mean) * inv_std * column(tb, GAIN) + column(tb, BIAS)
    act_ref[:feats, :] = first.astype(BF16)
    act_ref[feats:, :] = second.astype(BF16)
    projected = dot(weight[...], act_ref[...])
    rows = q_ref.shape[0]
    half = HEAD_DIM // 2
    cosine, sine = cos_ref[...], sin_ref[...]
    for out_ref, base in ((q_ref, 0), (k_ref, rows)):
        for head in range(0, rows, HEAD_DIM):
            front = projected[base + head : base + head + half]
            back = projected[base + head + half : base + head + HEAD_DIM]
            out_ref[head : head + half, :] = (front * cosine - back * sine).astype(BF16)
            out_ref[head + half : head + HEAD_DIM, :] = (back * cosine + front * sine).astype(BF16)
    v_ref[...] = projected[2 * rows :].astype(BF16)


def core_blocks(step, num):
    early = jnp.minimum(step, 1)
    late = jnp.maximum(step - 2, 0)
    flag = num[CORE] == 0
    return jnp.where(flag, early, late), jnp.where(flag, late, early)


def project(num, pieces, weights, tables, cosine, sine):
    feats, tokens = pieces[0].shape
    block = tokens // 2
    columns = weights[0].shape[1]
    rows = columns // 3
    own = lambda s, n: (0, core_blocks(s, n)[0])
    other = lambda s, n: (0, core_blocks(s, n)[1])
    here = lambda s, n: (0, s)
    maps = (own, own, other, other)
    inputs = [(piece, (feats, block), where) for piece, where in zip(pieces, maps)]
    inputs += [whole(w) for w in weights] + [whole(t) for t in tables]
    inputs += [(t, (t.shape[0], block), here) for t in (cosine, sine)]
    outputs = [((rows, 2 * tokens), BF16, (rows, block), here)] * 3
    outputs += [((2 * feats, 2 * tokens), BF16, (2 * feats, block), here)]
    scratch = [pltpu.VMEM((columns, 2 * feats), BF16)]
    return call(project_kernel, "project", num, inputs, outputs, (4,), scratch)


def diagonal_mask(num):
    key_block = lax.broadcasted_iota(jnp.int32, (CHUNK, CHUNK), 0) // num[BLOCK]
    query_block = lax.broadcasted_iota(jnp.int32, (CHUNK, CHUNK), 1) // num[BLOCK]
    return key_block <= query_block


def attend_forward_kernel(num, q_ref, k_ref, v_ref, keep_ref, send_ref, lse_ref, keys):
    keys[...] = k_ref[...].T
    visible = diagonal_mask(num)
    for step in range(q_ref.shape[1] // CHUNK):
        here = slice(step * CHUNK, (step + 1) * CHUNK)
        past = slice(0, step * CHUNK)
        query = q_ref[:, here] * BF16(0.125)
        diag = jnp.where(visible, dot(keys[here, :], query), -1e30)
        top = jnp.max(diag, axis=0, keepdims=True)
        if step:
            scores = dot(keys[past, :], query)
            top = jnp.maximum(top, jnp.max(scores, axis=0, keepdims=True))
        weight = jnp.exp(diag - top)
        total = jnp.sum(weight, axis=0, keepdims=True)
        mixed = dot(v_ref[:, here], weight.astype(BF16))
        if step:
            weight = jnp.exp(scores - top)
            total = total + jnp.sum(weight, axis=0, keepdims=True)
            mixed = mixed + dot(v_ref[:, past], weight.astype(BF16))
        mixed = (mixed / total).astype(BF16)
        lse_ref[0, :, here] = top + jnp.log(total)
        core, chip, part = step // 4, step // 2 % 2, step % 2
        slot = jnp.where(num[CORE] == core, 0, 2) + part
        place = pl.ds(pl.multiple_of(slot * CHUNK, CHUNK), CHUNK)

        @pl.when(num[CHIP] == chip)
        def _():
            keep_ref[:, place] = mixed

        @pl.when(num[CHIP] != chip)
        def _():
            send_ref[:, place] = mixed


def attend_forward(num, first, count, queries, keys, values):
    length = queries.shape[1]
    rows = count * HEAD_DIM
    there = lambda h, n: (first + h, 0)
    here = lambda h, n: (h, 0)
    inputs = [(a, (HEAD_DIM, length), there) for a in (queries, keys, values)]
    outputs = [((rows, length // 2), BF16, (HEAD_DIM, length // 2), here)] * 2
    outputs += [((count, 1, length), F32, (1, 1, length), lambda h, n: (h, 0, 0))]
    scratch = [pltpu.VMEM((length, HEAD_DIM), BF16)]
    return call(attend_forward_kernel, "attend_forward", num, inputs, outputs, (count,), scratch)


def attend_backward_kernel(
    num, q_ref, k_ref, v_ref, keep_ref, got_ref, lse_ref, cos_ref, sin_ref,
    dq_ref, dk_ref, dv_ref, g_ref, keys, values, queries, grads, key_sum, value_sum,
):
    length = q_ref.shape[1]
    half = HEAD_DIM // 2
    span = length // 4
    for place in range(4):
        core, chip = place // 2, place % 2
        slot = jnp.where(num[CORE] == core, 0, 1)
        there = pl.ds(pl.multiple_of(slot * span, span), span)
        part = jnp.where(num[CHIP] == chip, keep_ref[:, there], got_ref[:, there])
        g_ref[:, place * span : (place + 1) * span] = part
    keys[...] = k_ref[...].T
    values[...] = v_ref[...].T
    queries[...] = (q_ref[...] * BF16(0.125)).T
    grads[...] = g_ref[...].T
    visible = diagonal_mask(num)

    def store_unrotated(out_ref, grad, where):
        front, back = grad[:half], grad[half:]
        cosine, sine = cos_ref[:, where], sin_ref[:, where]
        out_ref[:half, where] = (front * cosine + back * sine).astype(BF16)
        out_ref[half:, where] = (back * cosine - front * sine).astype(BF16)

    for step in range(length // CHUNK):
        here = slice(step * CHUNK, (step + 1) * CHUNK)
        past = slice(0, step * CHUNK)
        query = q_ref[:, here] * BF16(0.125)
        grad = g_ref[:, here]
        lse = lse_ref[0, :, here]
        diag = jnp.where(visible, dot(keys[here, :], query), -1e30)
        weight = jnp.exp(diag - lse)
        grad_weight = dot(values[here, :], grad)
        delta = jnp.sum(weight * grad_weight, axis=0, keepdims=True)
        if step:
            weight_past = jnp.exp(dot(keys[past, :], query) - lse)
            grad_past = dot(values[past, :], grad)
            delta = delta + jnp.sum(weight_past * grad_past, axis=0, keepdims=True)
        grad_score = (weight * (grad_weight - delta)).astype(BF16)
        grad_query = dot(k_ref[:, here], grad_score)
        value_sum[here, :] = dot(weight.astype(BF16), grads[here, :])
        key_sum[here, :] = dot(grad_score, queries[here, :])
        if step:
            grad_score = (weight_past * (grad_past - delta)).astype(BF16)
            grad_query = grad_query + dot(k_ref[:, past], grad_score)
            value_sum[past, :] += dot(weight_past.astype(BF16), grads[here, :])
            key_sum[past, :] += dot(grad_score, queries[here, :])
        store_unrotated(dq_ref, grad_query * 0.125, here)
    store_unrotated(dk_ref, key_sum[...].T, slice(0, length))
    dv_ref[...] = value_sum[...].T.astype(BF16)


def attend_backward(num, queries, keys, values, kept, got, lse, cosine, sine):
    rows, length = queries.shape
    heads = rows // HEAD_DIM
    here = lambda h, n: (h, 0)
    inputs = [(a, (HEAD_DIM, length), here) for a in (queries, keys, values)]
    inputs += [(a, (HEAD_DIM, length // 2), here) for a in (kept, got)]
    inputs += [(lse, (1, 1, length), lambda h, n: (h, 0, 0)), whole(cosine), whole(sine)]
    outputs = [((rows, length), BF16, (HEAD_DIM, length), here)] * 3
    scratch = [pltpu.VMEM((HEAD_DIM, length), BF16)] + [pltpu.VMEM((length, HEAD_DIM), BF16)] * 4
    scratch += [pltpu.VMEM((length, HEAD_DIM), F32)] * 2
    return call(attend_backward_kernel, "attend_backward", num, inputs, outputs, (heads,), scratch)


def sorted_heads(num, kept, got):
    aligned = num[ALIGNED] == 1
    kept = jnp.concatenate([k[...] for k in kept], axis=0)
    got = jnp.concatenate([g[...] for g in got], axis=0)
    return jnp.where(aligned, kept, got), jnp.where(aligned, got, kept)


def mix_kernel(num, *refs):
    count = (len(refs) - 6) // 2
    aa, ba, ab, bb, own_ref, other_ref = refs[2 * count :]
    feats = aa.shape[0]
    mine, theirs = sorted_heads(num, refs[:count], refs[count : 2 * count])
    heads = mine.shape[0]
    span = own_ref.shape[1]
    for rows, near, far in ((slice(0, feats), aa, ab), (slice(feats, 2 * feats), ba, bb)):
        total = dot(near[:, :heads], mine) + dot(far[:, :heads], theirs)
        own_ref[rows, :] = total[:, :span]
        other_ref[rows, :] = total[:, span:].astype(BF16)


def mix(num, kept, got, blocks):
    feats = blocks[0].shape[0]
    span = kept[0].shape[1] // 2
    last = lambda s, n: (0, 3)
    inputs = [whole(a) for a in (*kept, *got)] + [(b, (feats, 256), last) for b in blocks]
    outputs = [made((2 * feats, span), F32), made((2 * feats, span), BF16)]
    return call(mix_kernel, "mix", num, inputs, outputs)


def enter_kernel(num, own, got, xa, xb, ta, tb, hidden_ref, act_ref):
    feats = xa.shape[0]
    total = own[...] + got[...].astype(F32)
    first = total[:feats] + xa[...].astype(F32)
    second = total[feats:] + xb[...].astype(F32)
    hidden_ref[:feats, :] = first
    hidden_ref[feats:, :] = second
    mean, inv_std = norm_stats(first, second)
    first = (first - mean) * inv_std * (1.0 + column(ta, SCALE)) + column(ta, SHIFT)
    second = (second - mean) * inv_std * (1.0 + column(tb, SCALE)) + column(tb, SHIFT)
    act_ref[:feats, :] = first.astype(BF16)
    act_ref[feats:, :] = second.astype(BF16)


def enter(num, own, got, pieces, tables):
    width, span = own.shape
    chip = lambda s, n: (0, n[CHIP])
    inputs = [whole(own), whole(got)] + [(p, (width // 2, span), chip) for p in pieces]
    inputs += [whole(t) for t in tables]
    outputs = [made((width, span), F32), made((width, span), BF16)]
    return call(enter_kernel, "enter", num, inputs, outputs)


def feed_kernel(
    num, ao_ref, at_ref, go_ref, gt_ref, uaa, uba, uab, ubb, daa, dba, dab, dbb,
    bo_ref, bt_ref, ho_ref, ht_ref, uk_ref, us_ref, dk_ref, ds_ref, acts, grads, branch, back,
):
    step = pl.program_id(0)
    feats, block = uaa.shape
    span = ao_ref.shape[1]

    @pl.when(step == 0)
    def _():
        acts[:, :span] = ao_ref[...]
        acts[:, span:] = at_ref[...]
        grads[:, :span] = go_ref[...]
        grads[:, span:] = gt_ref[...]

    up_a = jnp.concatenate([uaa[...], uab[...]], axis=1)
    up_b = jnp.concatenate([uba[...], ubb[...]], axis=1)
    down_a = jnp.concatenate([daa[...], dab[...]], axis=1)
    down_b = jnp.concatenate([dba[...], dbb[...]], axis=1)
    act, grad = acts[...], grads[...]
    pre = dot(up_a, act[:feats], 0, 0) + dot(up_b, act[feats:], 0, 0)
    raised = dot(down_a, grad[:feats], 0, 0) + dot(down_b, grad[feats:], 0, 0)
    root = math.sqrt(2.0 / math.pi)
    square = pre * pre
    bent = jnp.tanh(root * pre * (1.0 + 0.044715 * square))
    part = 0.5 + 0.5 * bent
    gelu = (pre * part).astype(BF16)
    slope = part + 0.5 * root * pre * (1.0 - bent * bent) * (1.0 + 3 * 0.044715 * square)
    grad_pre = (raised * slope).astype(BF16)
    for rows, up, down in ((slice(0, feats), up_a, down_a), (slice(feats, 2 * feats), up_b, down_b)):
        forward, backward = dot(down, gelu), dot(up, grad_pre)

        @pl.when(step == 0)
        def _():
            branch[rows, :] = forward
            back[rows, :] = backward

        @pl.when(step > 0)
        def _():
            branch[rows, :] += forward
            back[rows, :] += backward

    up_grad = dot(act, grad_pre, 1, 1).astype(BF16)
    down_grad = dot(grad, gelu, 1, 1).astype(BF16)
    uk_ref[...] = up_grad[:, :block]
    us_ref[...] = up_grad[:, block:]
    dk_ref[...] = down_grad[:, :block]
    ds_ref[...] = down_grad[:, block:]

    @pl.when(step == pl.num_programs(0) - 1)
    def _():
        bo_ref[...] = branch[:, :span]
        bt_ref[...] = branch[:, span:].astype(BF16)
        ho_ref[...] = back[:, :span]
        ht_ref[...] = back[:, span:].astype(BF16)


def feed(num, acts, grads, ups, downs):
    width, span = acts[0].shape
    feats = width // 2
    hidden = downs[0].shape[1]
    block = 256
    steps = hidden // block
    here = lambda s, n: (0, s)
    inputs = [whole(a) for a in (*acts, *grads)]
    inputs += [(w, (feats, block), here) for w in (*ups, *downs)]
    tokens = [made((width, span), F32), made((width, span), BF16)]
    outputs = tokens + tokens
    outputs += [((width, hidden), BF16, (width, block), here)] * 4
    scratch = [pltpu.VMEM((width, 2 * span), BF16)] * 2 + [pltpu.VMEM((width, 2 * span), F32)] * 2
    return call(feed_kernel, "feed", num, inputs, outputs, (steps,), scratch)


def turn_kernel(num, own, got, hidden, ga, gb, ta, tb, grad_ref, one_ref, sums_ref):
    feats = ga.shape[0]
    span = own.shape[1]
    grad = own[...] + got[...].astype(F32)
    values = hidden[...]
    mean, inv_std = norm_stats(values[:feats], values[feats:])
    normed = (values - mean) * inv_std
    cross = grad * normed
    sums_ref[:, 0:1] = jnp.sum(cross, axis=1, keepdims=True)
    sums_ref[:, 1:2] = jnp.sum(grad, axis=1, keepdims=True)
    scale = jnp.concatenate([column(ta, SCALE), column(tb, SCALE)], axis=0) + 1.0
    scaled = grad * scale
    mean_plain = jnp.mean(scaled, axis=0, keepdims=True)
    mean_cross = jnp.mean(scaled * normed, axis=0, keepdims=True)
    back = inv_std * (scaled - mean_plain - normed * mean_cross)
    for rows, grad_out in ((slice(0, feats), ga), (slice(feats, 2 * feats), gb)):
        total = back[rows] + grad_out[...].astype(F32)
        grad_ref[rows, :] = total
        one_ref[rows, :] = total.astype(BF16)


def turn(num, own, got, hidden, cots, tables):
    width, span = own.shape
    chip = lambda s, n: (0, n[CHIP])
    inputs = [whole(own), whole(got), whole(hidden)]
    inputs += [(cots[0], (width // 2, span), chip), whole(cots[1])]
    inputs += [whole(t) for t in tables]
    outputs = [made((width, span), F32), made((width, span), BF16), made((width, 128), F32)]
    return call(turn_kernel, "turn", num, inputs, outputs)


def leave_kernel(num, own, got, hidden, ga, gb, ta, tb, turned, oa_ref, ob_ref, sums_ref):
    feats = ga.shape[0]
    lane = lax.broadcasted_iota(jnp.int32, (feats, sums_ref.shape[1]), 1) - 3 * num[SLOT]
    for rows, grad_out, table, out_ref in (
        (slice(0, feats), ga, ta, oa_ref),
        (slice(feats, 2 * feats), gb, tb, ob_ref),
    ):
        branch = own[rows, :] + got[rows, :].astype(F32)
        out_ref[...] = (hidden[rows, :] + (1.0 + column(table, GATE)) * branch).astype(BF16)
        term = grad_out[...].astype(F32) * branch
        total = jnp.where(lane == 2, jnp.sum(term, axis=1, keepdims=True), 0.0)
        total = jnp.where(lane == 1, turned[rows, 1:2], total)
        sums_ref[rows, :] = jnp.where(lane == 0, turned[rows, 0:1], total)


def leave(num, own, got, hidden, cots, tables, turned, lanes):
    width, span = own.shape
    chip = lambda s, n: (0, n[CHIP])
    inputs = [whole(own), whole(got), whole(hidden)]
    inputs += [(cots[0], (width // 2, span), chip), whole(cots[1])]
    inputs += [whole(t) for t in (*tables, turned)]
    outputs = [made((width // 2, span), BF16)] * 2 + [made((width, lanes), F32)]
    return call(leave_kernel, "leave", num, inputs, outputs)


def unmix_kernel(num, one_own, one_other, *refs):
    count = (len(refs) - 8) // 2
    aa, ba, ab, bb, gk_ref, gs_ref, wn_ref, wf_ref = refs[2 * count :]
    feats = aa.shape[0]
    aligned = num[ALIGNED] == 1
    mine, theirs = sorted_heads(num, refs[:count], refs[count : 2 * count])
    heads = mine.shape[0]
    ones = jnp.concatenate([one_own[...], one_other[...]], axis=1)
    near = dot(aa[:, :heads], ones[:feats], 0, 0) + dot(ba[:, :heads], ones[feats:], 0, 0)
    far = dot(ab[:, :heads], ones[:feats], 0, 0) + dot(bb[:, :heads], ones[feats:], 0, 0)
    gk_ref[...] = jnp.where(aligned, near, far).astype(BF16)
    gs_ref[...] = jnp.where(aligned, far, near).astype(BF16)
    wn_ref[...] = dot(ones, mine, 1, 1).astype(BF16)
    wf_ref[...] = dot(ones, theirs, 1, 1).astype(BF16)


def unmix(num, ones, kept, got, blocks):
    feats = blocks[0].shape[0]
    heads, tokens = sum(k.shape[0] for k in kept), kept[0].shape[1]
    last = lambda s, n: (0, 3)
    inputs = [whole(a) for a in (*ones, *kept, *got)]
    inputs += [(b, (feats, 256), last) for b in blocks]
    outputs = [made((heads, tokens), BF16)] * 2 + [made((2 * feats, heads), BF16)] * 2
    return call(unmix_kernel, "unmix", num, inputs, outputs)


def unproject_kernel(num, *refs):
    wa, wb, keep_ref, send_ref = refs[-4:]
    step = pl.program_id(0)
    feats = wa.shape[0]
    grad = jnp.concatenate([g[...] for g in refs[:-4]], axis=0)
    first, second = dot(wa[...], grad), dot(wb[...], grad)
    own = step // 2 == num[CORE]

    @pl.when(own)
    def _():
        keep_ref[:feats, :] = first
        keep_ref[feats:, :] = second

    @pl.when(jnp.logical_not(own))
    def _():
        send_ref[:feats, :] = first.astype(BF16)
        send_ref[feats:, :] = second.astype(BF16)


def unproject(num, grads, weights):
    rows, length = grads[0].shape
    feats = weights[0].shape[0]
    block = length // 4
    here = lambda s, n: (0, s)
    own = lambda s, n: (0, core_blocks(s, n)[0])
    other = lambda s, n: (0, core_blocks(s, n)[1])
    inputs = [(g, (rows, block), here) for g in grads] + [whole(w) for w in weights]
    shape = (2 * feats, length // 2)
    outputs = [(shape, F32, (2 * feats, block), own), (shape, BF16, (2 * feats, block), other)]
    return call(unproject_kernel, "unproject", num, inputs, outputs, (4,))


def weigh_kernel(num, *refs):
    act, wa, wb, ta, tb, ga_ref, gb_ref, first_ref, sums_ref, total, plain = refs[-11:]
    step = pl.program_id(0)
    feats = wa.shape[0]
    grad = jnp.concatenate([g[...] for g in refs[:-11]], axis=0)
    product = dot(act[...], grad, 1, 1)
    row = dot(jnp.ones((8, grad.shape[1]), BF16), grad, 1, 1)

    @pl.when(step == 0)
    def _():
        total[...] = product
        plain[...] = row

    @pl.when(step > 0)
    def _():
        total[...] += product
        plain[...] += row

    @pl.when(step == pl.num_programs(0) - 1)
    def _():
        for rows, weight, table, out_ref in (
            (slice(0, feats), wa, ta, ga_ref),
            (slice(feats, 2 * feats), wb, tb, gb_ref),
        ):
            grad_weight = total[rows, :]
            out_ref[...] = grad_weight.astype(BF16)
            low = weight[...].astype(F32)
            gain, bias = column(table, GAIN), column(table, BIAS)
            weighed = jnp.sum(low * grad_weight, axis=1, keepdims=True)
            shifted = jnp.sum(low * plain[0:1, :], axis=1, keepdims=True)
            for row, value in ((0, (weighed - bias * shifted) / gain), (1, shifted)):
                sums_ref[row : row + 1, rows] = jnp.broadcast_to(value, (feats, 128)).T[:1]
        first_ref[...] = jnp.where(num[ALIGNED] == 1, gb_ref[...], ga_ref[...])


def weigh(num, grads, act, weights, tables):
    rows, length = grads[0].shape
    width = act.shape[0]
    feats, columns = weights[0].shape
    block = length // 4
    here = lambda s, n: (0, s)
    inputs = [(g, (rows, block), here) for g in grads] + [(act, (width, block), here)]
    inputs += [whole(w) for w in weights] + [whole(t) for t in tables]
    outputs = [made((feats, columns), BF16)] * 3 + [made((8, width), F32)]
    scratch = [pltpu.VMEM((width, columns), F32), pltpu.VMEM((8, columns), F32)]
    return call(weigh_kernel, "weigh", num, inputs, outputs, (4,), scratch)


def finish_kernel(num, own, got, xa, xb, hidden, ta, tb, oa_ref, ob_ref):
    feats = xa.shape[0]
    grad = own[...] + got[...].astype(F32)
    first, second = xa[...].astype(F32), xb[...].astype(F32)
    mean, inv_std = norm_stats(first, second)
    first, second = (first - mean) * inv_std, (second - mean) * inv_std
    grad_a, grad_b = grad[:feats] * column(ta, GAIN), grad[feats:] * column(tb, GAIN)
    count = 2 * feats
    plain = jnp.sum(grad_a, axis=0, keepdims=True) + jnp.sum(grad_b, axis=0, keepdims=True)
    cross = jnp.sum(grad_a * first, axis=0, keepdims=True)
    cross = cross + jnp.sum(grad_b * second, axis=0, keepdims=True)
    plain, cross = plain / count, cross / count
    oa_ref[...] = hidden[:feats, :] + inv_std * (grad_a - plain - first * cross)
    ob_ref[...] = (hidden[feats:, :] + inv_std * (grad_b - plain - second * cross)).astype(BF16)


def finish(num, own, got, pieces, hidden, tables):
    width, span = own.shape
    chip = lambda s, n: (0, n[CHIP])
    inputs = [whole(own), whole(got)] + [(p, (width // 2, span), chip) for p in pieces]
    inputs += [whole(hidden)] + [whole(t) for t in tables]
    outputs = [made((width // 2, span), F32), made((width // 2, span), BF16)]
    return call(finish_kernel, "finish", num, inputs, outputs)


def swap_rows(value):
    count = lax.axis_size("row")
    return lax.ppermute(value, "row", [(i, i ^ 1) for i in range(count)])


def swap_cores(value):
    count = lax.axis_size("col")
    return lax.ppermute(value, "col", [(i, i ^ 1) for i in range(count)])


def swap_cols(value):
    return lax.ppermute(value, "col", [(i, i ^ 2) for i in range(lax.axis_size("col"))])


def swap_dp(value, bit):
    count = lax.axis_size("dp")
    return lax.ppermute(value, "dp", [(i, i ^ bit) for i in range(count)])


def in_order(flag, own, other):
    first = jnp.where(flag == 0, own, other)
    second = jnp.where(flag == 0, other, own)
    return first, second


def cut(value, start, size, axis):
    return lax.dynamic_slice_in_dim(value, start, size, axis)


def after(value, *others):
    return lax.optimization_barrier((value, *others))[0]


def tie(*values):
    return lax.optimization_barrier(values)


def plus(left, right):
    return (left.astype(F32) + right.astype(F32)).astype(BF16)


def dp_first(value):
    half = value.shape[0] // 2
    low = lax.axis_index("dp") & 1
    return plus(cut(value, low * half, half, 0), swap_dp(cut(value, (1 - low) * half, half, 0), 1))


def dp_second(total, gate=None):
    reach = 2
    while reach < lax.axis_size("dp"):
        got = swap_dp(total, reach)
        if gate is not None:
            total, gate = tie(total, gate)
        total = plus(total, got)
        reach *= 2
    return total, gate


def dp_third(total):
    low = lax.axis_index("dp") & 1
    return jnp.concatenate(in_order(low, total, swap_dp(total, 1)), axis=0)


class PairMoves:
    def __init__(self, r, c, feats, heads):
        self.r, self.j, self.h, self.k, self.feats, self.heads = r, r, c // 2, c % 2, feats, heads
        self.aligned = self.j == self.h

    def pieces(self, value):
        other = swap_rows(value)
        return value, other, swap_cores(value), swap_cores(other)

    def tables(self, mods, gain, bias, seq):
        table = jnp.concatenate([gain[None], bias[None], mods[seq]], axis=0)
        table = jnp.pad(table, ((0, 3), (0, 0)))
        return table, swap_rows(table)

    def cotangents(self, value):
        span = value.shape[1] // 2
        return value, swap_rows(cut(value, (1 - self.j) * span, span, 1))

    def flip(self, value):
        return jnp.concatenate([value[self.feats :], value[: self.feats]], axis=0)

    def qkv(self, weight):
        other = swap_cols(weight)
        mine = jnp.where(self.aligned, weight, other)
        theirs = jnp.where(self.aligned, other, weight)
        self.gate_col = other
        return mine, swap_rows(theirs)

    def feed(self, weight, gate):
        return weight, swap_rows(after(weight, gate)), swap_cols(after(weight, self.gate_col)), None

    def corner(self, blocks, gate):
        return *blocks[:3], swap_cols(after(blocks[1], gate))

    first, second, third = map(staticmethod, (dp_first, dp_second, dp_third))

    def across(self, near, got):
        part = plus(near, got)
        return part[: self.feats], swap_rows(part[self.feats :])

    def down_columns(self, near, far):
        return near, swap_cols(far)

    def extras(self, out_near, out_far, sums):
        sums = (sums + swap_cores(sums)).astype(BF16)[:, : 256 - self.heads]
        both = jnp.concatenate([out_near, sums, out_far, sums], axis=1)
        return both[: self.feats], swap_rows(both[self.feats :])

    def extras_last(self, mine, got):
        both = plus(mine, got)
        return both[:, :256], swap_cols(both[:, 256:])

    def join(self, up, mine, got):
        return jnp.concatenate([up, plus(mine, got)], axis=1)

    def unpack(self, total, count):
        hidden = total.shape[1] - 256
        ends = hidden + self.heads
        parts = total[:, :hidden], total[:, hidden:ends].T, total[:, ends : ends + count]
        return tuple(part.astype(F32) for part in parts)

    def reduce_qkv(self, part_a, part_b, first):
        cycle, corner = [], []
        for core in range(2):
            for row in range(2):
                aligned, beside = row * 4 + 2 * row + core, row * 4 + 2 * (1 - row) + core
                cycle.append((aligned, (1 - row) * 4 + 2 * row + core))
                cycle.append((beside, aligned))
                corner.append((beside, (1 - row) * 4 + 2 * row + core))
        axes = ("row", "col")
        first = lax.ppermute(first, axes, cycle)
        second = lax.ppermute(part_b, axes, corner)
        return first, second, part_a

    def qkv_sum(self, first, second, part_a):
        return plus(first, jnp.where(self.aligned, part_a, second))

    def outputs(self, own, other):
        return jnp.concatenate(in_order(self.j, own, swap_rows(other)), axis=1)

    def own_sums(self, sums):
        total = sums + swap_cores(sums)
        return total + swap_cols(total)

    def row_sums(self, sums):
        return sums[:, : self.feats] + swap_rows(sums[:, self.feats :])

    def board(self, grad, sums):
        room = ((0, 32 - sums.shape[0]), (0, grad.shape[1] - sums.shape[1]))
        return jnp.concatenate([grad, jnp.pad(sums.astype(BF16), room)], axis=0)

    def leave_board(self, both, count):
        return both[: self.feats], both[self.feats : self.feats + count, : self.feats]


class AnyMoves:
    def __init__(self, r, c, feats, heads, pairs):
        self.heads = heads
        self.r, self.j, self.q, self.h, self.k = r, r % 2, r // 2, c // 2, c % 2
        self.feats, self.pairs = feats, pairs
        self.half = feats * lax.axis_size("row") // 2
        self.aligned = self.j == 0
        cols = lax.axis_size("col")
        self.cores = [[i, i + 1] for i in range(0, cols, 2)]
        self.likes = [list(range(core, cols, 2)) for core in range(2)]

    def halves(self, value):
        return value[: self.half], value[self.half :]

    def sequence(self, value):
        full = lax.all_gather(value, "row", axis=0, tiled=True)
        full = lax.all_gather(full, "col", axis=1, tiled=True, axis_index_groups=self.cores)
        return cut(full, self.q * LENGTH, LENGTH, 1)

    def pieces(self, value):
        full = self.sequence(value)
        own = cut(full, self.k * LENGTH // 2, LENGTH // 2, 1)
        other = cut(full, (1 - self.k) * LENGTH // 2, LENGTH // 2, 1)
        return *self.halves(own), *self.halves(other)

    def tables(self, mods, gain, bias, seq):
        count = mods.shape[0]
        table = jnp.concatenate([mods.reshape(3 * count, -1), gain[None], bias[None]], axis=0)
        table = lax.all_gather(table, "row", axis=1, tiled=True)
        table = jnp.concatenate([table[3 * count :], cut(table, 3 * seq, 3, 0)], axis=0)
        table = jnp.pad(table, ((0, 3), (0, 0)))
        return table[:, : self.half], table[:, self.half :]

    def cotangents(self, value):
        span = LENGTH // 4
        own = cut(self.sequence(value), (2 * self.k + self.j) * span, span, 1)
        first, second = self.halves(own)
        return jnp.concatenate([first, first], axis=1), second

    def flip(self, value):
        return value

    def likes_gather(self, value):
        rows = lax.all_gather(value, "row", axis=0, tiled=True)
        return lax.all_gather(rows, "col", axis=0, axis_index_groups=self.likes)

    def qkv(self, weight):
        return self.halves(cut(self.likes_gather(weight), self.j, 1, 0)[0])

    def feed(self, weight, gate):
        near, far = self.likes_gather(weight)
        return *self.halves(near), *self.halves(far)

    def corner(self, blocks, gate):
        return blocks

    def scatter(self, grad):
        grad = lax.psum_scatter(grad, "row", scatter_dimension=0, tiled=True)
        grad = lax.psum_scatter(
            grad, "col", scatter_dimension=1, tiled=True, axis_index_groups=self.likes
        )
        return lax.psum(grad, "dp").astype(F32)

    def first(self, value):
        return value

    third = first

    def second(self, value, gate=None):
        return value, gate

    def down_columns(self, near, far):
        return near, far

    def across(self, near, far):
        grad = self.scatter(jnp.concatenate([near, far], axis=1))
        return grad, jnp.zeros_like(grad)

    def extras(self, out_near, out_far, sums):
        return jnp.concatenate([out_near, out_far], axis=1), sums

    def extras_last(self, both, sums):
        return self.scatter(both), self.own_sums(sums.T).T

    def join(self, up, out, sums):
        return up, out, sums

    def row_sums(self, sums):
        return sums

    def board(self, grad, sums):
        return grad, sums

    def leave_board(self, both, count):
        return both

    def unpack(self, total, count):
        up, out, sums = total
        return up.astype(F32), out.T, sums[:, :count]

    def reduce_qkv(self, part_a, part_b, first):
        grad = jnp.concatenate([part_a, part_b], axis=0)
        both = in_order(self.j, grad, jnp.zeros_like(grad))
        total = self.scatter(jnp.concatenate(both, axis=1))
        return total, total, total

    def qkv_sum(self, first, second, part_a):
        return first

    def outputs(self, own, other):
        value = jnp.concatenate([own.astype(BF16), other], axis=0)
        parts = value.reshape(lax.axis_size("row"), self.feats, -1)
        parts = lax.all_to_all(parts, "row", split_axis=0, concat_axis=0, tiled=True)
        parts = lax.all_gather(parts, "col", axis=0, axis_index_groups=self.cores)
        span = parts.shape[-1]
        parts = parts.reshape(2, self.pairs, 2, self.feats, span).transpose(3, 1, 0, 2, 4)
        parts = parts.reshape(self.feats, -1)
        width = parts.shape[1] // 2
        return cut(parts, self.k * width, width, 1)

    def own_sums(self, sums):
        total = lax.psum(sums, ("dp", "row", "col"))
        return cut(total, self.r * self.feats, self.feats, 1)


def local(
    tokens, ln_gain, ln_bias, qkv_weight, out_weight, up_weight, down_weight,
    mod_weight, timestep, block_size, cotangent,
):
    rows, cols = lax.axis_size("row"), lax.axis_size("col")
    r, c, z = lax.axis_index("row"), lax.axis_index("col"), lax.axis_index("dp")
    width = mod_weight.shape[2]
    feats, local_tokens = tokens.shape
    pairs = 2 * local_tokens // LENGTH
    assert rows == 2 * pairs and cols == 4 and LENGTH % (8 * CHUNK) == 0
    sequences = timestep.shape[0]
    seq = (z * (cols // 2) + c // 2) * pairs + r // 2
    heads = out_weight.shape[0]
    moves = PairMoves(r, c, feats, heads) if pairs == 1 else AnyMoves(r, c, feats, heads, pairs)
    block_len = cut(block_size, seq, 1, 0)[0]
    num = jnp.stack([moves.k, moves.j, moves.aligned.astype(jnp.int32), block_len, seq])

    embedded = time_embed(timestep, width)
    mods = jnp.einsum("nd,ked->nke", embedded, mod_weight.astype(F32), precision=HIGH)
    cosine, sine = rope_tables(LENGTH, HEAD_DIM)

    pieces = moves.pieces(tokens)
    tables = moves.tables(mods, ln_gain, ln_bias, seq)
    qkv = moves.qkv(qkv_weight.reshape(feats, -1))
    packed = jnp.pad(jnp.concatenate([up_weight, out_weight.T], axis=1), ((0, 0), (0, 256 - heads)))
    gate = after(qkv[1], pieces[1], tables)
    ups = moves.feed(packed, gate)
    downs = moves.feed(down_weight, gate)

    up_col, *pieces = tie(ups[2], *pieces)
    ups = (*ups[:2], up_col, ups[3])
    queries, keys, values, act_one = project(num, pieces, qkv, tables, cosine, sine)
    cots = moves.cotangents(after(cotangent, queries))
    count = heads // HEAD_DIM
    down_col, queries = tie(downs[2], queries)
    early, early_sent, early_lse = attend_forward(num, 0, 1, queries, keys, values)
    early_got = swap_rows(early_sent)
    up_row, down_row, rest, early = tie(ups[1], downs[1], queries, early)
    ups = moves.corner((ups[0], up_row, *ups[2:]), early)
    downs = moves.corner((downs[0], down_row, down_col, downs[3]), early)
    late, late_sent, late_lse = attend_forward(num, 1, count - 1, rest, keys, values)
    got = (early_got, swap_rows(late_sent))
    early, late, ups, downs, cots = tie(early, late, ups, downs, cots)
    kept = (early, late)
    lse = jnp.concatenate([early_lse, late_lse], axis=0)

    span = cots[1].shape[1]
    own, other = mix(num, kept, got, ups)
    own, cots = tie(own, cots)
    gate_a, gate_b = tables[0][4][:, None], tables[1][4][:, None]
    cot_a = cut(cots[0], moves.j * span, span, 1).astype(F32)
    grad_a = cot_a * (1.0 + gate_a)
    grad_b = cots[1].astype(F32) * (1.0 + gate_b)
    grad_two = jnp.concatenate([grad_a, grad_b], axis=0).astype(BF16)
    grads = (grad_two, swap_cores(grad_two))
    hidden, act = enter(num, own, swap_cores(other), pieces[:2], tables)
    fed = feed(num, (act, swap_cores(act)), grads, ups, downs)
    branch_own, branch_other, back_own, back_other, up_near, up_far, down_near, down_far = fed
    back_got = swap_cores(back_other)
    grad_hidden, ones, turn_sums = turn(num, back_own, back_got, hidden, cots, tables)
    down_part = moves.down_columns(down_near, down_far)
    up_part = moves.down_columns(up_near, up_far)
    branch_got = swap_cores(branch_other)
    both_ones = (ones, swap_cores(ones))
    grad_kept, grad_sent, out_near, out_far = unmix(num, both_ones, kept, got, ups)
    grad_got = swap_rows(grad_sent)
    branch_own = after(branch_own, grad_sent)
    result_a, result_b, leave_sums = leave(
        num, branch_own, branch_got, hidden, cots, tables, turn_sums, -(-3 * sequences // 128) * 128
    )
    result = moves.outputs(result_a, result_b)
    down_part = moves.across(*after(down_part, result_a))
    extra = moves.extras(out_near, out_far, leave_sums)

    grad_kept, down_keep, extra_keep = tie(grad_kept, down_part[0], extra[0])
    grads = attend_backward(num, queries, keys, values, grad_kept, grad_got, lse, cosine, sine)
    down_part, extra = (down_keep, down_part[1]), (extra_keep, extra[1])
    up_part, down_part, extra, grads, result = tie(up_part, down_part, extra, grads, result)
    down_sum = moves.first(plus(*down_part))
    up_keep, up_got = moves.across(*up_part)
    extra_keep, extra_got = moves.extras_last(*extra)
    grads, up_keep, extra_keep = tie(grads, up_keep, extra_keep)
    keep, send = unproject(num, grads, qkv)
    send_got = swap_cores(send)
    up_sum = moves.join(plus(up_keep, up_got), extra_keep, extra_got)
    grads, keep, down_sum, up_sum = tie(grads, keep, down_sum, up_sum)
    qkv_a, qkv_b, qkv_first, norm_sums = weigh(num, grads, act_one, qkv, tables)
    norm_sums = moves.row_sums(norm_sums[:2])
    down_sum, _ = moves.second(down_sum)
    up_sum = moves.first(up_sum)
    send_got, norm_sums = tie(send_got, norm_sums)
    kept_core = keep + send_got.astype(F32)
    crossing = cut(kept_core, (1 - moves.j) * span, span, 1).astype(BF16)
    crossing = moves.flip(crossing)
    own = cut(kept_core, moves.j * span, span, 1)
    crossing, norm_sums, qkv_a, qkv_b, qkv_first = tie(crossing, norm_sums, qkv_a, qkv_b, qkv_first)
    qkv_part = moves.reduce_qkv(qkv_a, qkv_b, qkv_first)
    crossed = swap_rows(crossing)
    norm_sums = moves.own_sums(norm_sums)
    qkv_sum = moves.first(moves.board(moves.qkv_sum(*qkv_part), norm_sums))
    crossed, down_grad = tie(crossed, moves.third(down_sum))
    tokens_a, tokens_b = finish(num, own, crossed, pieces[:2], grad_hidden, tables)
    up_sum, tokens_b = moves.second(up_sum, tokens_b)
    qkv_sum, tokens_b = moves.second(qkv_sum, tokens_b)
    tokens_grad = moves.outputs(tokens_a, tokens_b)
    down_grad = down_grad.astype(F32)
    up_grad, out_grad, totals = moves.unpack(moves.third(up_sum), 3 * sequences)
    totals = totals.reshape(feats, sequences, 3)
    mod_grad = jnp.einsum("nd,enk->ked", embedded, totals, precision=HIGH)
    qkv_grad, norm_sums = moves.leave_board(moves.third(qkv_sum), 2)
    qkv_grad = qkv_grad.astype(F32)

    return (
        result,
        tokens_grad.astype(F32),
        norm_sums[0].astype(F32),
        norm_sums[1].astype(F32),
        qkv_grad.reshape(qkv_weight.shape),
        out_grad,
        up_grad,
        down_grad,
        mod_grad,
    )


def solution(mesh):
    placed = (
        P("row", ("dp", "col")),
        P("row"),
        P("row"),
        P("row", None, "col"),
        P("col", "row"),
        P("row", "col"),
        P("row", "col"),
        P(None, "row", None),
        P(),
        P(),
        P("row", ("dp", "col")),
    )
    return jax.shard_map(
        local,
        mesh=mesh,
        in_specs=placed,
        out_specs=(
            P("row", ("dp", "col")),
            P("row", ("dp", "col")),
            P("row"),
            P("row"),
            P("row", None, "col"),
            P("col", "row"),
            P("row", "col"),
            P("row", "col"),
            P(None, "row", None),
        ),
        check_vma=False,
    )
```

```python
from functools import partial
import math

import jax
import jax.numpy as jnp
from jax import lax
from jax.experimental import pallas as pl
from jax.experimental.pallas import tpu as pltpu
from jax.sharding import PartitionSpec as P

HEAD_DIM = 64
LENGTH = 2048
CHUNK = 256
LANES = 256
EPSILON = 1e-05
HIGH = lax.Precision.HIGHEST
F32 = jnp.float32
BF16 = jnp.bfloat16
SCALE_T = 0.03
MICROS = dict(project=9, attend_forward=26, mix=5, enter=5, feed=32, turn=6, leave=5, unmix=5, attend_backward=33,
              unproject=30, weigh=30, finish=5)
FULL = ("weigh", "unproject", "finish")
FLOPS = {k: int(v * (1.0 if k in FULL else SCALE_T) * 1_153_000_000) for k, v in MICROS.items()}
GAIN, BIAS, SCALE, SHIFT, GATE = range(5)
CORE, CHIP, ALIGNED, BLOCK, SLOT = range(5)


def time_embed(steps_in, width_all):
    half_width = width_all // 2
    frequency = jnp.exp(-math.log(10000.0) * jnp.arange(half_width, dtype=F32) / half_width)
    angles = steps_in.astype(F32)[:, None] * frequency[None, :]
    return jnp.concatenate([jnp.sin(angles), jnp.cos(angles)], axis=1)


def rope_tables(length, head_width):
    half_dim = head_width // 2
    frequency = jnp.exp(-math.log(10000.0) * jnp.arange(half_dim, dtype=F32) / half_dim)
    angles = frequency[:, None] * jnp.arange(length, dtype=F32)[None, :]
    return jnp.cos(angles), jnp.sin(angles)


def dot(left, right, left_dim=1, right_dim=0):
    dims = (((left_dim,), (right_dim,)), ((), ()))
    return lax.dot_general(left, right, dims, preferred_element_type=F32)


def call(kernel, name, numbers, inputs, outputs, grid=(1,), scratch=()):
    def spec(shape, block, index):
        if block is None:
            return pl.BlockSpec(shape, lambda *_: (0,) * len(shape))
        return pl.BlockSpec(block, index)

    return pl.pallas_call(
        kernel,
        grid_spec=pltpu.PrefetchScalarGridSpec(
            num_scalar_prefetch=1,
            grid=grid,
            in_specs=[spec(a.shape, block, index) for a, block, index in inputs],
            out_specs=[spec(shape, block, index) for shape, _, block, index in outputs],
            scratch_shapes=list(scratch),
        ),
        out_shape=[jax.ShapeDtypeStruct(shape, dtype) for shape, dtype, _, _ in outputs],
        compiler_params=pltpu.CompilerParams(vmem_limit_bytes=58 * 1024 * 1024),
        cost_estimate=pl.CostEstimate(flops=FLOPS[name], transcendentals=0, bytes_accessed=0),
        name=name,
    )(numbers, *[a for a, _, _ in inputs])


def whole(array):
    return array, None, None


def made(shape, dtype):
    return shape, dtype, None, None


def column(table, row):
    return table[...].T[:, row : row + 1]


def norm_stats(first, second):
    count = first.shape[0] + second.shape[0]
    total = jnp.sum(first, axis=0, keepdims=True) + jnp.sum(second, axis=0, keepdims=True)
    square = jnp.sum(first * first, axis=0, keepdims=True)
    square = square + jnp.sum(second * second, axis=0, keepdims=True)
    mean = total / count
    return mean, lax.rsqrt(square / count - mean * mean + EPSILON)


def project_kernel(
    num, xa, xb, ca, cb, wa, wb, ta, tb, cos_ref, sin_ref, q_ref, k_ref, v_ref, act_ref, weight
):
    step = pl.program_id(0)
    feats = xa.shape[0]

    @pl.when(step == 0)
    def _():
        weight[:, :feats] = wa[...].T
        weight[:, feats:] = wb[...].T

    own = step // 2 == num[CORE]
    first = jnp.where(own, xa[...], ca[...]).astype(F32)
    second = jnp.where(own, xb[...], cb[...]).astype(F32)
    mean, inv_std = norm_stats(first, second)
    first = (first - mean) * inv_std * column(ta, GAIN) + column(ta, BIAS)
    second = (second - mean) * inv_std * column(tb, GAIN) + column(tb, BIAS)
    act_ref[:feats, :] = first.astype(BF16)
    act_ref[feats:, :] = second.astype(BF16)
    projected = dot(weight[...], act_ref[...])
    rows = q_ref.shape[0]
    half = HEAD_DIM // 2
    cosine, sine = cos_ref[...], sin_ref[...]
    for out_ref, base in ((q_ref, 0), (k_ref, rows)):
        for head in range(0, rows, HEAD_DIM):
            front = projected[base + head : base + head + half]
            back = projected[base + head + half : base + head + HEAD_DIM]
            out_ref[head : head + half, :] = (front * cosine - back * sine).astype(BF16)
            out_ref[head + half : head + HEAD_DIM, :] = (back * cosine + front * sine).astype(BF16)
    v_ref[...] = projected[2 * rows :].astype(BF16)


def core_blocks(step, num):
    early = jnp.minimum(step, 1)
    late = jnp.maximum(step - 2, 0)
    flag = num[CORE] == 0
    return jnp.where(flag, early, late), jnp.where(flag, late, early)


def project(num, pieces, weights, tables, cosine, sine):
    feats, tokens = pieces[0].shape
    block = tokens // 2
    columns = weights[0].shape[1]
    rows = columns // 3
    own = lambda s, n: (0, core_blocks(s, n)[0])
    other = lambda s, n: (0, core_blocks(s, n)[1])
    here = lambda s, n: (0, s)
    maps = (own, own, other, other)
    inputs = [(piece, (feats, block), where) for piece, where in zip(pieces, maps)]
    inputs += [whole(w) for w in weights] + [whole(t) for t in tables]
    inputs += [(t, (t.shape[0], block), here) for t in (cosine, sine)]
    outputs = [((rows, 2 * tokens), BF16, (rows, block), here)] * 3
    outputs += [((2 * feats, 2 * tokens), BF16, (2 * feats, block), here)]
    scratch = [pltpu.VMEM((columns, 2 * feats), BF16)]
    return call(project_kernel, "project", num, inputs, outputs, (4,), scratch)


def diagonal_mask(num):
    key_block = lax.broadcasted_iota(jnp.int32, (CHUNK, CHUNK), 0) // num[BLOCK]
    query_block = lax.broadcasted_iota(jnp.int32, (CHUNK, CHUNK), 1) // num[BLOCK]
    return key_block <= query_block


def attend_forward_kernel(num, q_ref, k_ref, v_ref, keep_ref, send_ref, lse_ref, keys):
    keys[...] = k_ref[...].T
    visible = diagonal_mask(num)
    for step in range(q_ref.shape[1] // CHUNK):
        here = slice(step * CHUNK, (step + 1) * CHUNK)
        past = slice(0, step * CHUNK)
        query = q_ref[:, here] * BF16(0.125)
        diag = jnp.where(visible, dot(keys[here, :], query), -1e30)
        top = jnp.max(diag, axis=0, keepdims=True)
        if step:
            scores = dot(keys[past, :], query)
            top = jnp.maximum(top, jnp.max(scores, axis=0, keepdims=True))
        weight = jnp.exp(diag - top)
        total = jnp.sum(weight, axis=0, keepdims=True)
        mixed = dot(v_ref[:, here], weight.astype(BF16))
        if step:
            weight = jnp.exp(scores - top)
            total = total + jnp.sum(weight, axis=0, keepdims=True)
            mixed = mixed + dot(v_ref[:, past], weight.astype(BF16))
        mixed = (mixed / total).astype(BF16)
        lse_ref[0, :, here] = top + jnp.log(total)
        core, chip, part = step // 4, step // 2 % 2, step % 2
        slot = jnp.where(num[CORE] == core, 0, 2) + part
        place = pl.ds(pl.multiple_of(slot * CHUNK, CHUNK), CHUNK)

        @pl.when(num[CHIP] == chip)
        def _():
            keep_ref[:, place] = mixed

        @pl.when(num[CHIP] != chip)
        def _():
            send_ref[:, place] = mixed


def attend_forward(num, first, count, queries, keys, values):
    length = queries.shape[1]
    rows = count * HEAD_DIM
    there = lambda h, n: (first + h, 0)
    here = lambda h, n: (h, 0)
    inputs = [(a, (HEAD_DIM, length), there) for a in (queries, keys, values)]
    outputs = [((rows, length // 2), BF16, (HEAD_DIM, length // 2), here)] * 2
    outputs += [((count, 1, length), F32, (1, 1, length), lambda h, n: (h, 0, 0))]
    scratch = [pltpu.VMEM((length, HEAD_DIM), BF16)]
    return call(attend_forward_kernel, "attend_forward", num, inputs, outputs, (count,), scratch)


def attend_backward_kernel(
    num, q_ref, k_ref, v_ref, keep_ref, got_ref, lse_ref, cos_ref, sin_ref,
    dq_ref, dk_ref, dv_ref, g_ref, keys, values, queries, grads, key_sum, value_sum,
):
    length = q_ref.shape[1]
    half = HEAD_DIM // 2
    span = length // 4
    for place in range(4):
        core, chip = place // 2, place % 2
        slot = jnp.where(num[CORE] == core, 0, 1)
        there = pl.ds(pl.multiple_of(slot * span, span), span)
        part = jnp.where(num[CHIP] == chip, keep_ref[:, there], got_ref[:, there])
        g_ref[:, place * span : (place + 1) * span] = part
    keys[...] = k_ref[...].T
    values[...] = v_ref[...].T
    queries[...] = (q_ref[...] * BF16(0.125)).T
    grads[...] = g_ref[...].T
    visible = diagonal_mask(num)

    def store_unrotated(out_ref, grad, where):
        front, back = grad[:half], grad[half:]
        cosine, sine = cos_ref[:, where], sin_ref[:, where]
        out_ref[:half, where] = (front * cosine + back * sine).astype(BF16)
        out_ref[half:, where] = (back * cosine - front * sine).astype(BF16)

    for step in range(length // CHUNK):
        here = slice(step * CHUNK, (step + 1) * CHUNK)
        past = slice(0, step * CHUNK)
        query = q_ref[:, here] * BF16(0.125)
        grad = g_ref[:, here]
        lse = lse_ref[0, :, here]
        diag = jnp.where(visible, dot(keys[here, :], query), -1e30)
        weight = jnp.exp(diag - lse)
        grad_weight = dot(values[here, :], grad)
        delta = jnp.sum(weight * grad_weight, axis=0, keepdims=True)
        if step:
            weight_past = jnp.exp(dot(keys[past, :], query) - lse)
            grad_past = dot(values[past, :], grad)
            delta = delta + jnp.sum(weight_past * grad_past, axis=0, keepdims=True)
        grad_score = (weight * (grad_weight - delta)).astype(BF16)
        grad_query = dot(k_ref[:, here], grad_score)
        value_sum[here, :] = dot(weight.astype(BF16), grads[here, :])
        key_sum[here, :] = dot(grad_score, queries[here, :])
        if step:
            grad_score = (weight_past * (grad_past - delta)).astype(BF16)
            grad_query = grad_query + dot(k_ref[:, past], grad_score)
            value_sum[past, :] += dot(weight_past.astype(BF16), grads[here, :])
            key_sum[past, :] += dot(grad_score, queries[here, :])
        store_unrotated(dq_ref, grad_query * 0.125, here)
    store_unrotated(dk_ref, key_sum[...].T, slice(0, length))
    dv_ref[...] = value_sum[...].T.astype(BF16)


def attend_backward(num, queries, keys, values, kept, got, lse, cosine, sine):
    rows, length = queries.shape
    heads = rows // HEAD_DIM
    here = lambda h, n: (h, 0)
    inputs = [(a, (HEAD_DIM, length), here) for a in (queries, keys, values)]
    inputs += [(a, (HEAD_DIM, length // 2), here) for a in (kept, got)]
    inputs += [(lse, (1, 1, length), lambda h, n: (h, 0, 0)), whole(cosine), whole(sine)]
    outputs = [((rows, length), BF16, (HEAD_DIM, length), here)] * 3
    scratch = [pltpu.VMEM((HEAD_DIM, length), BF16)] + [pltpu.VMEM((length, HEAD_DIM), BF16)] * 4
    scratch += [pltpu.VMEM((length, HEAD_DIM), F32)] * 2
    return call(attend_backward_kernel, "attend_backward", num, inputs, outputs, (heads,), scratch)


def sorted_heads(num, kept, got):
    aligned = num[ALIGNED] == 1
    kept = jnp.concatenate([k[...] for k in kept], axis=0)
    got = jnp.concatenate([g[...] for g in got], axis=0)
    return jnp.where(aligned, kept, got), jnp.where(aligned, got, kept)


def mix_kernel(num, *refs):
    count = (len(refs) - 6) // 2
    aa, ba, ab, bb, own_ref, other_ref = refs[2 * count :]
    feats = aa.shape[0]
    mine, theirs = sorted_heads(num, refs[:count], refs[count : 2 * count])
    heads = mine.shape[0]
    span = own_ref.shape[1]
    for rows, near, far in ((slice(0, feats), aa, ab), (slice(feats, 2 * feats), ba, bb)):
        total = dot(near[:, :heads], mine) + dot(far[:, :heads], theirs)
        own_ref[rows, :] = total[:, :span]
        other_ref[rows, :] = total[:, span:].astype(BF16)


def mix(num, kept, got, blocks):
    feats = blocks[0].shape[0]
    span = kept[0].shape[1] // 2
    last = lambda s, n: (0, 3)
    inputs = [whole(a) for a in (*kept, *got)] + [(b, (feats, 256), last) for b in blocks]
    outputs = [made((2 * feats, span), F32), made((2 * feats, span), BF16)]
    return call(mix_kernel, "mix", num, inputs, outputs)


def enter_kernel(num, own, got, xa, xb, ta, tb, hidden_ref, act_ref):
    feats = xa.shape[0]
    total = own[...] + got[...].astype(F32)
    first = total[:feats] + xa[...].astype(F32)
    second = total[feats:] + xb[...].astype(F32)
    hidden_ref[:feats, :] = first
    hidden_ref[feats:, :] = second
    mean, inv_std = norm_stats(first, second)
    first = (first - mean) * inv_std * (1.0 + column(ta, SCALE)) + column(ta, SHIFT)
    second = (second - mean) * inv_std * (1.0 + column(tb, SCALE)) + column(tb, SHIFT)
    act_ref[:feats, :] = first.astype(BF16)
    act_ref[feats:, :] = second.astype(BF16)


def token_blocks(span):
    steps = span // LANES
    return steps, lambda s, n: (0, s), lambda s, n: (0, n[CHIP] * steps + s)


def enter(num, own, got, pieces, tables):
    width, span = own.shape
    steps, here, chip = token_blocks(span)
    inputs = [(a, (width, LANES), here) for a in (own, got)]
    inputs += [(p, (width // 2, LANES), chip) for p in pieces] + [whole(t) for t in tables]
    outputs = [((width, span), kind, (width, LANES), here) for kind in (F32, BF16)]
    return call(enter_kernel, "enter", num, inputs, outputs, (steps,))


def feed_kernel(
    num, ao_ref, at_ref, go_ref, gt_ref, uaa, uba, uab, ubb, daa, dba, dab, dbb,
    bo_ref, bt_ref, ho_ref, ht_ref, uk_ref, us_ref, dk_ref, ds_ref, acts, grads, branch, back,
):
    step = pl.program_id(0)
    feats, block = uaa.shape
    span = ao_ref.shape[1]

    @pl.when(step == 0)
    def _():
        acts[:, :span] = ao_ref[...]
        acts[:, span:] = at_ref[...]
        grads[:, :span] = go_ref[...]
        grads[:, span:] = gt_ref[...]

    up_a = jnp.concatenate([uaa[...], uab[...]], axis=1)
    up_b = jnp.concatenate([uba[...], ubb[...]], axis=1)
    down_a = jnp.concatenate([daa[...], dab[...]], axis=1)
    down_b = jnp.concatenate([dba[...], dbb[...]], axis=1)
    act, grad = acts[...], grads[...]
    pre = dot(up_a, act[:feats], 0, 0) + dot(up_b, act[feats:], 0, 0)
    raised = dot(down_a, grad[:feats], 0, 0) + dot(down_b, grad[feats:], 0, 0)
    root = math.sqrt(2.0 / math.pi)
    square = pre * pre
    bent = jnp.tanh(root * pre * (1.0 + 0.044715 * square))
    part = 0.5 + 0.5 * bent
    gelu = (pre * part).astype(BF16)
    slope = part + 0.5 * root * pre * (1.0 - bent * bent) * (1.0 + 3 * 0.044715 * square)
    grad_pre = (raised * slope).astype(BF16)
    for rows, up, down in ((slice(0, feats), up_a, down_a), (slice(feats, 2 * feats), up_b, down_b)):
        forward, backward = dot(down, gelu), dot(up, grad_pre)

        @pl.when(step == 0)
        def _():
            branch[rows, :] = forward
            back[rows, :] = backward

        @pl.when(step > 0)
        def _():
            branch[rows, :] += forward
            back[rows, :] += backward

    up_grad = dot(act, grad_pre, 1, 1).astype(BF16)
    down_grad = dot(grad, gelu, 1, 1).astype(BF16)
    uk_ref[...] = up_grad[:, :block]
    us_ref[...] = up_grad[:, block:]
    dk_ref[...] = down_grad[:, :block]
    ds_ref[...] = down_grad[:, block:]

    @pl.when(step == pl.num_programs(0) - 1)
    def _():
        bo_ref[...] = branch[:, :span]
        bt_ref[...] = branch[:, span:].astype(BF16)
        ho_ref[...] = back[:, :span]
        ht_ref[...] = back[:, span:].astype(BF16)


def feed(num, acts, grads, ups, downs):
    width, span = acts[0].shape
    feats = width // 2
    hidden = downs[0].shape[1]
    block = 256
    steps = hidden // block
    here = lambda s, n: (0, s)
    inputs = [whole(a) for a in (*acts, *grads)]
    inputs += [(w, (feats, block), here) for w in (*ups, *downs)]
    tokens = [made((width, span), F32), made((width, span), BF16)]
    outputs = tokens + tokens
    outputs += [((width, hidden), BF16, (width, block), here)] * 4
    scratch = [pltpu.VMEM((width, 2 * span), BF16)] * 2 + [pltpu.VMEM((width, 2 * span), F32)] * 2
    return call(feed_kernel, "feed", num, inputs, outputs, (steps,), scratch)


def turn_kernel(num, own, got, hidden, ga, gb, ta, tb, grad_ref, one_ref, sums_ref):
    feats = ga.shape[0]
    span = own.shape[1]
    grad = own[...] + got[...].astype(F32)
    values = hidden[...]
    mean, inv_std = norm_stats(values[:feats], values[feats:])
    normed = (values - mean) * inv_std
    cross = grad * normed

    @pl.when(pl.program_id(0) == 0)
    def _():
        sums_ref[...] = jnp.zeros_like(sums_ref)

    sums_ref[:, 0:1] += jnp.sum(cross, axis=1, keepdims=True)
    sums_ref[:, 1:2] += jnp.sum(grad, axis=1, keepdims=True)
    scale = jnp.concatenate([column(ta, SCALE), column(tb, SCALE)], axis=0) + 1.0
    scaled = grad * scale
    mean_plain = jnp.mean(scaled, axis=0, keepdims=True)
    mean_cross = jnp.mean(scaled * normed, axis=0, keepdims=True)
    back = inv_std * (scaled - mean_plain - normed * mean_cross)
    for rows, grad_out in ((slice(0, feats), ga), (slice(feats, 2 * feats), gb)):
        total = back[rows] + grad_out[...].astype(F32)
        grad_ref[rows, :] = total
        one_ref[rows, :] = total.astype(BF16)


def turn(num, own, got, hidden, cots, tables):
    width, span = own.shape
    steps, here, chip = token_blocks(span)
    inputs = [(a, (width, LANES), here) for a in (own, got, hidden)]
    inputs += [(c, (width // 2, LANES), where) for c, where in zip(cots, (chip, here))]
    inputs += [whole(t) for t in tables]
    outputs = [((width, span), kind, (width, LANES), here) for kind in (F32, BF16)]
    outputs += [made((width, 128), F32)]
    return call(turn_kernel, "turn", num, inputs, outputs, (steps,))


def leave_kernel(num, own, got, hidden, ga, gb, ta, tb, turned, oa_ref, ob_ref, sums_ref):
    feats = ga.shape[0]
    lane = lax.broadcasted_iota(jnp.int32, (feats, sums_ref.shape[1]), 1) - 3 * num[SLOT]
    for rows, grad_out, table, out_ref in (
        (slice(0, feats), ga, ta, oa_ref),
        (slice(feats, 2 * feats), gb, tb, ob_ref),
    ):
        branch = own[rows, :] + got[rows, :].astype(F32)
        out_ref[...] = (hidden[rows, :] + (1.0 + column(table, GATE)) * branch).astype(BF16)
        term = grad_out[...].astype(F32) * branch
        total = jnp.where(lane == 2, jnp.sum(term, axis=1, keepdims=True), 0.0)

        @pl.when(pl.program_id(0) == 0)
        def _():
            start = jnp.where(lane == 1, turned[rows, 1:2], total)
            sums_ref[rows, :] = jnp.where(lane == 0, turned[rows, 0:1], start)

        @pl.when(pl.program_id(0) > 0)
        def _():
            sums_ref[rows, :] += total


def leave(num, own, got, hidden, cots, tables, turned, lanes):
    width, span = own.shape
    steps, here, chip = token_blocks(span)
    inputs = [(a, (width, LANES), here) for a in (own, got, hidden)]
    inputs += [(c, (width // 2, LANES), where) for c, where in zip(cots, (chip, here))]
    inputs += [whole(t) for t in (*tables, turned)]
    outputs = [((width // 2, span), BF16, (width // 2, LANES), here)] * 2
    outputs += [made((width, lanes), F32)]
    return call(leave_kernel, "leave", num, inputs, outputs, (steps,))


def unmix_kernel(num, one_own, one_other, *refs):
    count = (len(refs) - 8) // 2
    aa, ba, ab, bb, gk_ref, gs_ref, wn_ref, wf_ref = refs[2 * count :]
    feats = aa.shape[0]
    aligned = num[ALIGNED] == 1
    mine, theirs = sorted_heads(num, refs[:count], refs[count : 2 * count])
    heads = mine.shape[0]
    ones = jnp.concatenate([one_own[...], one_other[...]], axis=1)
    near = dot(aa[:, :heads], ones[:feats], 0, 0) + dot(ba[:, :heads], ones[feats:], 0, 0)
    far = dot(ab[:, :heads], ones[:feats], 0, 0) + dot(bb[:, :heads], ones[feats:], 0, 0)
    gk_ref[...] = jnp.where(aligned, near, far).astype(BF16)
    gs_ref[...] = jnp.where(aligned, far, near).astype(BF16)
    wn_ref[...] = dot(ones, mine, 1, 1).astype(BF16)
    wf_ref[...] = dot(ones, theirs, 1, 1).astype(BF16)


def unmix(num, ones, kept, got, blocks):
    feats = blocks[0].shape[0]
    heads, tokens = sum(k.shape[0] for k in kept), kept[0].shape[1]
    last = lambda s, n: (0, 3)
    inputs = [whole(a) for a in (*ones, *kept, *got)]
    inputs += [(b, (feats, 256), last) for b in blocks]
    outputs = [made((heads, tokens), BF16)] * 2 + [made((2 * feats, heads), BF16)] * 2
    return call(unmix_kernel, "unmix", num, inputs, outputs)


def unproject_kernel(num, *refs):
    wa, wb, keep_ref, send_ref = refs[-4:]
    step = pl.program_id(0)
    feats = wa.shape[0]
    grad = jnp.concatenate([g[...] for g in refs[:-4]], axis=0)
    first, second = dot(wa[...], grad), dot(wb[...], grad)
    own = step // 2 == num[CORE]

    @pl.when(own)
    def _():
        keep_ref[:feats, :] = first
        keep_ref[feats:, :] = second

    @pl.when(jnp.logical_not(own))
    def _():
        send_ref[:feats, :] = first.astype(BF16)
        send_ref[feats:, :] = second.astype(BF16)


def unproject(num, grads, weights):
    rows, length = grads[0].shape
    feats = weights[0].shape[0]
    block = length // 4
    here = lambda s, n: (0, s)
    own = lambda s, n: (0, core_blocks(s, n)[0])
    other = lambda s, n: (0, core_blocks(s, n)[1])
    inputs = [(g, (rows, block), here) for g in grads] + [whole(w) for w in weights]
    shape = (2 * feats, length // 2)
    outputs = [(shape, F32, (2 * feats, block), own), (shape, BF16, (2 * feats, block), other)]
    return call(unproject_kernel, "unproject", num, inputs, outputs, (4,))


def weigh_kernel(num, *refs):
    act, wa, wb, ta, tb, ga_ref, gb_ref, first_ref, sums_ref, total, plain = refs[-11:]
    step = pl.program_id(0)
    feats = wa.shape[0]
    grad = jnp.concatenate([g[...] for g in refs[:-11]], axis=0)
    product = dot(act[...], grad, 1, 1)
    row = dot(jnp.ones((8, grad.shape[1]), BF16), grad, 1, 1)

    @pl.when(step == 0)
    def _():
        total[...] = product
        plain[...] = row

    @pl.when(step > 0)
    def _():
        total[...] += product
        plain[...] += row

    @pl.when(step == pl.num_programs(0) - 1)
    def _():
        for rows, weight, table, out_ref in (
            (slice(0, feats), wa, ta, ga_ref),
            (slice(feats, 2 * feats), wb, tb, gb_ref),
        ):
            grad_weight = total[rows, :]
            out_ref[...] = grad_weight.astype(BF16)
            low = weight[...].astype(F32)
            gain, bias = column(table, GAIN), column(table, BIAS)
            weighed = jnp.sum(low * grad_weight, axis=1, keepdims=True)
            shifted = jnp.sum(low * plain[0:1, :], axis=1, keepdims=True)
            for row, value in ((0, (weighed - bias * shifted) / gain), (1, shifted)):
                sums_ref[row : row + 1, rows] = jnp.broadcast_to(value, (feats, 128)).T[:1]
        first_ref[...] = jnp.where(num[ALIGNED] == 1, gb_ref[...], ga_ref[...])


def weigh(num, grads, act, weights, tables):
    rows, length = grads[0].shape
    width = act.shape[0]
    feats, columns = weights[0].shape
    block = length // 4
    here = lambda s, n: (0, s)
    inputs = [(g, (rows, block), here) for g in grads] + [(act, (width, block), here)]
    inputs += [whole(w) for w in weights] + [whole(t) for t in tables]
    outputs = [made((feats, columns), BF16)] * 3 + [made((8, width), F32)]
    scratch = [pltpu.VMEM((width, columns), F32), pltpu.VMEM((8, columns), F32)]
    return call(weigh_kernel, "weigh", num, inputs, outputs, (4,), scratch)


def finish_kernel(num, own, got, xa, xb, hidden, ta, tb, oa_ref, ob_ref):
    feats = xa.shape[0]
    grad = own[...] + got[...].astype(F32)
    first, second = xa[...].astype(F32), xb[...].astype(F32)
    mean, inv_std = norm_stats(first, second)
    first, second = (first - mean) * inv_std, (second - mean) * inv_std
    grad_a, grad_b = grad[:feats] * column(ta, GAIN), grad[feats:] * column(tb, GAIN)
    count = 2 * feats
    plain = jnp.sum(grad_a, axis=0, keepdims=True) + jnp.sum(grad_b, axis=0, keepdims=True)
    cross = jnp.sum(grad_a * first, axis=0, keepdims=True)
    cross = cross + jnp.sum(grad_b * second, axis=0, keepdims=True)
    plain, cross = plain / count, cross / count
    oa_ref[...] = hidden[:feats, :] + inv_std * (grad_a - plain - first * cross)
    ob_ref[...] = (hidden[feats:, :] + inv_std * (grad_b - plain - second * cross)).astype(BF16)


def finish(num, own, got, pieces, hidden, tables):
    width, span = own.shape
    steps, here, chip = token_blocks(span)
    inputs = [(a, (width, LANES), here) for a in (own, got)]
    inputs += [(p, (width // 2, LANES), chip) for p in pieces] + [(hidden, (width, LANES), here)]
    inputs += [whole(t) for t in tables]
    outputs = [((width // 2, span), kind, (width // 2, LANES), here) for kind in (F32, BF16)]
    return call(finish_kernel, "finish", num, inputs, outputs, (steps,))


def swap_rows(value):
    count = lax.axis_size("row")
    return lax.ppermute(value, "row", [(i, i ^ 1) for i in range(count)])


def swap_cores(value):
    count = lax.axis_size("col")
    return lax.ppermute(value, "col", [(i, i ^ 1) for i in range(count)])


def swap_cols(value):
    return lax.ppermute(value, "col", [(i, i ^ 2) for i in range(lax.axis_size("col"))])


def swap_dp(value, bit):
    count = lax.axis_size("dp")
    return lax.ppermute(value, "dp", [(i, i ^ bit) for i in range(count)])


def in_order(flag, own, other):
    first = jnp.where(flag == 0, own, other)
    second = jnp.where(flag == 0, other, own)
    return first, second


def cut(value, start, size, axis):
    return lax.dynamic_slice_in_dim(value, start, size, axis)


def after(value, *others):
    return lax.optimization_barrier((value, *others))[0]


def tie(*values):
    return lax.optimization_barrier(values)


def plus(left, right):
    return (left.astype(F32) + right.astype(F32)).astype(BF16)


def dp_first(value):
    half = value.shape[0] // 2
    low = lax.axis_index("dp") & 1
    return plus(cut(value, low * half, half, 0), swap_dp(cut(value, (1 - low) * half, half, 0), 1))


def dp_second(total, gate=None):
    reach = 2
    while reach < lax.axis_size("dp"):
        got = swap_dp(total, reach)
        if gate is not None:
            total, gate = tie(total, gate)
        total = plus(total, got)
        reach *= 2
    return total, gate


def dp_third(total):
    low = lax.axis_index("dp") & 1
    return jnp.concatenate(in_order(low, total, swap_dp(total, 1)), axis=0)


class PairMoves:
    def __init__(self, r, c, feats, heads):
        self.r, self.j, self.h, self.k, self.feats, self.heads = r, r, c // 2, c % 2, feats, heads
        self.aligned = self.j == self.h

    def pieces(self, value):
        other = swap_rows(value)
        return value, other, swap_cores(value), swap_cores(other)

    def tables(self, mods, gain, bias, seq):
        table = jnp.concatenate([gain[None], bias[None], mods[seq]], axis=0)
        table = jnp.pad(table, ((0, 3), (0, 0)))
        return table, swap_rows(table)

    def cotangents(self, value):
        span = value.shape[1] // 2
        return value, swap_rows(cut(value, (1 - self.j) * span, span, 1))

    def flip(self, value):
        return jnp.concatenate([value[self.feats :], value[: self.feats]], axis=0)

    def qkv(self, weight):
        other = swap_cols(weight)
        mine = jnp.where(self.aligned, weight, other)
        theirs = jnp.where(self.aligned, other, weight)
        self.gate_col = other
        return mine, swap_rows(theirs)

    def feed(self, weight, gate):
        return weight, swap_rows(after(weight, gate)), swap_cols(after(weight, self.gate_col)), None

    def corner(self, blocks, gate):
        return *blocks[:3], swap_cols(after(blocks[1], gate))

    first, second, third = map(staticmethod, (dp_first, dp_second, dp_third))

    def across(self, near, got):
        part = plus(near, got)
        return part[: self.feats], swap_rows(part[self.feats :])

    def down_columns(self, near, far):
        return near, swap_cols(far)

    def extras(self, out_near, out_far, sums):
        sums = (sums + swap_cores(sums)).astype(BF16)[:, : 256 - self.heads]
        both = jnp.concatenate([out_near, sums, out_far, sums], axis=1)
        return both[: self.feats], swap_rows(both[self.feats :])

    def extras_last(self, mine, got):
        both = plus(mine, got)
        return both[:, :256], swap_cols(both[:, 256:])

    def join(self, up, mine, got):
        return jnp.concatenate([up, plus(mine, got)], axis=1)

    def unpack(self, total, count):
        hidden = total.shape[1] - 256
        ends = hidden + self.heads
        parts = total[:, :hidden], total[:, hidden:ends].T, total[:, ends : ends + count]
        return tuple(part.astype(F32) for part in parts)

    def reduce_qkv(self, part_a, part_b, first):
        cycle, corner = [], []
        for core in range(2):
            for row in range(2):
                aligned, beside = row * 4 + 2 * row + core, row * 4 + 2 * (1 - row) + core
                cycle.append((aligned, (1 - row) * 4 + 2 * row + core))
                cycle.append((beside, aligned))
                corner.append((beside, (1 - row) * 4 + 2 * row + core))
        axes = ("row", "col")
        first = lax.ppermute(first, axes, cycle)
        second = lax.ppermute(part_b, axes, corner)
        return first, second, part_a

    def qkv_sum(self, first, second, part_a):
        return plus(first, jnp.where(self.aligned, part_a, second))

    def outputs(self, own, other):
        return jnp.concatenate(in_order(self.j, own, swap_rows(other)), axis=1)

    def own_sums(self, sums):
        total = sums + swap_cores(sums)
        return total + swap_cols(total)

    def row_sums(self, sums):
        return sums[:, : self.feats] + swap_rows(sums[:, self.feats :])

    def board(self, grad, sums):
        room = ((0, 32 - sums.shape[0]), (0, grad.shape[1] - sums.shape[1]))
        return jnp.concatenate([grad, jnp.pad(sums.astype(BF16), room)], axis=0)

    def leave_board(self, both, count):
        return both[: self.feats], both[self.feats : self.feats + count, : self.feats]


class AnyMoves:
    def __init__(self, r, c, feats, heads, pairs):
        self.heads = heads
        self.r, self.j, self.q, self.h, self.k = r, r % 2, r // 2, c // 2, c % 2
        self.feats, self.pairs = feats, pairs
        self.half = feats * lax.axis_size("row") // 2
        self.aligned = self.j == 0
        cols = lax.axis_size("col")
        self.cores = [[i, i + 1] for i in range(0, cols, 2)]
        self.likes = [list(range(core, cols, 2)) for core in range(2)]

    def halves(self, value):
        return value[: self.half], value[self.half :]

    def sequence(self, value):
        full = lax.all_gather(value, "row", axis=0, tiled=True)
        full = lax.all_gather(full, "col", axis=1, tiled=True, axis_index_groups=self.cores)
        return cut(full, self.q * LENGTH, LENGTH, 1)

    def pieces(self, value):
        full = self.sequence(value)
        own = cut(full, self.k * LENGTH // 2, LENGTH // 2, 1)
        other = cut(full, (1 - self.k) * LENGTH // 2, LENGTH // 2, 1)
        return *self.halves(own), *self.halves(other)

    def tables(self, mods, gain, bias, seq):
        count = mods.shape[0]
        table = jnp.concatenate([mods.reshape(3 * count, -1), gain[None], bias[None]], axis=0)
        table = lax.all_gather(table, "row", axis=1, tiled=True)
        table = jnp.concatenate([table[3 * count :], cut(table, 3 * seq, 3, 0)], axis=0)
        table = jnp.pad(table, ((0, 3), (0, 0)))
        return table[:, : self.half], table[:, self.half :]

    def cotangents(self, value):
        span = LENGTH // 4
        own = cut(self.sequence(value), (2 * self.k + self.j) * span, span, 1)
        first, second = self.halves(own)
        return jnp.concatenate([first, first], axis=1), second

    def flip(self, value):
        return value

    def likes_gather(self, value):
        rows = lax.all_gather(value, "row", axis=0, tiled=True)
        return lax.all_gather(rows, "col", axis=0, axis_index_groups=self.likes)

    def qkv(self, weight):
        return self.halves(cut(self.likes_gather(weight), self.j, 1, 0)[0])

    def feed(self, weight, gate):
        near, far = self.likes_gather(weight)
        return *self.halves(near), *self.halves(far)

    def corner(self, blocks, gate):
        return blocks

    def scatter(self, grad):
        grad = lax.psum_scatter(grad, "row", scatter_dimension=0, tiled=True)
        grad = lax.psum_scatter(
            grad, "col", scatter_dimension=1, tiled=True, axis_index_groups=self.likes
        )
        return lax.psum(grad, "dp").astype(F32)

    def first(self, value):
        return value

    third = first

    def second(self, value, gate=None):
        return value, gate

    def down_columns(self, near, far):
        return near, far

    def across(self, near, far):
        grad = self.scatter(jnp.concatenate([near, far], axis=1))
        return grad, jnp.zeros_like(grad)

    def extras(self, out_near, out_far, sums):
        return jnp.concatenate([out_near, out_far], axis=1), sums

    def extras_last(self, both, sums):
        return self.scatter(both), self.own_sums(sums.T).T

    def join(self, up, out, sums):
        return up, out, sums

    def row_sums(self, sums):
        return sums

    def board(self, grad, sums):
        return grad, sums

    def leave_board(self, both, count):
        return both

    def unpack(self, total, count):
        up, out, sums = total
        return up.astype(F32), out.T, sums[:, :count]

    def reduce_qkv(self, part_a, part_b, first):
        grad = jnp.concatenate([part_a, part_b], axis=0)
        both = in_order(self.j, grad, jnp.zeros_like(grad))
        total = self.scatter(jnp.concatenate(both, axis=1))
        return total, total, total

    def qkv_sum(self, first, second, part_a):
        return first

    def outputs(self, own, other):
        value = jnp.concatenate([own.astype(BF16), other], axis=0)
        parts = value.reshape(lax.axis_size("row"), self.feats, -1)
        parts = lax.all_to_all(parts, "row", split_axis=0, concat_axis=0, tiled=True)
        parts = lax.all_gather(parts, "col", axis=0, axis_index_groups=self.cores)
        span = parts.shape[-1]
        parts = parts.reshape(2, self.pairs, 2, self.feats, span).transpose(3, 1, 0, 2, 4)
        parts = parts.reshape(self.feats, -1)
        width = parts.shape[1] // 2
        return cut(parts, self.k * width, width, 1)

    def own_sums(self, sums):
        total = lax.psum(sums, ("dp", "row", "col"))
        return cut(total, self.r * self.feats, self.feats, 1)


def local(
    tokens, ln_gain, ln_bias, qkv_weight, out_weight, up_weight, down_weight,
    mod_weight, timestep, block_size, cotangent,
):
    rows, cols = lax.axis_size("row"), lax.axis_size("col")
    r, c, z = lax.axis_index("row"), lax.axis_index("col"), lax.axis_index("dp")
    width = mod_weight.shape[2]
    feats, local_tokens = tokens.shape
    pairs = 2 * local_tokens // LENGTH
    assert rows == 2 * pairs and cols == 4 and LENGTH % (8 * CHUNK) == 0
    sequences = timestep.shape[0]
    seq = (z * (cols // 2) + c // 2) * pairs + r // 2
    heads = out_weight.shape[0]
    moves = PairMoves(r, c, feats, heads) if pairs == 1 else AnyMoves(r, c, feats, heads, pairs)
    block_len = cut(block_size, seq, 1, 0)[0]
    num = jnp.stack([moves.k, moves.j, moves.aligned.astype(jnp.int32), block_len, seq])

    embedded = time_embed(timestep, width)
    mods = jnp.einsum("nd,ked->nke", embedded, mod_weight.astype(F32), precision=HIGH)
    cosine, sine = rope_tables(LENGTH, HEAD_DIM)

    pieces = moves.pieces(tokens)
    tables = moves.tables(mods, ln_gain, ln_bias, seq)
    qkv = moves.qkv(qkv_weight.reshape(feats, -1))
    packed = jnp.pad(jnp.concatenate([up_weight, out_weight.T], axis=1), ((0, 0), (0, 256 - heads)))
    gate = after(qkv[1], pieces[1], tables)
    ups = moves.feed(packed, gate)
    downs = moves.feed(down_weight, gate)

    up_col, *pieces = tie(ups[2], *pieces)
    ups = (*ups[:2], up_col, ups[3])
    queries, keys, values, act_one = project(num, pieces, qkv, tables, cosine, sine)
    cots = moves.cotangents(after(cotangent, queries))
    count = heads // HEAD_DIM
    down_col, queries = tie(downs[2], queries)
    early, early_sent, early_lse = attend_forward(num, 0, 1, queries, keys, values)
    early_got = swap_rows(early_sent)
    up_row, down_row, rest, early = tie(ups[1], downs[1], queries, early)
    ups = moves.corner((ups[0], up_row, *ups[2:]), early)
    downs = moves.corner((downs[0], down_row, down_col, downs[3]), early)
    late, late_sent, late_lse = attend_forward(num, 1, count - 1, rest, keys, values)
    got = (early_got, swap_rows(late_sent))
    early, late, ups, downs, cots = tie(early, late, ups, downs, cots)
    kept = (early, late)
    lse = jnp.concatenate([early_lse, late_lse], axis=0)

    span = cots[1].shape[1]
    own, other = mix(num, kept, got, ups)
    own, cots = tie(own, cots)
    gate_a, gate_b = tables[0][4][:, None], tables[1][4][:, None]
    cot_a = cut(cots[0], moves.j * span, span, 1).astype(F32)
    grad_a = cot_a * (1.0 + gate_a)
    grad_b = cots[1].astype(F32) * (1.0 + gate_b)
    grad_two = jnp.concatenate([grad_a, grad_b], axis=0).astype(BF16)
    grads = (grad_two, swap_cores(grad_two))
    hidden, act = enter(num, own, swap_cores(other), pieces[:2], tables)
    fed = feed(num, (act, swap_cores(act)), grads, ups, downs)
    branch_own, branch_other, back_own, back_other, up_near, up_far, down_near, down_far = fed
    back_got = swap_cores(back_other)
    grad_hidden, ones, turn_sums = turn(num, back_own, back_got, hidden, cots, tables)
    down_part = moves.down_columns(down_near, down_far)
    up_part = moves.down_columns(up_near, up_far)
    branch_got = swap_cores(branch_other)
    both_ones = (ones, swap_cores(ones))
    grad_kept, grad_sent, out_near, out_far = unmix(num, both_ones, kept, got, ups)
    grad_got = swap_rows(grad_sent)
    branch_own = after(branch_own, grad_sent)
    result_a, result_b, leave_sums = leave(
        num, branch_own, branch_got, hidden, cots, tables, turn_sums, -(-3 * sequences // 128) * 128
    )
    result = moves.outputs(result_a, result_b)
    down_part = moves.across(*after(down_part, result_a))
    extra = moves.extras(out_near, out_far, leave_sums)

    grad_kept, down_keep, extra_keep = tie(grad_kept, down_part[0], extra[0])
    grads = attend_backward(num, queries, keys, values, grad_kept, grad_got, lse, cosine, sine)
    down_part, extra = (down_keep, down_part[1]), (extra_keep, extra[1])
    up_part, down_part, extra, grads, result = tie(up_part, down_part, extra, grads, result)
    down_sum = moves.first(plus(*down_part))
    up_keep, up_got = moves.across(*up_part)
    extra_keep, extra_got = moves.extras_last(*extra)
    grads, up_keep, extra_keep = tie(grads, up_keep, extra_keep)
    keep, send = unproject(num, grads, qkv)
    send_got = swap_cores(send)
    up_sum = moves.join(plus(up_keep, up_got), extra_keep, extra_got)
    grads, keep, down_sum, up_sum = tie(grads, keep, down_sum, up_sum)
    qkv_a, qkv_b, qkv_first, norm_sums = weigh(num, grads, act_one, qkv, tables)
    norm_sums = moves.row_sums(norm_sums[:2])
    down_sum, _ = moves.second(down_sum)
    up_sum = moves.first(up_sum)
    send_got, norm_sums = tie(send_got, norm_sums)
    kept_core = keep + send_got.astype(F32)
    crossing = cut(kept_core, (1 - moves.j) * span, span, 1).astype(BF16)
    crossing = moves.flip(crossing)
    own = cut(kept_core, moves.j * span, span, 1)
    crossing, norm_sums, qkv_a, qkv_b, qkv_first = tie(crossing, norm_sums, qkv_a, qkv_b, qkv_first)
    qkv_part = moves.reduce_qkv(qkv_a, qkv_b, qkv_first)
    crossed = swap_rows(crossing)
    norm_sums = moves.own_sums(norm_sums)
    qkv_sum = moves.first(moves.board(moves.qkv_sum(*qkv_part), norm_sums))
    crossed, down_grad = tie(crossed, moves.third(down_sum))
    tokens_a, tokens_b = finish(num, own, crossed, pieces[:2], grad_hidden, tables)
    up_sum, tokens_b = moves.second(up_sum, tokens_b)
    qkv_sum, tokens_b = moves.second(qkv_sum, tokens_b)
    tokens_grad = moves.outputs(tokens_a, tokens_b)
    down_grad = down_grad.astype(F32)
    up_grad, out_grad, totals = moves.unpack(moves.third(up_sum), 3 * sequences)
    totals = totals.reshape(feats, sequences, 3)
    mod_grad = jnp.einsum("nd,enk->ked", embedded, totals, precision=HIGH)
    qkv_grad, norm_sums = moves.leave_board(moves.third(qkv_sum), 2)
    qkv_grad = qkv_grad.astype(F32)

    return (
        result,
        tokens_grad.astype(F32),
        norm_sums[0].astype(F32),
        norm_sums[1].astype(F32),
        qkv_grad.reshape(qkv_weight.shape),
        out_grad,
        up_grad,
        down_grad,
        mod_grad,
    )


def solution(mesh):
    placed = (
        P("row", ("dp", "col")),
        P("row"),
        P("row"),
        P("row", None, "col"),
        P("col", "row"),
        P("row", "col"),
        P("row", "col"),
        P(None, "row", None),
        P(),
        P(),
        P("row", ("dp", "col")),
    )
    return jax.shard_map(
        local,
        mesh=mesh,
        in_specs=placed,
        out_specs=(
            P("row", ("dp", "col")),
            P("row", ("dp", "col")),
            P("row"),
            P("row"),
            P("row", None, "col"),
            P("col", "row"),
            P("row", "col"),
            P("row", "col"),
            P(None, "row", None),
        ),
        check_vma=False,
    )
```
